32 devices in a mesh: seq: 8 (over y, x, core), tp: 4 (over z).
Axes of the slice: x: 2, y: 2, z: 4, core: 2. Of those that a mesh axis runs over, the one named last changes fastest.
Arguments:
- x_prefix: bfloat16 [2048, 2048], P('seq', 'tp'), may hold values from -6 to 6
- x_action: bfloat16 [128, 1024], P('seq', 'tp'), may hold values from -6 to 6
- prefix_segment: int32 [2048], replicated, may hold values from 0 to 2, as said below
- prefix_attn_gain: bfloat16 [2048], P('seq'), may hold values from 0.5 to 1.5
- prefix_query: bfloat16 [2048, 2048], P('seq', 'tp'), may hold values from -0.125 to 0.125
- prefix_key: bfloat16 [2048, 256], P('seq'), may hold values from -0.125 to 0.125
- prefix_value: bfloat16 [2048, 256], P('seq'), may hold values from -0.125 to 0.125
- prefix_out: bfloat16 [2048, 2048], P('tp', 'seq'), may hold values from -2 to 2
- prefix_mlp_gain: bfloat16 [2048], P('seq'), may hold values from 0.5 to 1.5
- prefix_gate: bfloat16 [2048, 16384], P('seq', 'tp'), may hold values from -0.125 to 0.125
- prefix_up: bfloat16 [2048, 16384], P('seq', 'tp'), may hold values from -0.125 to 0.125
- prefix_down: bfloat16 [16384, 2048], P('tp', 'seq'), may hold values from -0.046875 to 0.046875
- action_attn_gain: bfloat16 [1024], P('seq'), may hold values from 0.5 to 1.5
- action_query: bfloat16 [1024, 2048], P('seq', 'tp'), may hold values from -0.1875 to 0.1875
- action_key: bfloat16 [1024, 256], P('seq'), may hold values from -0.1875 to 0.1875
- action_value: bfloat16 [1024, 256], P('seq'), may hold values from -0.1875 to 0.1875
- action_out: bfloat16 [2048, 1024], P('tp', 'seq'), may hold values from -2 to 2
- action_mlp_gain: bfloat16 [1024], P('seq'), may hold values from 0.5 to 1.5
- action_gate: bfloat16 [1024, 4096], P('seq', 'tp'), may hold values from -0.1875 to 0.1875
- action_up: bfloat16 [1024, 4096], P('seq', 'tp'), may hold values from -0.1875 to 0.1875
- action_down: bfloat16 [4096, 1024], P('tp', 'seq'), may hold values from -0.09375 to 0.09375
- cot_prefix: bfloat16 [2048, 2048], P('seq'), may hold values from -6 to 6
- cot_action: bfloat16 [128, 1024], P('seq'), may hold values from -6 to 6
Outputs:
- out_prefix: bfloat16 [2048, 2048], P('seq', 'tp')
- out_action: bfloat16 [128, 1024], P('seq', 'tp')
- grad_x_prefix: bfloat16 [2048, 2048], P('seq', 'tp')
- grad_x_action: bfloat16 [128, 1024], P('seq', 'tp')
- grad_prefix_attn_gain: float32 [2048], P('seq')
- grad_prefix_query: float32 [2048, 2048], P('seq', 'tp')
- grad_prefix_key: float32 [2048, 256], P(('seq', 'tp'))
- grad_prefix_value: float32 [2048, 256], P(('seq', 'tp'))
- grad_prefix_out: float32 [2048, 2048], P('tp', 'seq')
- grad_prefix_mlp_gain: float32 [2048], P('seq')
- grad_prefix_gate: float32 [2048, 16384], P('seq', 'tp')
- grad_prefix_up: float32 [2048, 16384], P('seq', 'tp')
- grad_prefix_down: float32 [16384, 2048], P('tp', 'seq')
- grad_action_attn_gain: float32 [1024], P('seq')
- grad_action_query: float32 [1024, 2048], P('seq', 'tp')
- grad_action_key: float32 [1024, 256], P(('seq', 'tp'))
- grad_action_value: float32 [1024, 256], P(('seq', 'tp'))
- grad_action_out: float32 [2048, 1024], P('tp', 'seq')
- grad_action_mlp_gain: float32 [1024], P('seq')
- grad_action_gate: float32 [1024, 4096], P('seq', 'tp')
- grad_action_up: float32 [1024, 4096], P('seq', 'tp')
- grad_action_down: float32 [4096, 1024], P('tp', 'seq')
The draws below stay inside these ranges and needn't reach their ends.
Inputs may be any that keep to these rules, and one draw needn't show every extreme that they name: prefix_segment never falls along the rows; items 0 to 1 follow in order, each of 768 + t rows with t from 5 to 48; all later rows carry 2.
All inputs are finite; a program needn't handle non-finite values.
Results may differ from the reference program's by a relative error of at most 0.028.
Values may be sent and summed in bfloat16 or wider, within the bound.
No kernel may reach another device: no remote copies, remote signals or barrier semaphores. Data moves between devices by JAX's collectives and lax.ppermute only.
A program may use at most 256 MiB of HBM per device.

```python
import jax
import jax.numpy as jnp
from jax import lax

D_P = 2048
FF_P = 16384
D_A = 1024
FF_A = 4096
HEADS = 8
HD = 256
IMG = 768
TXT = 48
TXT_MIN = 5
ACT = 50
ITEMS = 2
NPRE = 2048
NSUF = 128
N_SEQ = 8


def draw_prefix_segment(key, part):
    text_len = jax.random.randint(jax.random.fold_in(key, 11), (ITEMS,), TXT_MIN, TXT + 1)
    item_ends = jnp.cumsum(IMG + text_len)
    places = jnp.arange(NPRE, dtype=jnp.int32)
    return jnp.sum((places[:, None] >= item_ends[None, :]).astype(jnp.int32), axis=1).astype(jnp.int32)


def shard_levels(key, shape, cuts, least, largest):
    factor_of = 1.0
    for position, blocks in cuts:
        steps = jax.random.uniform(jax.random.fold_in(jax.random.fold_in(key, 6), position), (blocks,), jnp.float32, least / len(cuts), largest / len(cuts))
        factor_of = factor_of * jnp.repeat(jnp.exp(steps), shape[position] // blocks).reshape((-1,) + (1,) * (len(shape) - 1 - position))
    return factor_of


def bell_draw(own_key, dims, width, reach, cuts=(), kind=jnp.bfloat16):
    loudness = shard_levels(own_key, dims, cuts, -0.22, 0.18) if cuts else 1.0
    entries = jax.random.normal(own_key, dims, jnp.float32) * width * loudness
    return jnp.minimum(jnp.maximum(entries, -reach), reach).astype(kind)


def setup_inputs(seed: int = 0) -> dict:
    keys = jax.random.split(jax.random.key(seed), 24)
    return {
        "x_prefix": bell_draw(keys[0], (NPRE, D_P), 1.0, 6.0, ((0, 8), (1, 4))),
        "x_action": bell_draw(keys[1], (NSUF, D_A), 1.0, 6.0, ((0, 8), (1, 4))),
        "prefix_segment": draw_prefix_segment(jax.random.fold_in(keys[23], 71), 0),
        "prefix_attn_gain": jnp.clip(1.0 + 0.1 * jax.random.normal(keys[3], (D_P,), jnp.float32), 0.5, 1.5).astype(jnp.bfloat16),
        "prefix_query": bell_draw(keys[4], (D_P, HEADS * HD), D_P ** -0.5, 0.125, ((0, 8), (1, 4))),
        "prefix_key": bell_draw(keys[5], (D_P, HD), D_P ** -0.5, 0.125, ((0, 8),)),
        "prefix_value": bell_draw(keys[6], (D_P, HD), D_P ** -0.5, 0.125, ((0, 8),)),
        "prefix_out": bell_draw(keys[7], (HEADS * HD, D_P), (3 * HEADS * HD // (IMG + TXT)) ** -0.5, 2.0, ((0, 4), (1, 8))),
        "prefix_mlp_gain": jnp.clip(1.0 + 0.1 * jax.random.normal(keys[8], (D_P,), jnp.float32), 0.5, 1.5).astype(jnp.bfloat16),
        "prefix_gate": bell_draw(keys[9], (D_P, FF_P), D_P ** -0.5, 0.125, ((0, 8), (1, 4))),
        "prefix_up": bell_draw(keys[10], (D_P, FF_P), D_P ** -0.5, 0.125, ((0, 8), (1, 4))),
        "prefix_down": bell_draw(keys[11], (FF_P, D_P), FF_P ** -0.5, 0.046875, ((0, 4), (1, 8))),
        "action_attn_gain": jnp.clip(1.0 + 0.1 * jax.random.normal(keys[12], (D_A,), jnp.float32), 0.5, 1.5).astype(jnp.bfloat16),
        "action_query": bell_draw(keys[13], (D_A, HEADS * HD), D_A ** -0.5, 0.1875, ((0, 8), (1, 4))),
        "action_key": bell_draw(keys[14], (D_A, HD), D_A ** -0.5, 0.1875, ((0, 8),)),
        "action_value": bell_draw(keys[15], (D_A, HD), D_A ** -0.5, 0.1875, ((0, 8),)),
        "action_out": bell_draw(keys[16], (HEADS * HD, D_A), (3 * HEADS * HD // (IMG + TXT)) ** -0.5, 2.0, ((0, 4), (1, 8))),
        "action_mlp_gain": jnp.clip(1.0 + 0.1 * jax.random.normal(keys[17], (D_A,), jnp.float32), 0.5, 1.5).astype(jnp.bfloat16),
        "action_gate": bell_draw(keys[18], (D_A, FF_A), D_A ** -0.5, 0.1875, ((0, 8), (1, 4))),
        "action_up": bell_draw(keys[19], (D_A, FF_A), D_A ** -0.5, 0.1875, ((0, 8), (1, 4))),
        "action_down": bell_draw(keys[20], (FF_A, D_A), FF_A ** -0.5, 0.09375, ((0, 4), (1, 8))),
        "cot_prefix": bell_draw(keys[21], (NPRE, D_P), 1.0, 6.0, ((0, 8),)),
        "cot_action": bell_draw(keys[22], (NSUF, D_A), 1.0, 6.0, ((0, 8),)),
    }


@jax.custom_vjp
def low(v):
    return lax.optimization_barrier(v.astype(jnp.bfloat16)).astype(jnp.float32)

@jax.custom_vjp
def low_back(v):
    return v

def low_keep(v):
    return (low(v), None)

def low_pass(kept, output_gradient):
    return (output_gradient,)

def back_keep(v):
    return (v, None)

def back_low(kept, output_gradient):
    return (low(output_gradient),)
low.defvjp(low_keep, low_pass)
low_back.defvjp(back_keep, back_low)
EPS = 1e-06
HIGH = lax.Precision.HIGHEST

def matmul(left, right):
    return jnp.dot(left, right, precision=HIGH, preferred_element_type=jnp.float32)

def rms_norm(values, norm_scale):
    inverse_norm = lax.rsqrt(lax.optimization_barrier(jnp.mean(values * values, axis=1, keepdims=True)) + EPS)
    return values * inverse_norm * norm_scale

def token_tables(prefix_segment):
    places = jnp.arange(NSUF, dtype=jnp.int32)
    items_of = places // (ACT + 1)
    suffix_seg = jnp.where(items_of < ITEMS, items_of, ITEMS).astype(jnp.int32)
    suffix_lvl = jnp.where((items_of < ITEMS) & (places % (ACT + 1) == 0), 1, 2).astype(jnp.int32)
    segment = jnp.concatenate([prefix_segment.astype(jnp.int32), suffix_seg])
    levels = jnp.concatenate([jnp.zeros((NPRE,), jnp.int32), suffix_lvl])
    return (segment, levels)

def attend(query_matrix, key_matrix, value_matrix, segment, levels):
    query_blocks = query_matrix.reshape(N_SEQ, -1, HEADS, HD)
    seg_blocks = segment.reshape(N_SEQ, -1)
    lvl_blocks = levels.reshape(N_SEQ, -1)

    def one_block(blocks_in):
        query_part, seg_part, lvl_part = blocks_in
        scores = jnp.einsum('qhd,kd->qhk', query_part, key_matrix, precision=HIGH) * HD ** (-0.5)
        scores = low_back(scores)
        allowed = (seg_part[:, None] == segment[None, :]) & (levels[None, :] <= lvl_part[:, None])
        scores = jnp.where(allowed[:, None, :], scores, -1e+30)
        row_max = lax.optimization_barrier(jnp.max(scores, axis=2, keepdims=True))
        weights = jnp.exp(scores - row_max)
        attn_probs = low(weights / lax.optimization_barrier(jnp.sum(weights, axis=2, keepdims=True)))
        return jnp.einsum('qhk,kd->qhd', attn_probs, value_matrix, precision=HIGH)
    attended = lax.map(jax.checkpoint(one_block), (query_blocks, seg_blocks, lvl_blocks))
    return attended.reshape(-1, HEADS * HD)

def front_half(x_rows, weights):
    normed = low(rms_norm(x_rows, weights[0]))
    query_matrix = low(low_back(matmul(normed, weights[1])))
    key_matrix = low(low_back(matmul(normed, weights[2])))
    value_matrix = low(low_back(matmul(normed, weights[3])))
    return (query_matrix, key_matrix, value_matrix)

def back_half(x_rows, mixed_rows, weights):
    residual = x_rows + low_back(matmul(mixed_rows, weights[4]))
    normed = low(rms_norm(low(residual), weights[5]))
    gate_output = low_back(matmul(normed, weights[6]))
    up_output = low_back(matmul(normed, weights[7]))
    hidden_state = low(jax.nn.gelu(gate_output, approximate=True) * up_output)
    return residual + low_back(matmul(hidden_state, weights[8]))

def block_layer(x_pre, x_act, weights_pre, weights_act, segment, levels):
    query_pre, key_pre, value_pre = front_half(x_pre, weights_pre)
    query_act, key_act, value_act = front_half(x_act, weights_act)
    attended = attend(jnp.concatenate([query_pre, query_act]), jnp.concatenate([key_pre, key_act]), jnp.concatenate([value_pre, value_act]), segment, levels)
    mixed_rows = low(low_back(attended))
    return (back_half(x_pre, mixed_rows[:NPRE], weights_pre), back_half(x_act, mixed_rows[NPRE:], weights_act))

def to_float(value):
    return value.astype(jnp.float32)

def reference(x_prefix, x_action, prefix_segment, prefix_attn_gain, prefix_query, prefix_key, prefix_value, prefix_out, prefix_mlp_gain, prefix_gate, prefix_up, prefix_down, action_attn_gain, action_query, action_key, action_value, action_out, action_mlp_gain, action_gate, action_up, action_down, cot_prefix, cot_action):
    segment, levels = token_tables(prefix_segment)
    weights_pre = tuple((to_float(w) for w in (prefix_attn_gain, prefix_query, prefix_key, prefix_value, prefix_out, prefix_mlp_gain, prefix_gate, prefix_up, prefix_down)))
    weights_act = tuple((to_float(w) for w in (action_attn_gain, action_query, action_key, action_value, action_out, action_mlp_gain, action_gate, action_up, action_down)))

    def forward(x_pre, x_act, w_pre, w_act):
        return block_layer(x_pre, x_act, w_pre, w_act, segment, levels)
    outputs, pull = jax.vjp(forward, to_float(x_prefix), to_float(x_action), weights_pre, weights_act)
    grad_pre, grad_act, wgrad_pre, wgrad_act = pull((to_float(cot_prefix), to_float(cot_action)))
    return (outputs[0].astype(jnp.bfloat16), outputs[1].astype(jnp.bfloat16), grad_pre.astype(jnp.bfloat16), grad_act.astype(jnp.bfloat16), wgrad_pre[0], wgrad_pre[1], wgrad_pre[2], wgrad_pre[3], wgrad_pre[4], wgrad_pre[5], wgrad_pre[6], wgrad_pre[7], wgrad_pre[8], wgrad_act[0], wgrad_act[1], wgrad_act[2], wgrad_act[3], wgrad_act[4], wgrad_act[5], wgrad_act[6], wgrad_act[7], wgrad_act[8])
```

```python
import functools

import jax
import jax.numpy as jnp
from jax import lax
from jax.experimental import pallas as pl
from jax.experimental.pallas import tpu as pltpu
from jax.sharding import PartitionSpec as P

HD = 256
IMG = 768
TXT = 48
ACT = 50
EPS = 1e-06
NEG = -1e30
BF = jnp.bfloat16
F32 = jnp.float32


def swap(value, axis, mask):
    count = lax.axis_size(axis)
    return lax.ppermute(value, axis, [(i, i ^ mask) for i in range(count)])


def gather_seq(halves):
    count = lax.axis_size("seq")
    masks = [1 << b for b in range(count.bit_length() - 1)]
    far = masks[1:]
    results = []
    for number, half in enumerate(halves):
        blocks = {0: half}
        for mask in far if number % 2 == 0 else far[::-1]:
            keys = sorted(blocks)
            got = swap(jnp.stack([blocks[k] for k in keys]), "seq", mask)
            for place, k in enumerate(keys):
                blocks[k ^ mask] = got[place]
        results.append(blocks)
    whole = []
    for blocks in results:
        keys = sorted(blocks)
        got = swap(jnp.stack([blocks[k] for k in keys]), "seq", 1)
        for place, k in enumerate(keys):
            blocks[k ^ 1] = got[place]
        whole.append([blocks[k] for k in range(count)])
    return whole


def scatter_seq(halves):
    count = lax.axis_size("seq")
    masks = [1 << b for b in range(count.bit_length() - 1)]
    far = masks[1:]
    results = []
    for number, half in enumerate(halves):
        blocks = dict(enumerate(half))
        for mask in [1] + (far if number % 2 == 0 else far[::-1]):
            keys = sorted(blocks)
            sent = [k for k in keys if k & mask]
            got = swap(jnp.stack([blocks[k].astype(BF) for k in sent]), "seq", mask)
            blocks = {k: blocks[k] for k in keys if not k & mask}
            for place, k in enumerate(sent):
                blocks[k ^ mask] = blocks[k ^ mask].astype(F32) + got[place].astype(F32)
        results.append(blocks[0])
    return results


def scatter_tp(make_piece):
    count = lax.axis_size("tp")
    rank = lax.axis_index("tp")
    total = make_piece(rank).astype(F32)
    for k in range(1, count):
        total = total + swap(make_piece(rank ^ k).astype(BF), "tp", k).astype(F32)
    return total


def gather_tp(piece):
    count = lax.axis_size("tp")
    rank = lax.axis_index("tp")
    return [(rank, piece)] + [(rank ^ k, swap(piece, "tp", k)) for k in range(1, count)]


def columns_of(pieces, rows, width, dtype):
    count = len(pieces)
    whole = jnp.zeros((rows, count * width), dtype)
    for place, piece in pieces:
        whole = lax.dynamic_update_slice(whole, piece, (0, place * width))
    return whole


def fold_action(piece, width):
    count = width // piece.shape[1]
    return jnp.concatenate(jnp.split(piece, count, axis=0), axis=1)


def unfold_action(piece, width):
    count = piece.shape[1] // width
    return jnp.concatenate(jnp.split(piece, count, axis=1), axis=0)


def normalized_rows(values):
    inverse = lax.rsqrt(jnp.mean(values * values, axis=1, keepdims=True) + EPS)
    return values * inverse, inverse


def gated(gate_in, up_in):
    return jax.nn.gelu(gate_in, approximate=True) * up_in


def dot(left, right):
    return jnp.dot(left, right, preferred_element_type=F32)


def dot_t(left, right):
    return lax.dot_general(left, right, (((1,), (1,)), ((), ())), preferred_element_type=F32)


def t_dot(left, right):
    return lax.dot_general(left, right, (((0,), (0,)), ((), ())), preferred_element_type=F32)


def token_codes(prefix_segment, seq_count, suf_rows):
    items_all = prefix_segment.shape[0] // (IMG + TXT)
    places = jnp.arange(seq_count * suf_rows, dtype=jnp.int32)
    items_of = places // (ACT + 1)
    suffix_seg = jnp.where(items_of < items_all, items_of, items_all)
    suffix_lvl = jnp.where((items_of < items_all) & (places % (ACT + 1) == 0), 1, 2)
    suffix = (suffix_seg * 4 + suffix_lvl).astype(jnp.int32)
    return jnp.concatenate(
        [(prefix_segment * 4).reshape(seq_count, -1), suffix.reshape(seq_count, -1)], axis=1
    )


def key_step(count):
    for step in (2176, 1088, 544, 272):
        if count % step == 0:
            return step
    return count


def attend_kernel(q_ref, k_ref, v_ref, qc_ref, kc_ref, att_ref, lse_ref):
    rows = q_ref.shape[0]
    heads = q_ref.shape[1] // HD
    count = k_ref.shape[0]
    step = key_step(count)
    code = qc_ref[...]
    low = code - code % 4
    for h in range(heads):
        query = q_ref[:, h * HD : (h + 1) * HD] * BF(HD**-0.5)
        top = jnp.full((rows, 1), NEG, F32)
        mass = jnp.zeros((rows, 1), F32)
        total = jnp.zeros((rows, HD), F32)
        for begin in range(0, count, step):
            keys = k_ref[begin : begin + step, :]
            marks = kc_ref[:, begin : begin + step]
            allowed = (marks >= low) & (marks <= code)
            scores = jnp.where(allowed, dot_t(query, keys), NEG)
            new_top = jnp.maximum(top, jnp.max(scores, axis=1, keepdims=True))
            expo = jnp.where(allowed, jnp.exp(scores - new_top), 0.0)
            shrink = jnp.exp(top - new_top)
            mass = mass * shrink + jnp.sum(expo, axis=1, keepdims=True)
            total = total * shrink + dot(expo.astype(BF), v_ref[begin : begin + step, :])
            top = new_top
        att_ref[:, h * HD : (h + 1) * HD] = total / mass
        lse_ref[:, h * 128 : (h + 1) * 128] = jnp.broadcast_to(top + jnp.log(mass), (rows, 128))


def attend(queries, keys, values, query_code, key_code):
    rows, width = queries.shape
    heads = width // HD
    count = keys.shape[0]
    return pl.pallas_call(
        attend_kernel,
        out_shape=(
            jax.ShapeDtypeStruct((rows, width), F32),
            jax.ShapeDtypeStruct((rows, heads * 128), F32),
        ),
        compiler_params=pltpu.CompilerParams(vmem_limit_bytes=48 << 20),
        cost_estimate=pl.CostEstimate(
            flops=4 * rows * width * count,
            bytes_accessed=4 * count * HD + 8 * rows * width,
            transcendentals=rows * heads * count,
        ),
    )(queries, keys, values, query_code, key_code)


def attend_back_kernel(
    q_ref, k_ref, v_ref, qc_ref, kc_ref, att_ref, lse_ref, dm_ref, dq_ref, dk_ref, dv_ref
):
    rows = q_ref.shape[0]
    heads = q_ref.shape[1] // HD
    count = k_ref.shape[0]
    step = key_step(count)
    code = qc_ref[...]
    low = code - code % 4
    dq = [jnp.zeros((rows, HD), F32) for _ in range(heads)]
    for begin in range(0, count, step):
        keys = k_ref[begin : begin + step, :]
        vals = v_ref[begin : begin + step, :]
        marks = kc_ref[:, begin : begin + step]
        allowed = (marks >= low) & (marks <= code)
        dk = jnp.zeros((step, HD), F32)
        dv = jnp.zeros((step, HD), F32)
        for h in range(heads):
            span = slice(h * HD, (h + 1) * HD)
            query = q_ref[:, span] * BF(HD**-0.5)
            dmix = dm_ref[:, span]
            delta = jnp.sum(dmix.astype(F32) * att_ref[:, span], axis=1, keepdims=True)
            scores = dot_t(query, keys)
            probs = jnp.where(allowed, jnp.exp(scores - lse_ref[:, h * 128 : h * 128 + 1]), 0.0)
            dscores = (probs * (dot_t(dmix, vals) - delta)).astype(BF)
            dq[h] = dq[h] + dot(dscores, keys)
            dk = dk + t_dot(dscores, query)
            dv = dv + t_dot(probs.astype(BF), dmix)
        dk_ref[begin : begin + step, :] = dk.astype(BF)
        dv_ref[begin : begin + step, :] = dv.astype(BF)
    for h in range(heads):
        dq_ref[:, h * HD : (h + 1) * HD] = (dq[h] * HD**-0.5).astype(BF)


def attend_back(queries, keys, values, query_code, key_code, attended, log_sum, dmixed):
    rows, width = queries.shape
    count = keys.shape[0]
    return pl.pallas_call(
        attend_back_kernel,
        out_shape=(
            jax.ShapeDtypeStruct((rows, width), BF),
            jax.ShapeDtypeStruct((count, HD), BF),
            jax.ShapeDtypeStruct((count, HD), BF),
        ),
        compiler_params=pltpu.CompilerParams(vmem_limit_bytes=56 << 20),
        cost_estimate=pl.CostEstimate(
            flops=10 * rows * width * count,
            bytes_accessed=8 * count * HD + 12 * rows * width,
            transcendentals=rows * width // HD * count,
        ),
    )(queries, keys, values, query_code, key_code, attended, log_sum, dmixed)


def shards(
    x_prefix,
    x_action,
    prefix_segment,
    prefix_attn_gain,
    prefix_query,
    prefix_key,
    prefix_value,
    prefix_out,
    prefix_mlp_gain,
    prefix_gate,
    prefix_up,
    prefix_down,
    action_attn_gain,
    action_query,
    action_key,
    action_value,
    action_out,
    action_mlp_gain,
    action_gate,
    action_up,
    action_down,
    cot_prefix,
    cot_action,
):
    n = lax.axis_size("seq")
    tp = lax.axis_size("tp")
    s = lax.axis_index("seq")
    t = lax.axis_index("tp")
    rp, cp = x_prefix.shape
    ra, ca = x_action.shape
    rows = rp + ra
    dp, da = cp * tp, ca * tp
    kp, ka = dp // n, da // n
    width = prefix_query.shape[1]
    fp, fa = prefix_gate.shape[1] // n, action_gate.shape[1] // n

    def pack_columns(prefix_part, action_part):
        return jnp.concatenate([prefix_part, fold_action(action_part, prefix_part.shape[1])], 0)

    def unpack_columns(packed):
        return packed[:rp], unfold_action(packed[rp:], ca)

    def full_rows(packed_pieces):
        parts = [(place, unpack_columns(piece)) for place, piece in packed_pieces]
        return (
            columns_of([(p, v[0]) for p, v in parts], rp, cp, packed_pieces[0][1].dtype),
            columns_of([(p, v[1]) for p, v in parts], ra, ca, packed_pieces[0][1].dtype),
        )

    def halves_of(prefix_rows, action_rows):
        return [
            jnp.concatenate([prefix_rows[:, : dp // 2], action_rows[: ra // 2]], axis=0),
            jnp.concatenate([prefix_rows[:, dp // 2 :], action_rows[ra // 2 :]], axis=0),
        ]

    def tokens_of(halves):
        prefix_all = jnp.concatenate(
            [
                jnp.concatenate([halves[0][k][:rp], halves[1][k][:rp]], axis=1)
                for k in range(n)
            ],
            axis=0,
        )
        action_all = jnp.concatenate(
            [x for k in range(n) for x in (halves[0][k][rp:], halves[1][k][rp:])], axis=0
        )
        return prefix_all, action_all

    def reduce_tokens(prefix_all, action_all):
        halves = [[], []]
        for k in range(n):
            pair = halves_of(prefix_all[k * rp : (k + 1) * rp], action_all[k * ra : (k + 1) * ra])
            for half, part in zip(halves, pair):
                half.append(part)
        left, right = scatter_seq(halves)
        prefix_sum = jnp.concatenate([left[:rp], right[:rp]], axis=1)
        action_sum = jnp.concatenate([left[rp:], right[rp:]], axis=0)
        return prefix_sum, action_sum

    def own_columns(prefix_rows, action_rows, rank):
        return (
            lax.dynamic_slice_in_dim(prefix_rows, rank * cp, cp, 1),
            lax.dynamic_slice_in_dim(action_rows, rank * ca, ca, 1),
        )

    def reduce_columns(prefix_rows, action_rows):
        return unpack_columns(
            scatter_tp(lambda rank: pack_columns(*own_columns(prefix_rows, action_rows, rank)))
        )

    gains = jnp.concatenate(
        [prefix_attn_gain, prefix_mlp_gain, action_attn_gain, action_mlp_gain]
    )
    qkv_width = width + 2 * HD
    gain_rows = -(-gains.shape[0] // qkv_width)
    gains = jnp.pad(gains, (0, 8 * qkv_width - gains.shape[0])).reshape(8, qkv_width)
    pack_qkv = jnp.concatenate(
        [
            jnp.concatenate([prefix_query, prefix_key, prefix_value], axis=1),
            jnp.concatenate([action_query, action_key, action_value], axis=1),
            gains,
        ],
        axis=0,
    )
    got_qkv = lax.all_gather(pack_qkv, "seq", axis=0)
    qkv_prefix = got_qkv[:, :kp].reshape(dp, qkv_width)
    qkv_action = got_qkv[:, kp : kp + ka].reshape(da, qkv_width)
    got_gains = got_qkv[:, kp + ka : kp + ka + gain_rows].reshape(n, -1).astype(F32)
    attn_gain_p = got_gains[:, :kp].reshape(dp)
    mlp_gain_p = got_gains[:, kp : 2 * kp].reshape(dp)
    attn_gain_a = got_gains[:, 2 * kp : 2 * kp + ka].reshape(da)
    mlp_gain_a = got_gains[:, 2 * kp + ka : 2 * kp + 2 * ka].reshape(da)
    pack_out = jnp.concatenate([prefix_out.T, action_out.T], axis=0)
    got_out = lax.all_gather(pack_out, "seq", axis=0)
    out_prefix_t = got_out[:, :kp].reshape(dp, width)
    out_action_t = got_out[:, kp:].reshape(da, width)

    down_prefix_t = prefix_down.T
    down_action_t = action_down.T

    def ff_piece(rank):
        prefix_part = jnp.concatenate(
            [
                lax.dynamic_slice_in_dim(w, rank * fp, fp, 1)
                for w in (prefix_gate, prefix_up, down_prefix_t)
            ],
            axis=1,
        )
        action_part = jnp.concatenate(
            [
                lax.dynamic_slice_in_dim(w, rank * fa, fa, 1)
                for w in (action_gate, action_up, down_action_t)
            ],
            axis=1,
        )
        return jnp.concatenate([prefix_part, fold_action(action_part, 3 * fp)], axis=0)

    ff_prefix = jnp.zeros((dp, 3 * fp), BF)
    ff_action = jnp.zeros((da, 3 * fa), BF)
    for k in range(n):
        piece = ff_piece(s ^ k)
        if k:
            piece = swap(piece, "seq", k)
        ff_prefix = lax.dynamic_update_slice(ff_prefix, piece[:kp], ((s ^ k) * kp, 0))
        ff_action = lax.dynamic_update_slice(
            ff_action, unfold_action(piece[kp:], 3 * fa), ((s ^ k) * ka, 0)
        )

    x_parts = full_rows(gather_tp(pack_columns(x_prefix, x_action)))
    norms1 = []
    projected = []
    for part, gain, weights in zip(
        x_parts, (attn_gain_p, attn_gain_a), (qkv_prefix, qkv_action)
    ):
        centered, inverse = normalized_rows(part.astype(F32))
        normed = (centered * gain).astype(BF)
        norms1.append((centered, inverse, gain, normed))
        projected.append(dot(normed, weights).astype(BF))
    qkv = jnp.concatenate(projected, axis=0)
    queries = qkv[:, :width]
    key_blocks, value_blocks = gather_seq([qkv[:, width : width + HD], qkv[:, width + HD :]])
    keys = jnp.concatenate(key_blocks, axis=0)
    values = jnp.concatenate(value_blocks, axis=0)
    codes = token_codes(prefix_segment, n, ra)
    query_code = lax.dynamic_slice_in_dim(codes, s, 1, 0).reshape(rows, 1)
    key_code = jnp.concatenate(
        [lax.dynamic_slice_in_dim(codes, s ^ k, 1, 0) for k in range(n)], axis=1
    )
    attended, log_sum = attend(queries, keys, values, query_code, key_code)
    mixed = attended.astype(BF)
    mixed_parts = (mixed[:rp], mixed[rp:])
    branch = reduce_columns(
        dot_t(mixed_parts[0], out_prefix_t), dot_t(mixed_parts[1], out_action_t)
    )
    residuals = (x_prefix.astype(F32) + branch[0], x_action.astype(F32) + branch[1])
    mids = full_rows(
        gather_tp(pack_columns(residuals[0].astype(BF), residuals[1].astype(BF)))
    )
    norms2 = []
    for part, gain in zip(mids, (mlp_gain_p, mlp_gain_a)):
        centered, inverse = normalized_rows(part.astype(F32))
        norms2.append((centered, inverse, gain, (centered * gain).astype(BF)))

    cot_all = tokens_of(gather_seq(halves_of(cot_prefix, cot_action)))
    normed_all = tokens_of(gather_seq(halves_of(norms2[0][3], norms2[1][3])))
    lifted = []
    dnormed = []
    ff_grads = []
    for rows_in, cot_rows, weights, f in zip(
        normed_all, cot_all, (ff_prefix, ff_action), (fp, fa)
    ):
        gate, up, down_t = weights[:, :f], weights[:, f : 2 * f], weights[:, 2 * f :]
        gate_out = dot(rows_in, gate)
        up_out = dot(rows_in, up)
        hidden, pull = jax.vjp(gated, gate_out, up_out)
        hidden = hidden.astype(BF)
        dhidden = dot(cot_rows, down_t)
        dgate, dup = (g.astype(BF) for g in pull(dhidden))
        dnormed.append((dot_t(dgate, gate) + dot_t(dup, up)).astype(BF))
        lifted.append(dot_t(hidden, down_t).astype(BF))
        ff_grads.append(
            (
                t_dot(rows_in, dgate).astype(BF),
                t_dot(rows_in, dup).astype(BF),
                t_dot(cot_rows, hidden).astype(BF),
            )
        )
    dnormed2 = reduce_columns(*reduce_tokens(*dnormed))
    lifted_own = reduce_columns(*reduce_tokens(*lifted))
    outputs = [(r + m).astype(BF) for r, m in zip(residuals, lifted_own)]

    def ff_grad_piece(rank):
        prefix_part = jnp.concatenate(
            [lax.dynamic_slice_in_dim(g, rank * kp, kp, 0) for g in ff_grads[0]], axis=1
        )
        action_part = jnp.concatenate(
            [lax.dynamic_slice_in_dim(g, rank * ka, ka, 0) for g in ff_grads[1]], axis=1
        )
        return jnp.concatenate([prefix_part, fold_action(action_part, 3 * fp)], axis=0)

    home_prefix = [jnp.zeros((kp, n * fp), F32) for _ in range(3)]
    home_action = [jnp.zeros((ka, n * fa), F32) for _ in range(3)]
    for k in range(n):
        piece = ff_grad_piece(s ^ k)
        if k:
            piece = swap(piece, "seq", k)
        action_piece = unfold_action(piece[kp:], 3 * fa)
        for i in range(3):
            home_prefix[i] = lax.dynamic_update_slice(
                home_prefix[i],
                piece[:kp, i * fp : (i + 1) * fp].astype(F32),
                (0, (s ^ k) * fp),
            )
            home_action[i] = lax.dynamic_update_slice(
                home_action[i],
                action_piece[:, i * fa : (i + 1) * fa].astype(F32),
                (0, (s ^ k) * fa),
            )

    dnormed2_full = full_rows(gather_tp(pack_columns(*(d.astype(BF) for d in dnormed2))))
    dresids = []
    dbranches = []
    mlp_gain_grads = []
    for part, cot_rows, (centered, inverse, gain, _), cols in zip(
        dnormed2_full, (cot_prefix, cot_action), norms2, (cp, ca)
    ):
        gradient = part.astype(F32)
        inner = gradient * gain
        moved = inverse * (
            inner - centered * jnp.mean(inner * centered, axis=1, keepdims=True)
        )
        dresid = cot_rows.astype(F32) + moved
        mlp_gain_grads.append(jnp.sum(gradient * centered, axis=0))
        dbranches.append(dresid.astype(BF))
        dresids.append(lax.dynamic_slice_in_dim(dresid, t * cols, cols, 1))

    dmixed = jnp.concatenate(
        [dot(dbranches[0], out_prefix_t), dot(dbranches[1], out_action_t)], axis=0
    ).astype(BF)
    out_grads = jnp.concatenate(
        [
            t_dot(dbranches[0], mixed_parts[0]).astype(BF).reshape(n, kp, width),
            t_dot(dbranches[1], mixed_parts[1]).astype(BF).reshape(n, ka, width),
        ],
        axis=1,
    )
    out_home = lax.psum_scatter(out_grads, "seq", scatter_dimension=0).astype(F32)
    dquery, dkey_all, dvalue_all = attend_back(
        queries, keys, values, query_code, key_code, attended, log_sum, dmixed
    )
    dkey, dvalue = scatter_seq(
        [
            [part[k * rows : (k + 1) * rows] for k in range(n)]
            for part in (dkey_all, dvalue_all)
        ]
    )
    dqkv = jnp.concatenate([dquery, dkey.astype(BF), dvalue.astype(BF)], axis=1)
    dqkv_parts = (dqkv[:rp], dqkv[rp:])
    qkv_grads = []
    dnormed1 = []
    dots = []
    attn_gain_grads = []
    for part, weights, (centered, inverse, gain, normed) in zip(
        dqkv_parts, (qkv_prefix, qkv_action), norms1
    ):
        qkv_grads.append(t_dot(normed, part).astype(BF))
        partial = dot_t(part, weights)
        product = partial * centered
        dots.append(jnp.sum(product * gain, axis=1))
        attn_gain_grads.append(jnp.sum(product, axis=0))
        dnormed1.append(partial)
    row_dots = jnp.pad(jnp.concatenate(dots), (0, cp * (-(-rows // cp)) - rows)).reshape(-1, cp)
    dots_high = row_dots.astype(BF)
    dots_low = (row_dots - dots_high.astype(F32)).astype(BF)
    dot_rows = jnp.concatenate([dots_high, dots_low], axis=0)
    dot_count = row_dots.shape[0]
    dot_rows = jnp.pad(dot_rows, ((0, 8 - dot_rows.shape[0]), (0, 0)))
    own = pack_columns(*own_columns(*dnormed1, t))
    packed_own = jnp.concatenate([own, dot_rows.astype(F32)], axis=0)
    total = packed_own
    for k in range(1, tp):
        message = pack_columns(*own_columns(*dnormed1, t ^ k)).astype(BF)
        total = total + swap(jnp.concatenate([message, dot_rows], axis=0), "tp", k).astype(F32)
    columns1 = unpack_columns(total[: own.shape[0]])
    dot_totals = total[own.shape[0] : own.shape[0] + 2 * dot_count].reshape(2, -1).sum(axis=0)
    dot_parts = (dot_totals[:rp, None], dot_totals[rp:rows, None])
    grad_x = []
    for gradient, row_dot, dresid, (centered, inverse, gain, _), cols in zip(
        columns1, dot_parts, dresids, norms1, (cp, ca)
    ):
        own_centered = lax.dynamic_slice_in_dim(centered, t * cols, cols, 1)
        own_gain = lax.dynamic_slice_in_dim(gain, t * cols, cols, 0)
        mean = row_dot / (cols * tp)
        moved = inverse * (gradient * own_gain - own_centered * mean)
        grad_x.append((dresid + moved).astype(BF))

    gain_rows_sent = jnp.concatenate(
        [
            mlp_gain_grads[0].reshape(n, kp),
            mlp_gain_grads[1].reshape(n, ka),
            attn_gain_grads[0].reshape(n, kp),
            attn_gain_grads[1].reshape(n, ka),
        ],
        axis=1,
    ).astype(BF)
    gain_rows_sent = jnp.pad(
        gain_rows_sent, ((0, 0), (0, 8 * qkv_width - gain_rows_sent.shape[1]))
    ).reshape(n, 8, qkv_width)
    qkv_sent = jnp.concatenate(
        [
            qkv_grads[0].reshape(n, kp, qkv_width),
            qkv_grads[1].reshape(n, ka, qkv_width),
            gain_rows_sent,
        ],
        axis=1,
    )
    qkv_home = lax.psum_scatter(qkv_sent, "seq", scatter_dimension=0).astype(F32)
    gains_home = qkv_home[kp + ka :].reshape(-1)
    shared = qkv_home[: kp + ka, width:]
    qp, qa = kp // tp, ka // tp
    attn_gains_partial = jnp.pad(
        gains_home[kp + ka : 2 * (kp + ka)], (0, (-(kp + ka)) % (2 * HD))
    ).reshape(-1, 2 * HD)
    attn_gains_partial = jnp.pad(
        attn_gains_partial, ((0, (-attn_gains_partial.shape[0]) % 8), (0, 0))
    )

    def shared_piece(rank):
        return jnp.concatenate(
            [
                lax.dynamic_slice_in_dim(shared, rank * qp, qp, 0),
                lax.dynamic_slice_in_dim(shared, kp + rank * qa, qa, 0),
                attn_gains_partial,
            ],
            axis=0,
        )

    shared_home = scatter_tp(shared_piece)
    attn_gains_home = shared_home[qp + qa :].reshape(-1)
    return (
        outputs[0],
        outputs[1],
        grad_x[0],
        grad_x[1],
        attn_gains_home[:kp],
        qkv_home[:kp, :width],
        shared_home[:qp, :HD],
        shared_home[:qp, HD:],
        out_home[:kp].T,
        gains_home[:kp],
        home_prefix[0],
        home_prefix[1],
        home_prefix[2].T,
        attn_gains_home[kp : kp + ka],
        qkv_home[kp : kp + ka, :width],
        shared_home[qp : qp + qa, :HD],
        shared_home[qp : qp + qa, HD:],
        out_home[kp:].T,
        gains_home[kp : kp + ka],
        home_action[0],
        home_action[1],
        home_action[2].T,
    )


def solution(mesh):
    split = P("seq", "tp")
    turned = P("tp", "seq")
    both = P(("seq", "tp"), None)
    one = P("seq")
    rows = P("seq", None)
    stream_in = (one, split, rows, rows, turned, one, split, split, turned)
    stream_out = (one, split, both, both, turned, one, split, split, turned)
    return jax.shard_map(
        shards,
        mesh=mesh,
        in_specs=(split, split, P()) + stream_in + stream_in + (rows, rows),
        out_specs=(split, split, split, split) + stream_out + stream_out,
        check_vma=False,
    )
```

```python
import jax
import jax.numpy as jnp
from jax import lax
from jax.experimental import pallas as pl
from jax.experimental.pallas import tpu as pltpu
from jax.sharding import PartitionSpec as P

HD = 256
IMG = 768
TXT = 48
ACT = 50
EPS = 1e-06
NEG = -1e30
BF = jnp.bfloat16
F32 = jnp.float32
MIB = 1 << 20


def swap(value, axis, mask):
    count = lax.axis_size(axis)
    return lax.ppermute(value, axis, [(i, i ^ mask) for i in range(count)])


def after(values, *tokens):
    return lax.optimization_barrier((values, tokens))[0]


def far_masks():
    count = lax.axis_size("seq")
    masks = [1 << b for b in range(1, count.bit_length() - 1)]
    return masks, masks[::-1]


def block_order(number):
    order = [0]
    for mask in far_masks()[number]:
        order = order + [k ^ mask for k in order]
    return order


def gather_far(halves):
    results = []
    for half, masks in zip(halves, far_masks()):
        blocks = [half]
        for mask in masks:
            blocks = blocks + [swap(b, "seq", mask) for b in blocks]
        results.append(blocks)
    return results


def gather_rows(halves):
    even = jnp.concatenate([b for blocks in gather_far(halves) for b in blocks], axis=0)
    return swap(even, "seq", 1), even


def scatter_far(halves):
    results = []
    for half, masks in zip(halves, far_masks()):
        blocks = half
        for mask in masks[:0:-1]:
            keep = blocks.shape[0] // 2
            got = swap(blocks[keep:].astype(BF), "seq", mask)
            blocks = blocks[:keep].astype(F32) + got.astype(F32)
        got = swap(blocks[1].astype(BF), "seq", masks[0])
        results.append((blocks[0], got))
    return results


def gather_tp(piece):
    return [piece] + [swap(piece, "tp", k) for k in range(1, lax.axis_size("tp"))]


def sum_tp(pieces):
    total = pieces[0].astype(F32)
    for k in range(1, len(pieces)):
        total = total + swap(pieces[k].astype(BF), "tp", k).astype(F32)
    return total


def dot(left, right):
    return jnp.dot(left, right, preferred_element_type=F32)


def dot_t(left, right):
    return lax.dot_general(left, right, (((1,), (1,)), ((), ())), preferred_element_type=F32)


def t_dot(left, right):
    return lax.dot_general(left, right, (((0,), (0,)), ((), ())), preferred_element_type=F32)


def whole_call(kernel, outs, args, flops, scratch=(), limit=48, transcendentals=0):
    specs = [
        pl.BlockSpec(memory_space=pltpu.SMEM if a.ndim == 1 else pltpu.VMEM) for a in args
    ]
    outs = tuple(jax.ShapeDtypeStruct(shape, dtype) for shape, dtype in outs)
    moved = sum(a.size * a.dtype.itemsize for a in args)
    moved += sum(o.size * o.dtype.itemsize for o in outs)
    return pl.pallas_call(
        kernel,
        out_shape=outs,
        in_specs=specs,
        out_specs=tuple(pl.BlockSpec(memory_space=pltpu.VMEM) for _ in outs),
        scratch_shapes=list(scratch),
        compiler_params=pltpu.CompilerParams(vmem_limit_bytes=limit * MIB),
        cost_estimate=pl.CostEstimate(
            flops=int(flops), bytes_accessed=int(moved), transcendentals=int(transcendentals)
        ),
    )(*args)


def inverse_rms(values):
    return lax.rsqrt(jnp.mean(values * values, axis=1, keepdims=True) + EPS)


def place(rank, width):
    return pl.ds(pl.multiple_of(rank * width, width), width)


def token_codes(prefix_segment, seq_count, suf_rows):
    items_all = prefix_segment.shape[0] // (IMG + TXT)
    places = jnp.arange(seq_count * suf_rows, dtype=jnp.int32)
    items_of = places // (ACT + 1)
    suffix_seg = jnp.where(items_of < items_all, items_of, items_all)
    suffix_lvl = jnp.where((items_of < items_all) & (places % (ACT + 1) == 0), 1, 2)
    suffix = (suffix_seg * 4 + suffix_lvl).astype(jnp.int32)
    return jnp.concatenate(
        [(prefix_segment * 4).reshape(seq_count, -1), suffix.reshape(seq_count, -1)], axis=1
    )


def front_kernel(t_ref, *refs):
    tp = lax.axis_size("tp")
    xs = refs[:tp]
    w_ref, gp_ref, ga_ref, q_ref, kva_ref, kvb_ref, xp_ref, xa_ref, inv_ref = refs[tp:]
    rp, dp = xp_ref.shape
    ra, da = xa_ref.shape
    cp, ca = dp // tp, da // tp
    kp, ka = dp // w_ref.shape[0], da // w_ref.shape[0]
    width = q_ref.shape[1]
    half = kva_ref.shape[0]
    for k in range(tp):
        xp_ref[:, place(t_ref[0] ^ k, cp)] = xs[k][:rp, :]
        xa_ref[:, place(t_ref[0] ^ k, ca)] = xs[k][rp:, :ca]
    parts = []
    inverses = []
    for x_ref, g_ref, first, last, size in (
        (xp_ref, gp_ref, 0, kp, dp),
        (xa_ref, ga_ref, kp, kp + ka, da),
    ):
        rows = x_ref[...].astype(F32)
        inverse = inverse_rms(rows)
        normed = (rows * inverse * g_ref[...]).astype(BF)
        parts.append(dot(normed, w_ref[:, first:last, :].reshape(size, -1)))
        inverses.append(inverse)
    qkv = jnp.concatenate(parts, axis=0)
    q_ref[...] = qkv[:, :width].astype(BF)
    kva_ref[...] = qkv[:half, width:].astype(BF)
    kvb_ref[...] = qkv[half:, width:].astype(BF)
    inv_ref[...] = jnp.broadcast_to(jnp.concatenate(inverses, axis=0), inv_ref.shape)


def key_step(count):
    for step in (2176, 1088, 544, 272):
        if count % step == 0:
            return step
    return count


def attend_kernel(q_ref, kv_ref, qc_ref, kc_ref, att_ref, mix_ref, lse_ref):
    rows = q_ref.shape[0]
    heads = q_ref.shape[1] // HD
    count = kv_ref.shape[0]
    step = key_step(count)
    code = qc_ref[...]
    low = code - code % 4
    for h in range(heads):
        query = q_ref[:, h * HD : (h + 1) * HD] * BF(HD**-0.5)
        top = jnp.full((rows, 1), NEG, F32)
        mass = jnp.zeros((rows, 1), F32)
        total = jnp.zeros((rows, HD), F32)
        for begin in range(0, count, step):
            keys = kv_ref[begin : begin + step, :HD]
            marks = kc_ref[:, begin : begin + step]
            allowed = (marks >= low) & (marks <= code)
            scores = jnp.where(allowed, dot_t(query, keys), NEG)
            new_top = jnp.maximum(top, jnp.max(scores, axis=1, keepdims=True))
            expo = jnp.where(allowed, jnp.exp(scores - new_top), 0.0)
            shrink = jnp.exp(top - new_top)
            mass = mass * shrink + jnp.sum(expo, axis=1, keepdims=True)
            total = total * shrink + dot(expo.astype(BF), kv_ref[begin : begin + step, HD:])
            top = new_top
        attended = total / mass
        att_ref[:, h * HD : (h + 1) * HD] = attended
        mix_ref[:, h * HD : (h + 1) * HD] = attended.astype(BF)
        lse_ref[:, h * 128 : (h + 1) * 128] = jnp.broadcast_to(top + jnp.log(mass), (rows, 128))


def attend_back_kernel(
    q_ref, kv_ref, qc_ref, kc_ref, att_ref, lse_ref, dm_ref, dq_ref, *dkv_refs
):
    rows = q_ref.shape[0]
    heads = q_ref.shape[1] // HD
    count = kv_ref.shape[0]
    step = key_step(count)
    each = dkv_refs[0].shape[0]
    code = qc_ref[...]
    low = code - code % 4
    dq = [jnp.zeros((rows, HD), F32) for _ in range(heads)]
    for begin in range(0, count, step):
        keys = kv_ref[begin : begin + step, :HD]
        vals = kv_ref[begin : begin + step, HD:]
        marks = kc_ref[:, begin : begin + step]
        allowed = (marks >= low) & (marks <= code)
        dk = jnp.zeros((step, HD), F32)
        dv = jnp.zeros((step, HD), F32)
        for h in range(heads):
            span = slice(h * HD, (h + 1) * HD)
            query = q_ref[:, span] * BF(HD**-0.5)
            dmix = dm_ref[:, span]
            delta = jnp.sum(dmix.astype(F32) * att_ref[:, span], axis=1, keepdims=True)
            scores = dot_t(query, keys)
            probs = jnp.where(allowed, jnp.exp(scores - lse_ref[:, h * 128 : h * 128 + 1]), 0.0)
            dscores = (probs * (dot_t(dmix, vals) - delta)).astype(BF)
            dq[h] = dq[h] + dot(dscores, keys)
            dk = dk + t_dot(dscores, query)
            dv = dv + t_dot(probs.astype(BF), dmix)
        dkv = jnp.concatenate([dk, dv], axis=1).astype(BF)
        for part in range(len(dkv_refs)):
            first, last = max(begin, part * each), min(begin + step, (part + 1) * each)
            if first < last:
                dkv_refs[part][first - part * each : last - part * each, :] = dkv[
                    first - begin : last - begin
                ]
    for h in range(heads):
        dq_ref[:, h * HD : (h + 1) * HD] = (dq[h] * HD**-0.5).astype(BF)


def branch_kernel(t_ref, mix_ref, w_ref, *outs):
    tp = len(outs)
    n = w_ref.shape[0]
    cp = outs[0].shape[1]
    ra = mix_ref.shape[0] - (outs[0].shape[0] - 16)
    rp = mix_ref.shape[0] - ra
    kp = cp * tp // n
    for k in range(tp):
        rank = t_ref[0] ^ k
        blocks = w_ref[pl.ds(rank * (n // tp), n // tp)]
        prefix = dot_t(mix_ref[:rp, :], blocks[:, :kp].reshape(cp, -1))
        action = dot_t(mix_ref[rp:, :], blocks[:, kp:].reshape(-1, mix_ref.shape[1]))
        outs[k][:rp, :] = prefix.astype(BF)
        outs[k][rp:, :] = jnp.concatenate(
            [action, jnp.zeros((ra, cp - action.shape[1]), F32)], axis=1
        ).astype(BF)


def middle_kernel(t_ref, *refs):
    tp = lax.axis_size("tp")
    mids = refs[:tp]
    gp_ref, ga_ref, mp_ref, ma_ref, a_ref, b_ref = refs[tp:]
    rp, dp = mp_ref.shape
    ra, da = ma_ref.shape
    cp, ca = dp // tp, da // tp
    for k in range(tp):
        mp_ref[:, place(t_ref[0] ^ k, cp)] = mids[k][:rp, :]
        ma_ref[:, place(t_ref[0] ^ k, ca)] = mids[k][rp:, :ca]
    rows = mp_ref[...].astype(F32)
    prefix = rows * inverse_rms(rows) * gp_ref[...]
    rows = ma_ref[...].astype(F32)
    action = rows * inverse_rms(rows) * ga_ref[...]
    action = jnp.concatenate([action, jnp.zeros((ra, dp - da), F32)], axis=1)
    for number, out in enumerate((a_ref, b_ref)):
        out[...] = jnp.concatenate(
            [
                prefix[number * (rp // 2) : (number + 1) * (rp // 2)],
                action[number * (ra // 2) : (number + 1) * (ra // 2)],
            ],
            axis=0,
        ).astype(BF)


def gelu_parts(value):
    scale = 0.7978845608028654
    square = value * value
    bent = jnp.tanh(scale * (value + 0.044715 * value * square))
    gelu = 0.5 * value * (1.0 + bent)
    slope = 0.5 * (1.0 + bent) + 0.5 * value * (1.0 - bent * bent) * scale * (
        1.0 + 3.0 * 0.044715 * square
    )
    return gelu, slope


def forward_back(rows, cot_rows, gate_up, down):
    f = down.shape[0]
    both = dot(rows, gate_up)
    gelu, slope = gelu_parts(both[:, :f])
    up = both[:, f:]
    dhidden = dot_t(cot_rows, down)
    return gelu * up, jnp.concatenate([dhidden * up * slope, dhidden * gelu], axis=1)


def feed_kernel(pair, x_ref, c_ref, w_ref, d_ref, act_ref, *refs):
    near_ref = refs[0] if len(refs) == 4 else None
    h_ref, g_ref, dn_ref = refs[-3:]
    rows, dp = x_ref.shape
    each = rows // pair
    prefix = each - act_ref.shape[0] // pair
    hidden, dgate_up = forward_back(x_ref[...], c_ref[...], w_ref[...], d_ref[...])
    inside = lax.broadcasted_iota(jnp.int32, (rows, 1), 0) % each < prefix
    dgate_up = jnp.where(inside, dgate_up, 0.0).astype(BF)
    h_ref[...] = jnp.where(inside, hidden, 0.0).astype(BF)
    g_ref[...] = dgate_up
    dn = dot_t(dgate_up, w_ref[...])
    action = act_ref[...]
    action = jnp.concatenate(
        [action, jnp.zeros((action.shape[0], dp - action.shape[1]), F32)], axis=1
    )
    pieces = []
    for i in range(pair):
        pieces.append(dn[i * each : i * each + prefix])
        pieces.append(action[i * (each - prefix) : (i + 1) * (each - prefix)])
    dn = jnp.concatenate(pieces, axis=0)
    if near_ref is not None:
        dn = dn + near_ref[...].astype(F32)
    dn_ref[...] = dn.astype(BF)


def feed(rows_in, cot_rows, gate_up, down, dn_action, near, each):
    total, dp = rows_in.shape
    pair = 2
    step = pair * each
    f = down.shape[0]
    act_step = dn_action.shape[0] * step // total
    row_spec = pl.BlockSpec((step, dp), lambda i: (i, 0))
    in_specs = [
        row_spec,
        row_spec,
        pl.BlockSpec(gate_up.shape, lambda i: (0, 0)),
        pl.BlockSpec(down.shape, lambda i: (0, 0)),
        pl.BlockSpec((act_step, dn_action.shape[1]), lambda i: (i, 0)),
    ]
    args = [rows_in, cot_rows, gate_up, down, dn_action]
    if near is not None:
        in_specs.append(row_spec)
        args.append(near)
    return pl.pallas_call(
        lambda *refs: feed_kernel(pair, *refs),
        grid=(total // step,),
        in_specs=in_specs,
        out_specs=(
            pl.BlockSpec((step, f), lambda i: (i, 0)),
            pl.BlockSpec((step, 2 * f), lambda i: (i, 0)),
            row_spec,
        ),
        out_shape=(
            jax.ShapeDtypeStruct((total, f), BF),
            jax.ShapeDtypeStruct((total, 2 * f), BF),
            jax.ShapeDtypeStruct((total, dp), BF),
        ),
        compiler_params=pltpu.CompilerParams(vmem_limit_bytes=48 * MIB),
        cost_estimate=pl.CostEstimate(
            flops=10 * total * dp * f,
            bytes_accessed=8 * total * dp + 6 * f * dp,
            transcendentals=total * f,
        ),
    )(*args)


def feed_action_kernel(x_ref, c_ref, w_ref, d_ref, dn_ref, lift_ref, gw_ref, gd_ref):
    rows, cot_rows = x_ref[...], c_ref[...]
    hidden, dgate_up = forward_back(rows, cot_rows, w_ref[...], d_ref[...])
    hidden, dgate_up = hidden.astype(BF), dgate_up.astype(BF)
    dn_ref[...] = dot_t(dgate_up, w_ref[...])
    lift_ref[...] = dot(hidden, d_ref[...])
    gw_ref[...] = t_dot(rows, dgate_up).astype(BF)
    gd_ref[...] = t_dot(hidden, cot_rows).astype(BF)


def weights_kernel(
    xo_ref, xe_ref, co_ref, ce_ref, ho_ref, he_ref, go_ref, ge_ref, act_ref, gw_ref, gd_ref
):
    f = ho_ref.shape[1]
    kp = gd_ref.shape[2]
    gw_ref[...] = (t_dot(xo_ref[...], go_ref[...]) + t_dot(xe_ref[...], ge_ref[...])).astype(BF)
    down = (t_dot(ho_ref[...], co_ref[...]) + t_dot(he_ref[...], ce_ref[...])).astype(BF)
    for i in range(gd_ref.shape[0]):
        gd_ref[i, :f, :] = down[:, i * kp : (i + 1) * kp]
        gd_ref[i, f:, :] = act_ref[i]


def weight_grads(x_odd, x_even, c_odd, c_even, h_odd, h_even, g_odd, g_even, action):
    total, dp = x_odd.shape
    f = h_odd.shape[1]
    n, extra, kp = action.shape
    wide = 256
    cols = pl.BlockSpec((total, wide), lambda i: (0, i))
    h_spec = pl.BlockSpec((total, f), lambda i: (0, 0))
    g_spec = pl.BlockSpec((total, 2 * f), lambda i: (0, 0))
    return pl.pallas_call(
        weights_kernel,
        grid=(dp // wide,),
        in_specs=[
            cols,
            cols,
            cols,
            cols,
            h_spec,
            h_spec,
            g_spec,
            g_spec,
            pl.BlockSpec((wide // kp, extra, kp), lambda i: (i, 0, 0)),
        ],
        out_specs=(
            pl.BlockSpec((wide, 2 * f), lambda i: (i, 0)),
            pl.BlockSpec((wide // kp, f + extra, kp), lambda i: (i, 0, 0)),
        ),
        out_shape=(
            jax.ShapeDtypeStruct((dp, 2 * f), BF),
            jax.ShapeDtypeStruct((n, f + extra, kp), BF),
        ),
        compiler_params=pltpu.CompilerParams(vmem_limit_bytes=48 * MIB),
        cost_estimate=pl.CostEstimate(
            flops=12 * total * dp * f, bytes_accessed=8 * total * dp, transcendentals=0
        ),
    )(x_odd, x_even, c_odd, c_even, h_odd, h_even, g_odd, g_even, action)


def lift_kernel(
    odd_ref, pa_ref, pb_ref, la_ref, lb_ref,
    oa_ref, ea_ref, ob_ref, eb_ref, aa_ref, ab_ref, d_ref, out_ref,
):
    odd = odd_ref[pl.program_id(0)] == 1
    dp = out_ref.shape[2]
    prefix = oa_ref.shape[0] - aa_ref.shape[0]
    outs = []
    for o_ref, e_ref in ((oa_ref, ea_ref), (ob_ref, eb_ref)):
        hidden = jnp.where(odd, o_ref[...].astype(F32), e_ref[...].astype(F32)).astype(BF)
        outs.append(dot(hidden, d_ref[...])[:prefix])
    action = jnp.concatenate([aa_ref[...], ab_ref[...]], axis=0)
    action = jnp.concatenate(
        [action, jnp.zeros((action.shape[0], dp - action.shape[1]), F32)], axis=1
    )
    out_ref[0] = jnp.concatenate(outs + [action], axis=0).astype(BF)


def lift(odd, place_a, place_b, lift_a, lift_b, h_odd, h_even, lifted_action, down, each, ra):
    n = odd.shape[0]
    f, dp = down.shape
    da = lifted_action.shape[1]
    a_spec = pl.BlockSpec((each, f), lambda j, o, a, b, la, lb: (a[j], 0))
    b_spec = pl.BlockSpec((each, f), lambda j, o, a, b, la, lb: (b[j], 0))
    rows = 2 * each
    return pl.pallas_call(
        lift_kernel,
        grid_spec=pltpu.PrefetchScalarGridSpec(
            num_scalar_prefetch=5,
            grid=(n,),
            in_specs=[
                a_spec,
                a_spec,
                b_spec,
                b_spec,
                pl.BlockSpec((ra // 2, da), lambda j, o, a, b, la, lb: (la[j], 0)),
                pl.BlockSpec((ra // 2, da), lambda j, o, a, b, la, lb: (lb[j], 0)),
                pl.BlockSpec((f, dp), lambda j, o, a, b, la, lb: (0, 0)),
            ],
            out_specs=pl.BlockSpec((1, rows, dp), lambda j, o, a, b, la, lb: (j, 0, 0)),
        ),
        out_shape=jax.ShapeDtypeStruct((n, rows, dp), BF),
        compiler_params=pltpu.CompilerParams(vmem_limit_bytes=32 * MIB),
        cost_estimate=pl.CostEstimate(
            flops=2 * n * rows * dp * f, bytes_accessed=2 * n * rows * dp, transcendentals=0
        ),
    )(odd, place_a, place_b, lift_a, lift_b, h_odd, h_even, h_odd, h_even,
      lifted_action, lifted_action, down)


def pieces_kernel(t_ref, ka_ref, ga_ref, kb_ref, gb_ref, *outs):
    tp = len(outs)
    each, dp = ka_ref.shape
    cp = dp // tp
    rp = outs[0].shape[0] * 2 * each // (2 * each)
    extra = 8
    prefix = each - extra
    ca = outs[0].shape[1] // 2
    del rp
    for k in range(tp):
        rank = t_ref[0] ^ k
        tops, ends = [], []
        for keep, got in ((ka_ref, ga_ref), (kb_ref, gb_ref)):
            wide = place(rank, cp)
            tops.append(keep[:prefix, wide].astype(F32) + got[:prefix, wide].astype(F32))
            slim = place(rank, ca)
            ends.append(
                keep[prefix:, slim].astype(F32) + got[prefix:, slim].astype(F32)
            )
        action = jnp.concatenate(ends, axis=0)
        action = jnp.concatenate(
            [action, jnp.zeros((action.shape[0], cp - ca), F32)], axis=1
        )
        outs[k][...] = jnp.concatenate(tops + [action], axis=0).astype(BF)


def middle_back_kernel(t_ref, *refs):
    tp = lax.axis_size("tp")
    ds = refs[:tp]
    mp_ref, ma_ref, gp_ref, ga_ref, cp_ref, ca_ref, w_ref = refs[tp : tp + 7]
    bp_ref, ba_ref, own_ref, lp_ref, la_ref, dm_ref, dp_scr, da_scr, rp_scr, ra_scr = refs[tp + 7 :]
    rp, dp = mp_ref.shape
    ra, da = ma_ref.shape
    cp, ca = dp // tp, da // tp
    n = w_ref.shape[0]
    kp = dp // n
    t = t_ref[0]
    for k in range(tp):
        dp_scr[:, place(t ^ k, cp)] = ds[k][:rp, :]
        da_scr[:, place(t ^ k, ca)] = ds[k][rp:, :ca]
    mixes = []
    for d_ref, m_ref, g_ref, c_ref, b_ref, r_ref, l_ref, first, last in (
        (dp_scr, mp_ref, gp_ref, cp_ref, bp_ref, rp_scr, lp_ref, 0, kp),
        (da_scr, ma_ref, ga_ref, ca_ref, ba_ref, ra_scr, la_ref, kp, w_ref.shape[1]),
    ):
        gradient = d_ref[...].astype(F32)
        rows = m_ref[...].astype(F32)
        inverse = inverse_rms(rows)
        centered = rows * inverse
        inner = gradient * g_ref[...]
        dresid = c_ref[...].astype(F32) + inverse * (
            inner - centered * jnp.mean(inner * centered, axis=1, keepdims=True)
        )
        l_ref[...] = jnp.sum(gradient * centered, axis=0, keepdims=True)
        r_ref[...] = dresid
        branch = dresid.astype(BF)
        b_ref[...] = branch
        mixes.append(dot(branch, w_ref[:, first:last, :].reshape(rows.shape[1], -1)))
    dm_ref[...] = jnp.concatenate(mixes, axis=0).astype(BF)
    own_ref[:rp, :] = rp_scr[:, place(t, cp)]
    own_ref[rp:, :] = jnp.concatenate(
        [ra_scr[:, place(t, ca)], jnp.zeros((ra, cp - ca), F32)], axis=1
    )


def out_grad_kernel(bp_ref, ba_ref, mix_ref, out_ref):
    rp, dp = bp_ref.shape
    n = out_ref.shape[0]
    kp = dp // n
    width = mix_ref.shape[1]
    out_ref[:, :kp, :] = t_dot(bp_ref[...], mix_ref[:rp, :]).astype(BF).reshape(n, kp, width)
    out_ref[:, kp:, :] = t_dot(ba_ref[...], mix_ref[rp:, :]).astype(BF).reshape(n, -1, width)


def front_back_kernel(heads_width, s_ref, t_ref, dq_ref, *refs):
    tp = lax.axis_size("tp")
    n = lax.axis_size("seq")
    (ka_ref, ra_ref, kb_ref, rb_ref, xp_ref, xa_ref, inv_ref, gp_ref, ga_ref, w_ref, lp_ref,
     la_ref) = refs[:12]
    groups = refs[12:16]
    pieces = refs[16 : 16 + tp]
    gwp_scr, gwa_scr, gain_scr, dp_scr, da_scr = refs[16 + tp :]
    rp, dp = xp_ref.shape
    ra, da = xa_ref.shape
    kp, ka = dp // n, da // n
    cp, ca = dp // tp, da // tp
    width = heads_width
    dkv = jnp.concatenate(
        [
            ka_ref[...].astype(F32) + ra_ref[...].astype(F32),
            kb_ref[...].astype(F32) + rb_ref[...].astype(F32),
        ],
        axis=0,
    )
    dqkv = jnp.concatenate([dq_ref[...].astype(F32), dkv], axis=1)
    gain_scr[...] = jnp.zeros(gain_scr.shape, F32)
    dots = []
    for x_ref, g_ref, d_scr, gw_scr, l_ref, begin, end, first, last, size, at in (
        (xp_ref, gp_ref, dp_scr, gwp_scr, lp_ref, 0, rp, 0, kp, kp, 0),
        (xa_ref, ga_ref, da_scr, gwa_scr, la_ref, rp, rp + ra, kp, kp + ka, ka, 256),
    ):
        grad_rows = dqkv[begin:end].astype(BF)
        centered = x_ref[...].astype(F32) * inv_ref[begin:end, :1]
        normed = (centered * g_ref[...]).astype(BF)
        gw_scr[...] = t_dot(normed, grad_rows).astype(BF)
        weights = w_ref[:, first:last, :].reshape(x_ref.shape[1], -1)
        partial = dot_t(grad_rows, weights)
        d_scr[...] = partial
        product = partial * centered
        gains = jnp.sum(product, axis=0, keepdims=True)
        mlp_gains = l_ref[...]
        for d in range(n):
            gain_scr[d, 0:1, at : at + size] = gains[:, d * size : (d + 1) * size]
            gain_scr[d, 0:1, at + 512 : at + 512 + size] = mlp_gains[
                :, d * size : (d + 1) * size
            ]
        dots.append(jnp.sum(product * g_ref[...], axis=1, keepdims=True))
    column = jnp.concatenate(dots, axis=0)
    lanes = lax.broadcasted_iota(jnp.int32, (rp + ra, cp), 1)
    rows = lax.broadcasted_iota(jnp.int32, (rp + ra, cp), 0)
    row = jnp.sum(jnp.where(lanes == rows, column, 0.0), axis=0, keepdims=True)
    high = row.astype(BF).astype(F32)
    tail = jnp.concatenate([high, row - high, jnp.zeros((6, cp), F32)], axis=0)
    for k in range(tp):
        rank = t_ref[0] ^ k
        action = jnp.concatenate(
            [da_scr[:, place(rank, ca)], jnp.zeros((ra, cp - ca), F32)], axis=1
        )
        pieces[k][...] = jnp.concatenate([dp_scr[:, place(rank, cp)], action, tail], axis=0).astype(
            BF
        )
    for odd in range(2):
        for number in range(2):
            out = groups[2 * odd + number]
            for i, k in enumerate(block_order(number)):
                d = s_ref[0] ^ (k ^ odd)
                hp, ha = kp // 2, ka // 2
                out[i, :hp, :] = gwp_scr[
                    pl.ds(pl.multiple_of(d * kp + number * hp, hp), hp), :
                ]
                out[i, hp : hp + ha, :] = gwa_scr[
                    pl.ds(pl.multiple_of(d * ka + number * ha, ha), ha), :
                ]
                out[i, hp + ha :, :] = gain_scr[d].astype(BF) * BF(1 - number)


def grad_x_kernel(t_ref, *refs):
    tp = lax.axis_size("tp")
    ds = refs[:tp]
    x_ref, inv_ref, gp_ref, ga_ref, r_ref, op_ref, oa_ref = refs[tp:]
    rp, cp = op_ref.shape
    ra, ca = oa_ref.shape
    t = t_ref[0]
    total = ds[0][...].astype(F32)
    for k in range(1, tp):
        total = total + ds[k][...].astype(F32)
    row = total[rp + ra : rp + ra + 1] + total[rp + ra + 1 : rp + ra + 2]
    lanes = lax.broadcasted_iota(jnp.int32, (rp + ra, cp), 1)
    rows = lax.broadcasted_iota(jnp.int32, (rp + ra, cp), 0)
    column = jnp.sum(jnp.where(lanes == rows, row, 0.0), axis=1, keepdims=True)
    for o_ref, g_ref, begin, end, wide in (
        (op_ref, gp_ref, 0, rp, cp),
        (oa_ref, ga_ref, rp, rp + ra, ca),
    ):
        inverse = inv_ref[begin:end, :1]
        centered = x_ref[begin:end, :wide].astype(F32) * inverse
        mean = column[begin:end] / (wide * tp)
        moved = inverse * (
            total[begin:end, :wide] * g_ref[:, place(t, wide)] - centered * mean
        )
        o_ref[...] = (r_ref[begin:end, :wide] + moved).astype(BF)


def home_kernel(in_ref, gate_ref, up_ref):
    f = gate_ref.shape[1]
    gate_ref[...] = in_ref[0, :, :f].astype(F32)
    up_ref[...] = in_ref[0, :, f:].astype(F32)


def home(got):
    n, kp, both = got.shape
    f = both // 2
    out = pl.BlockSpec((kp, f), lambda j: (0, j))
    return pl.pallas_call(
        home_kernel,
        grid=(n,),
        in_specs=[pl.BlockSpec((1, kp, both), lambda j: (j, 0, 0))],
        out_specs=(out, out),
        out_shape=(jax.ShapeDtypeStruct((kp, n * f), F32),) * 2,
        cost_estimate=pl.CostEstimate(
            flops=0, bytes_accessed=6 * n * kp * both, transcendentals=0
        ),
    )(got)


def shards(
    x_prefix,
    x_action,
    prefix_segment,
    prefix_attn_gain,
    prefix_query,
    prefix_key,
    prefix_value,
    prefix_out,
    prefix_mlp_gain,
    prefix_gate,
    prefix_up,
    prefix_down,
    action_attn_gain,
    action_query,
    action_key,
    action_value,
    action_out,
    action_mlp_gain,
    action_gate,
    action_up,
    action_down,
    cot_prefix,
    cot_action,
):
    n = lax.axis_size("seq")
    tp = lax.axis_size("tp")
    s = lax.axis_index("seq")
    t = lax.axis_index("tp")
    rank_t = t.astype(jnp.int32).reshape(1)
    rank_s = s.astype(jnp.int32).reshape(1)
    rp, cp = x_prefix.shape
    ra, ca = x_action.shape
    rows = rp + ra
    half = rows // 2
    dp, da = cp * tp, ca * tp
    kp, ka = dp // n, da // n
    width = prefix_query.shape[1]
    qkv_width = width + 2 * HD
    fp, fa = prefix_gate.shape[1] // n, action_gate.shape[1] // n

    x_pack = jnp.concatenate(
        [x_prefix, jnp.pad(x_action, ((0, 0), (0, cp - ca)))], axis=0
    )
    x_pieces = gather_tp(x_pack)
    gains = jnp.concatenate(
        [prefix_attn_gain, prefix_mlp_gain, action_attn_gain, action_mlp_gain]
    )
    gain_rows = -(-gains.shape[0] // qkv_width)
    gains = jnp.pad(gains, (0, 8 * qkv_width - gains.shape[0])).reshape(8, qkv_width)
    pack_qkv = jnp.concatenate(
        [
            jnp.concatenate([prefix_query, prefix_key, prefix_value], axis=1),
            jnp.concatenate([action_query, action_key, action_value], axis=1),
            gains,
        ],
        axis=0,
    )
    got_qkv = lax.all_gather(pack_qkv, "seq", axis=0)
    got_gains = got_qkv[:, kp + ka : kp + ka + gain_rows].reshape(n, -1).astype(F32)
    attn_gain_p = got_gains[:, :kp].reshape(1, dp)
    mlp_gain_p = got_gains[:, kp : 2 * kp].reshape(1, dp)
    attn_gain_a = got_gains[:, 2 * kp : 2 * kp + ka].reshape(1, da)
    mlp_gain_a = got_gains[:, 2 * kp + ka : 2 * kp + 2 * ka].reshape(1, da)
    pack_out = jnp.concatenate([prefix_out.T, action_out.T], axis=0)
    cot_wide = jnp.pad(cot_action, ((0, 0), (0, dp - da)))
    cot_odd, cot_even = gather_rows(
        [
            jnp.concatenate(
                [
                    cot_prefix[i * (rp // 2) : (i + 1) * (rp // 2)],
                    cot_wide[i * (ra // 2) : (i + 1) * (ra // 2)],
                ],
                axis=0,
            )
            for i in range(2)
        ]
    )

    def by_units(w, f):
        return w.reshape(w.shape[0], n, f).transpose(1, 0, 2)

    gate_up_sent = jnp.concatenate([by_units(prefix_gate, fp), by_units(prefix_up, fp)], axis=2)
    action_sent = jnp.concatenate(
        [
            by_units(action_gate, fa),
            by_units(action_up, fa),
            action_down.reshape(n, fa, ka).transpose(0, 2, 1),
        ],
        axis=2,
    ).reshape(n, -1, kp)
    extra = action_sent.shape[1]
    down_sent = jnp.concatenate([prefix_down.reshape(n, fp, kp), action_sent], axis=1)

    queries, kv_a, kv_b, x_full_p, x_full_a, inverse1 = whole_call(
        front_kernel,
        (
            ((rows, width), BF),
            ((half, 2 * HD), BF),
            ((half, 2 * HD), BF),
            ((rp, dp), BF),
            ((ra, da), BF),
            ((rows, 128), F32),
        ),
        [rank_t, *x_pieces, got_qkv, attn_gain_p, attn_gain_a],
        2 * rp * dp * qkv_width,
    )
    kv_even = [jnp.concatenate(blocks, axis=0) for blocks in gather_far([kv_a, kv_b])]
    kv_odd = [swap(e, "seq", 1) for e in kv_even]
    keys_values = jnp.concatenate([kv_even[0], kv_odd[0], kv_even[1], kv_odd[1]], axis=0)
    codes = token_codes(prefix_segment, n, ra)
    query_code = lax.dynamic_slice_in_dim(codes, s, 1, 0).reshape(rows, 1)
    key_code = jnp.concatenate(
        [
            lax.dynamic_slice(codes, (s ^ k ^ odd, number * half), (1, half))
            for number in range(2)
            for odd in range(2)
            for k in block_order(number)
        ],
        axis=1,
    )
    attended, mixed, log_sum = whole_call(
        attend_kernel,
        (
            ((rows, width), F32),
            ((rows, width), BF),
            ((rows, width // HD * 128), F32),
        ),
        [queries, keys_values, query_code, key_code],
        4 * rows * width * n * rows,
        transcendentals=rows * width // HD * n * rows,
    )
    got_out = lax.all_gather(after(pack_out, queries), "seq", axis=0)
    gate_up_sent, down_sent = after((gate_up_sent, down_sent), keys_values)
    gate_up = lax.all_to_all(gate_up_sent, "seq", 0, 0).reshape(dp, 2 * fp)
    down_got = lax.all_to_all(down_sent, "seq", 0, 0)

    piece = (((rows, cp), BF),)
    branch = sum_tp(
        whole_call(
            branch_kernel, piece * tp, [rank_t, mixed, got_out], 2 * rows * dp * width
        )
    )
    residual = x_pack.astype(F32) + branch
    block = (((half, dp), BF),)
    mid_p, mid_a, normed_a, normed_b = whole_call(
        middle_kernel,
        (((rp, dp), BF), ((ra, da), BF)) + block * 2,
        [rank_t, *gather_tp(residual.astype(BF)), mlp_gain_p, mlp_gain_a],
        rp * dp,
    )

    normed_odd, normed_even = gather_rows([normed_a, normed_b])
    down = down_got[:, :fp].transpose(1, 0, 2).reshape(fp, dp)
    action_got = down_got[:, fp:].reshape(da, 3 * fa)
    gate_up_action = action_got[:, : 2 * fa]
    down_action = action_got[:, 2 * fa :].T

    def action_rows(blocks):
        return blocks.reshape(n, half, dp)[:, rp // 2 :, :da].reshape(-1, da)

    normed_action = jnp.concatenate([action_rows(normed_odd), action_rows(normed_even)], axis=0)
    cot_action_all = jnp.concatenate([action_rows(cot_odd), action_rows(cot_even)], axis=0)
    tokens = n * ra
    dn_action, lifted_action, grad_gu_action, grad_down_action = whole_call(
        feed_action_kernel,
        (
            ((tokens, da), F32),
            ((tokens, da), F32),
            ((da, 2 * fa), BF),
            ((fa, da), BF),
        ),
        [normed_action, cot_action_all, gate_up_action, down_action],
        18 * tokens * da * fa,
    )
    h_odd, g_odd, dn_odd = feed(
        normed_odd, cot_odd, gate_up, down, dn_action[: tokens // 2], None, half
    )
    h_even, g_even, dn_even = feed(
        normed_even,
        cot_even,
        gate_up,
        down,
        dn_action[tokens // 2 :],
        swap(dn_odd, "seq", 1),
        half,
    )
    dn_blocks = dn_even.reshape(2, n // 2, half, dp)
    (keep_a, got_a), (keep_b, got_b) = scatter_far([dn_blocks[0], dn_blocks[1]])
    dn_own = sum_tp(
        whole_call(
            pieces_kernel, piece * tp, [rank_t, keep_a, got_a, keep_b, got_b], rp * dp
        )
    )
    dn_pieces = gather_tp(dn_own.astype(BF))

    action_grads = jnp.concatenate(
        [
            grad_gu_action.reshape(n, ka, 2 * fa),
            grad_down_action.reshape(fa, n, ka).transpose(1, 2, 0),
        ],
        axis=2,
    ).reshape(n, extra, kp)
    grad_gu, grad_down = weight_grads(
        normed_odd, normed_even, cot_odd, cot_even, h_odd, h_even, g_odd, g_even, action_grads
    )
    ranks = s ^ jnp.arange(n, dtype=jnp.int32)
    odd_bits = ranks & 1
    places = []
    for number in range(2):
        table = [0] * n
        for i, k in enumerate(block_order(number)):
            table[k] = table[k ^ 1] = number * (n // 2) + i
        places.append(jnp.array(table, jnp.int32)[ranks])
    lift_places = [p + (1 - odd_bits) * n for p in places]
    lifted = lift(
        odd_bits, *places, *lift_places, h_odd, h_even, lifted_action, down, half, ra
    )
    lifted_home = lax.psum_scatter(after(lifted, got_a), "seq", scatter_dimension=0)
    grad_gu, grad_down = after((grad_gu, grad_down), got_a)
    grad_gu_home = lax.all_to_all(grad_gu.reshape(n, kp, 2 * fp), "seq", 0, 0)
    grad_down_home = lax.all_to_all(grad_down, "seq", 0, 0)

    row = ((1, dp), F32)
    row_a = ((1, da), F32)
    dbranch_p, dbranch_a, dresid, mlp_gains_p, mlp_gains_a, dmixed = whole_call(
        middle_back_kernel,
        (((rp, dp), BF), ((ra, da), BF), ((rows, cp), F32), row, row_a, ((rows, width), BF)),
        [rank_t, *dn_pieces, mid_p, mid_a, mlp_gain_p, mlp_gain_a, cot_prefix, cot_action, got_out],
        2 * rows * dp * width,
        scratch=(
            pltpu.VMEM((rp, dp), BF),
            pltpu.VMEM((ra, da), BF),
            pltpu.VMEM((rp, dp), F32),
            pltpu.VMEM((ra, da), F32),
        ),
    )
    dquery, *dkv_parts = whole_call(
        attend_back_kernel,
        (((rows, width), BF),) + (((n * rows // 4, 2 * HD), BF),) * 4,
        [queries, keys_values, query_code, key_code, attended, log_sum, dmixed],
        10 * rows * width * n * rows,
        limit=56,
        transcendentals=rows * width // HD * n * rows,
    )
    dkv_even = [
        (e.astype(F32) + swap(o, "seq", 1).astype(F32)).astype(BF).reshape(n // 2, half, 2 * HD)
        for e, o in ((dkv_parts[0], dkv_parts[1]), (dkv_parts[2], dkv_parts[3]))
    ]
    dkv = [part for pair in scatter_far(dkv_even) for part in pair]
    (out_grads,) = whole_call(
        out_grad_kernel,
        (((n, kp + ka, width), BF),),
        [dbranch_p, dbranch_a, mixed],
        2 * rows * dp * width,
    )
    out_home = lax.psum_scatter(out_grads, "seq", scatter_dimension=0).astype(F32)
    tall = (kp + ka) // 2 + 8
    *groups_and_pieces, = whole_call(
        lambda *refs: front_back_kernel(width, *refs),
        (((n // 2, tall, qkv_width), BF),) * 4 + (((rows + 8, cp), BF),) * tp,
        [
            rank_s, rank_t, dquery, *dkv, x_full_p, x_full_a, inverse1, attn_gain_p, attn_gain_a,
            got_qkv, mlp_gains_p, mlp_gains_a,
        ],
        4 * rows * dp * qkv_width,
        scratch=(
            pltpu.VMEM((dp, qkv_width), BF),
            pltpu.VMEM((da, qkv_width), BF),
            pltpu.VMEM((n, 8, qkv_width), F32),
            pltpu.VMEM((rp, dp), F32),
            pltpu.VMEM((ra, da), F32),
        ),
    )
    groups, pieces = groups_and_pieces[:4], groups_and_pieces[4:]
    grad_x_p, grad_x_a = whole_call(
        grad_x_kernel,
        (((rp, cp), BF), ((ra, ca), BF)),
        [
            rank_t, pieces[0], *[swap(pieces[k], "tp", k) for k in range(1, tp)], x_pack,
            inverse1, attn_gain_p, attn_gain_a, dresid,
        ],
        rp * dp,
    )
    group_even = [
        (e.astype(F32) + swap(o, "seq", 1).astype(F32)).astype(BF)
        for e, o in ((groups[2 * 0], groups[2]), (groups[1], groups[3]))
    ]
    qkv_a, qkv_b = [
        keep.astype(F32) + got.astype(F32) for keep, got in scatter_far(group_even)
    ]
    hp, ha = kp // 2, ka // 2
    qkv_home_p = jnp.concatenate([qkv_a[:hp], qkv_b[:hp]], axis=0)
    qkv_home_a = jnp.concatenate([qkv_a[hp : hp + ha], qkv_b[hp : hp + ha]], axis=0)
    gains_home = qkv_a[hp + ha :]
    qp, qa = kp // tp, ka // tp
    attn_gains = jnp.pad(gains_home[:1, :512], ((0, 7), (0, 0)))

    def shared_piece(rank):
        return jnp.concatenate(
            [
                lax.dynamic_slice_in_dim(qkv_home_p[:, width:], rank * qp, qp, 0),
                lax.dynamic_slice_in_dim(qkv_home_a[:, width:], rank * qa, qa, 0),
                attn_gains,
            ],
            axis=0,
        )

    shared_home = sum_tp([shared_piece(t ^ k) for k in range(tp)])
    attn_gains_home = shared_home[qp + qa]

    def own_piece(rank):
        return jnp.concatenate(
            [
                lax.dynamic_slice(lifted_home, (0, rank * cp), (rp, cp)),
                jnp.pad(
                    lax.dynamic_slice(lifted_home, (rp, rank * ca), (ra, ca)),
                    ((0, 0), (0, cp - ca)),
                ),
            ],
            axis=0,
        )

    output = (residual + sum_tp([own_piece(t ^ k) for k in range(tp)])).astype(BF)
    grad_gate_p, grad_up_p = home(grad_gu_home)
    grad_down_p = grad_down_home[:, :fp].astype(F32).reshape(n * fp, kp)
    action_home = grad_down_home[:, fp:].reshape(n, ka, 3 * fa).astype(F32)

    def units(part):
        return part.transpose(1, 0, 2).reshape(ka, n * fa)

    grad_gate_a = units(action_home[:, :, :fa])
    grad_up_a = units(action_home[:, :, fa : 2 * fa])
    grad_down_a = action_home[:, :, 2 * fa :].transpose(0, 2, 1).reshape(n * fa, ka)
    return (
        output[:rp],
        output[rp:, :ca],
        grad_x_p,
        grad_x_a,
        attn_gains_home[:kp],
        qkv_home_p[:, :width],
        shared_home[:qp, :HD],
        shared_home[:qp, HD:],
        out_home[:kp].T,
        gains_home[0, 512 : 512 + kp],
        grad_gate_p,
        grad_up_p,
        grad_down_p,
        attn_gains_home[256 : 256 + ka],
        qkv_home_a[:, :width],
        shared_home[qp : qp + qa, :HD],
        shared_home[qp : qp + qa, HD:],
        out_home[kp:].T,
        gains_home[0, 768 : 768 + ka],
        grad_gate_a,
        grad_up_a,
        grad_down_a,
    )


def solution(mesh):
    split = P("seq", "tp")
    turned = P("tp", "seq")
    both = P(("seq", "tp"), None)
    one = P("seq")
    rows = P("seq", None)
    stream_in = (one, split, rows, rows, turned, one, split, split, turned)
    stream_out = (one, split, both, both, turned, one, split, split, turned)
    return jax.shard_map(
        shards,
        mesh=mesh,
        in_specs=(split, split, P()) + stream_in + stream_in + (rows, rows),
        out_specs=(split, split, split, split) + stream_out + stream_out,
        check_vma=False,
    )
```

```python
import jax
import jax.numpy as jnp
from jax import lax
from jax.experimental import pallas as pl
from jax.experimental.pallas import tpu as pltpu
from jax.sharding import PartitionSpec as P

HD = 256
IMG = 768
TXT = 48
ACT = 50
EPS = 1e-06
NEG = -1e30
BF = jnp.bfloat16
F32 = jnp.float32
MIB = 1 << 20


def swap(value, axis, mask):
    count = lax.axis_size(axis)
    return lax.ppermute(value, axis, [(i, i ^ mask) for i in range(count)])


def after(values, *tokens):
    return lax.optimization_barrier((values, tokens))[0]


def far_masks():
    count = lax.axis_size("seq")
    masks = [1 << b for b in range(1, count.bit_length() - 1)]
    return masks, masks[::-1]


def block_order(number):
    order = [0]
    for mask in far_masks()[number]:
        order = order + [k ^ mask for k in order]
    return order


def gather_far(halves):
    results = []
    for half, masks in zip(halves, far_masks()):
        blocks = [half]
        for mask in masks:
            blocks = blocks + [swap(b, "seq", mask) for b in blocks]
        results.append(blocks)
    return results


def near_rows(far):
    even = jnp.concatenate([b for blocks in far for b in blocks], axis=0)
    return swap(even, "seq", 1), even


def add(left, right):
    return left.astype(F32) + right.astype(F32)


def scatter_rows(halves, token=None):
    results = []
    for (mine, other), masks in zip(halves, far_masks()):
        for mask in masks[:0:-1]:
            keep = mine.shape[0] // 2
            got = swap(add(mine[keep:], other[keep:]).astype(BF), "seq", mask)
            mine, other = add(mine[:keep], other[:keep]), got
        sent = add(mine[1], other[1]).astype(BF)
        if token is not None:
            sent = after(sent, token)
        got = swap(sent, "seq", masks[0])
        results.append((add(mine[0], other[0]), got))
    return results


def gather_tp(piece):
    return [piece] + [swap(piece, "tp", k) for k in range(1, lax.axis_size("tp"))]


def sum_tp(pieces):
    total = pieces[0].astype(F32)
    for k in range(1, len(pieces)):
        total = total + swap(pieces[k].astype(BF), "tp", k).astype(F32)
    return total


def dot(left, right):
    return jnp.dot(left, right, preferred_element_type=F32)


def dot_t(left, right):
    return lax.dot_general(left, right, (((1,), (1,)), ((), ())), preferred_element_type=F32)


def t_dot(left, right):
    return lax.dot_general(left, right, (((0,), (0,)), ((), ())), preferred_element_type=F32)


def whole_call(kernel, outs, args, flops, scratch=(), limit=48, transcendentals=0):
    specs = [
        pl.BlockSpec(memory_space=pltpu.SMEM if a.ndim == 1 else pltpu.VMEM) for a in args
    ]
    outs = tuple(jax.ShapeDtypeStruct(shape, dtype) for shape, dtype in outs)
    moved = sum(a.size * a.dtype.itemsize for a in args)
    moved += sum(o.size * o.dtype.itemsize for o in outs)
    return pl.pallas_call(
        kernel,
        out_shape=outs,
        in_specs=specs,
        out_specs=tuple(pl.BlockSpec(memory_space=pltpu.VMEM) for _ in outs),
        scratch_shapes=list(scratch),
        compiler_params=pltpu.CompilerParams(vmem_limit_bytes=limit * MIB),
        cost_estimate=pl.CostEstimate(
            flops=int(flops), bytes_accessed=int(moved), transcendentals=int(transcendentals)
        ),
    )(*args)


def inverse_rms(values):
    return lax.rsqrt(jnp.mean(values * values, axis=1, keepdims=True) + EPS)


def place(rank, width):
    return pl.ds(pl.multiple_of(rank * width, width), width)


def token_codes(prefix_segment, seq_count, suf_rows):
    items_all = prefix_segment.shape[0] // (IMG + TXT)
    places = jnp.arange(seq_count * suf_rows, dtype=jnp.int32)
    items_of = places // (ACT + 1)
    suffix_seg = jnp.where(items_of < items_all, items_of, items_all)
    suffix_lvl = jnp.where((items_of < items_all) & (places % (ACT + 1) == 0), 1, 2)
    suffix = (suffix_seg * 4 + suffix_lvl).astype(jnp.int32)
    return jnp.concatenate(
        [(prefix_segment * 4).reshape(seq_count, -1), suffix.reshape(seq_count, -1)], axis=1
    )


def front_kernel(t_ref, *refs):
    tp = lax.axis_size("tp")
    xs = refs[:tp]
    w_ref, gp_ref, ga_ref, q_ref, kva_ref, kvb_ref, xp_ref, xa_ref, inv_ref = refs[tp:]
    rp, dp = xp_ref.shape
    ra, da = xa_ref.shape
    cp, ca = dp // tp, da // tp
    kp, ka = dp // w_ref.shape[0], da // w_ref.shape[0]
    width = q_ref.shape[1]
    half = kva_ref.shape[0]
    for k in range(tp):
        xp_ref[:, place(t_ref[0] ^ k, cp)] = xs[k][:rp, :]
        xa_ref[:, place(t_ref[0] ^ k, ca)] = xs[k][rp:, :ca]
    parts = []
    inverses = []
    for x_ref, g_ref, first, last, size in (
        (xp_ref, gp_ref, 0, kp, dp),
        (xa_ref, ga_ref, kp, kp + ka, da),
    ):
        rows = x_ref[...].astype(F32)
        inverse = inverse_rms(rows)
        normed = (rows * inverse * g_ref[...]).astype(BF)
        parts.append(dot(normed, w_ref[:, first:last, :].reshape(size, -1)))
        inverses.append(inverse)
    qkv = jnp.concatenate(parts, axis=0)
    q_ref[...] = qkv[:, :width].astype(BF)
    kva_ref[...] = qkv[:half, width:].astype(BF)
    kvb_ref[...] = qkv[half:, width:].astype(BF)
    inv_ref[...] = jnp.broadcast_to(jnp.concatenate(inverses, axis=0), inv_ref.shape)


def key_step(count):
    for step in (2176, 1088, 544, 272):
        if count % step == 0:
            return step
    return count


def attend_kernel(q_ref, kv_ref, qc_ref, kc_ref, att_ref, mix_ref, lse_ref):
    rows = q_ref.shape[0]
    heads = q_ref.shape[1] // HD
    count = kv_ref.shape[0]
    step = key_step(count)
    code = qc_ref[...]
    low = code - code % 4
    for h in range(heads):
        query = q_ref[:, h * HD : (h + 1) * HD] * BF(HD**-0.5)
        top = jnp.full((rows, 1), NEG, F32)
        mass = jnp.zeros((rows, 1), F32)
        total = jnp.zeros((rows, HD), F32)
        for begin in range(0, count, step):
            keys = kv_ref[begin : begin + step, :HD]
            marks = kc_ref[:, begin : begin + step]
            allowed = (marks >= low) & (marks <= code)
            scores = jnp.where(allowed, dot_t(query, keys), NEG)
            new_top = jnp.maximum(top, jnp.max(scores, axis=1, keepdims=True))
            expo = jnp.where(allowed, jnp.exp(scores - new_top), 0.0)
            shrink = jnp.exp(top - new_top)
            mass = mass * shrink + jnp.sum(expo, axis=1, keepdims=True)
            total = total * shrink + dot(expo.astype(BF), kv_ref[begin : begin + step, HD:])
            top = new_top
        attended = total / mass
        att_ref[:, h * HD : (h + 1) * HD] = attended
        mix_ref[:, h * HD : (h + 1) * HD] = attended.astype(BF)
        lse_ref[:, h * 128 : (h + 1) * 128] = jnp.broadcast_to(top + jnp.log(mass), (rows, 128))


def attend_back_kernel(
    q_ref, kv_ref, qc_ref, kc_ref, att_ref, lse_ref, dm_ref, dq_ref, *dkv_refs
):
    rows = q_ref.shape[0]
    heads = q_ref.shape[1] // HD
    count = kv_ref.shape[0]
    step = key_step(count)
    each = dkv_refs[0].shape[0]
    code = qc_ref[...]
    low = code - code % 4
    dq = [jnp.zeros((rows, HD), F32) for _ in range(heads)]
    for begin in range(0, count, step):
        keys = kv_ref[begin : begin + step, :HD]
        vals = kv_ref[begin : begin + step, HD:]
        marks = kc_ref[:, begin : begin + step]
        allowed = (marks >= low) & (marks <= code)
        dk = jnp.zeros((step, HD), F32)
        dv = jnp.zeros((step, HD), F32)
        for h in range(heads):
            span = slice(h * HD, (h + 1) * HD)
            query = q_ref[:, span] * BF(HD**-0.5)
            dmix = dm_ref[:, span]
            delta = jnp.sum(dmix.astype(F32) * att_ref[:, span], axis=1, keepdims=True)
            scores = dot_t(query, keys)
            probs = jnp.where(allowed, jnp.exp(scores - lse_ref[:, h * 128 : h * 128 + 1]), 0.0)
            dscores = (probs * (dot_t(dmix, vals) - delta)).astype(BF)
            dq[h] = dq[h] + dot(dscores, keys)
            dk = dk + t_dot(dscores, query)
            dv = dv + t_dot(probs.astype(BF), dmix)
        dkv = jnp.concatenate([dk, dv], axis=1).astype(BF)
        for part in range(len(dkv_refs)):
            first, last = max(begin, part * each), min(begin + step, (part + 1) * each)
            if first < last:
                dkv_refs[part][first - part * each : last - part * each, :] = dkv[
                    first - begin : last - begin
                ]
    for h in range(heads):
        dq_ref[:, h * HD : (h + 1) * HD] = (dq[h] * HD**-0.5).astype(BF)


def branch_kernel(t_ref, mix_ref, w_ref, *outs):
    tp = len(outs)
    n = w_ref.shape[0]
    cp = outs[0].shape[1]
    ra = mix_ref.shape[0] - (outs[0].shape[0] - 16)
    rp = mix_ref.shape[0] - ra
    kp = cp * tp // n
    for k in range(tp):
        rank = t_ref[0] ^ k
        blocks = w_ref[pl.ds(rank * (n // tp), n // tp)]
        prefix = dot_t(mix_ref[:rp, :], blocks[:, :kp].reshape(cp, -1))
        action = dot_t(mix_ref[rp:, :], blocks[:, kp:].reshape(-1, mix_ref.shape[1]))
        outs[k][:rp, :] = prefix.astype(BF)
        outs[k][rp:, :] = jnp.concatenate(
            [action, jnp.zeros((ra, cp - action.shape[1]), F32)], axis=1
        ).astype(BF)


def middle_kernel(t_ref, *refs):
    tp = lax.axis_size("tp")
    mids = refs[:tp]
    gp_ref, ga_ref, mp_ref, ma_ref, a_ref, b_ref = refs[tp:]
    rp, dp = mp_ref.shape
    ra, da = ma_ref.shape
    cp, ca = dp // tp, da // tp
    for k in range(tp):
        mp_ref[:, place(t_ref[0] ^ k, cp)] = mids[k][:rp, :]
        ma_ref[:, place(t_ref[0] ^ k, ca)] = mids[k][rp:, :ca]
    rows = mp_ref[...].astype(F32)
    prefix = rows * inverse_rms(rows) * gp_ref[...]
    rows = ma_ref[...].astype(F32)
    action = rows * inverse_rms(rows) * ga_ref[...]
    action = jnp.concatenate([action, jnp.zeros((ra, dp - da), F32)], axis=1)
    for number, out in enumerate((a_ref, b_ref)):
        out[...] = jnp.concatenate(
            [
                prefix[number * (rp // 2) : (number + 1) * (rp // 2)],
                action[number * (ra // 2) : (number + 1) * (ra // 2)],
            ],
            axis=0,
        ).astype(BF)


def gelu_parts(value):
    scale = 0.7978845608028654
    square = value * value
    bent = jnp.tanh(scale * (value + 0.044715 * value * square))
    gelu = 0.5 * value * (1.0 + bent)
    slope = 0.5 * (1.0 + bent) + 0.5 * value * (1.0 - bent * bent) * scale * (
        1.0 + 3.0 * 0.044715 * square
    )
    return gelu, slope


def forward_back(rows, cot_rows, gate_up, down):
    f = down.shape[0]
    both = dot(rows, gate_up)
    gelu, slope = gelu_parts(both[:, :f])
    up = both[:, f:]
    dhidden = dot_t(cot_rows, down)
    return gelu * up, jnp.concatenate([dhidden * up * slope, dhidden * gelu], axis=1)


def feed_kernel(pair, x_ref, c_ref, w_ref, d_ref, act_ref, h_ref, g_ref, dn_ref):
    rows, dp = x_ref.shape
    each = rows // pair
    prefix = each - act_ref.shape[0] // pair
    hidden, dgate_up = forward_back(x_ref[...], c_ref[...], w_ref[...], d_ref[...])
    inside = lax.broadcasted_iota(jnp.int32, (rows, 1), 0) % each < prefix
    dgate_up = jnp.where(inside, dgate_up, 0.0).astype(BF)
    h_ref[...] = jnp.where(inside, hidden, 0.0).astype(BF)
    g_ref[...] = dgate_up
    dn = dot_t(dgate_up, w_ref[...])
    action = act_ref[...]
    action = jnp.concatenate(
        [action, jnp.zeros((action.shape[0], dp - action.shape[1]), F32)], axis=1
    )
    pieces = []
    for i in range(pair):
        pieces.append(dn[i * each : i * each + prefix])
        pieces.append(action[i * (each - prefix) : (i + 1) * (each - prefix)])
    dn_ref[...] = jnp.concatenate(pieces, axis=0).astype(BF)


def feed(rows_in, cot_rows, gate_up, down, dn_action, each):
    total, dp = rows_in.shape
    pair = 2
    step = pair * each
    f = down.shape[0]
    act_step = dn_action.shape[0] * step // total
    row_spec = pl.BlockSpec((step, dp), lambda i: (i, 0))
    in_specs = [
        row_spec,
        row_spec,
        pl.BlockSpec(gate_up.shape, lambda i: (0, 0)),
        pl.BlockSpec(down.shape, lambda i: (0, 0)),
        pl.BlockSpec((act_step, dn_action.shape[1]), lambda i: (i, 0)),
    ]
    return pl.pallas_call(
        lambda *refs: feed_kernel(pair, *refs),
        grid=(total // step,),
        in_specs=in_specs,
        out_specs=(
            pl.BlockSpec((step, f), lambda i: (i, 0)),
            pl.BlockSpec((step, 2 * f), lambda i: (i, 0)),
            row_spec,
        ),
        out_shape=(
            jax.ShapeDtypeStruct((total, f), BF),
            jax.ShapeDtypeStruct((total, 2 * f), BF),
            jax.ShapeDtypeStruct((total, dp), BF),
        ),
        compiler_params=pltpu.CompilerParams(vmem_limit_bytes=48 * MIB),
        cost_estimate=pl.CostEstimate(
            flops=10 * total * dp * f,
            bytes_accessed=8 * total * dp + 6 * f * dp,
            transcendentals=total * f,
        ),
    )(rows_in, cot_rows, gate_up, down, dn_action)


def feed_action_kernel(x_ref, c_ref, w_ref, d_ref, dn_ref, lift_ref, gw_ref, gd_ref):
    rows, cot_rows = x_ref[...], c_ref[...]
    hidden, dgate_up = forward_back(rows, cot_rows, w_ref[...], d_ref[...])
    hidden, dgate_up = hidden.astype(BF), dgate_up.astype(BF)
    dn_ref[...] = dot_t(dgate_up, w_ref[...])
    lift_ref[...] = dot(hidden, d_ref[...])
    gw_ref[...] = t_dot(rows, dgate_up).astype(BF)
    gd_ref[...] = t_dot(hidden, cot_rows).astype(BF)


def weights_kernel(
    xo_ref, xe_ref, co_ref, ce_ref, ho_ref, he_ref, go_ref, ge_ref, act_ref, gw_ref, gd_ref
):
    f = ho_ref.shape[1]
    kp = gd_ref.shape[2]
    gw_ref[...] = (t_dot(xo_ref[...], go_ref[...]) + t_dot(xe_ref[...], ge_ref[...])).astype(BF)
    down = (t_dot(ho_ref[...], co_ref[...]) + t_dot(he_ref[...], ce_ref[...])).astype(BF)
    for i in range(gd_ref.shape[0]):
        gd_ref[i, :f, :] = down[:, i * kp : (i + 1) * kp]
        gd_ref[i, f:, :] = act_ref[i]


def weight_grads(x_odd, x_even, c_odd, c_even, h_odd, h_even, g_odd, g_even, action):
    total, dp = x_odd.shape
    f = h_odd.shape[1]
    n, extra, kp = action.shape
    wide = 256
    cols = pl.BlockSpec((total, wide), lambda i: (0, i))
    h_spec = pl.BlockSpec((total, f), lambda i: (0, 0))
    g_spec = pl.BlockSpec((total, 2 * f), lambda i: (0, 0))
    return pl.pallas_call(
        weights_kernel,
        grid=(dp // wide,),
        in_specs=[
            cols,
            cols,
            cols,
            cols,
            h_spec,
            h_spec,
            g_spec,
            g_spec,
            pl.BlockSpec((wide // kp, extra, kp), lambda i: (i, 0, 0)),
        ],
        out_specs=(
            pl.BlockSpec((wide, 2 * f), lambda i: (i, 0)),
            pl.BlockSpec((wide // kp, f + extra, kp), lambda i: (i, 0, 0)),
        ),
        out_shape=(
            jax.ShapeDtypeStruct((dp, 2 * f), BF),
            jax.ShapeDtypeStruct((n, f + extra, kp), BF),
        ),
        compiler_params=pltpu.CompilerParams(vmem_limit_bytes=48 * MIB),
        cost_estimate=pl.CostEstimate(
            flops=12 * total * dp * f, bytes_accessed=8 * total * dp, transcendentals=0
        ),
    )(x_odd, x_even, c_odd, c_even, h_odd, h_even, g_odd, g_even, action)


def lift_kernel(
    odd_ref, pa_ref, pb_ref, la_ref, lb_ref,
    oa_ref, ea_ref, ob_ref, eb_ref, aa_ref, ab_ref, d_ref, out_ref,
):
    odd = odd_ref[pl.program_id(0)] == 1
    dp = out_ref.shape[2]
    prefix = oa_ref.shape[0] - aa_ref.shape[0]
    outs = []
    for o_ref, e_ref in ((oa_ref, ea_ref), (ob_ref, eb_ref)):
        hidden = jnp.where(odd, o_ref[...].astype(F32), e_ref[...].astype(F32)).astype(BF)
        outs.append(dot(hidden, d_ref[...])[:prefix])
    action = jnp.concatenate([aa_ref[...], ab_ref[...]], axis=0)
    action = jnp.concatenate(
        [action, jnp.zeros((action.shape[0], dp - action.shape[1]), F32)], axis=1
    )
    out_ref[0] = jnp.concatenate(outs + [action], axis=0).astype(BF)


def lift(odd, place_a, place_b, lift_a, lift_b, h_odd, h_even, lifted_action, down, each, ra):
    n = odd.shape[0]
    f, dp = down.shape
    da = lifted_action.shape[1]
    a_spec = pl.BlockSpec((each, f), lambda j, o, a, b, la, lb: (a[j], 0))
    b_spec = pl.BlockSpec((each, f), lambda j, o, a, b, la, lb: (b[j], 0))
    rows = 2 * each
    return pl.pallas_call(
        lift_kernel,
        grid_spec=pltpu.PrefetchScalarGridSpec(
            num_scalar_prefetch=5,
            grid=(n,),
            in_specs=[
                a_spec,
                a_spec,
                b_spec,
                b_spec,
                pl.BlockSpec((ra // 2, da), lambda j, o, a, b, la, lb: (la[j], 0)),
                pl.BlockSpec((ra // 2, da), lambda j, o, a, b, la, lb: (lb[j], 0)),
                pl.BlockSpec((f, dp), lambda j, o, a, b, la, lb: (0, 0)),
            ],
            out_specs=pl.BlockSpec((1, rows, dp), lambda j, o, a, b, la, lb: (j, 0, 0)),
        ),
        out_shape=jax.ShapeDtypeStruct((n, rows, dp), BF),
        compiler_params=pltpu.CompilerParams(vmem_limit_bytes=32 * MIB),
        cost_estimate=pl.CostEstimate(
            flops=2 * n * rows * dp * f, bytes_accessed=2 * n * rows * dp, transcendentals=0
        ),
    )(odd, place_a, place_b, lift_a, lift_b, h_odd, h_even, h_odd, h_even,
      lifted_action, lifted_action, down)


def pieces_kernel(t_ref, ka_ref, ga_ref, kb_ref, gb_ref, *outs):
    tp = len(outs)
    each, dp = ka_ref.shape
    cp = dp // tp
    rp = outs[0].shape[0] * 2 * each // (2 * each)
    extra = 8
    prefix = each - extra
    ca = outs[0].shape[1] // 2
    del rp
    for k in range(tp):
        rank = t_ref[0] ^ k
        tops, ends = [], []
        for keep, got in ((ka_ref, ga_ref), (kb_ref, gb_ref)):
            wide = place(rank, cp)
            tops.append(keep[:prefix, wide].astype(F32) + got[:prefix, wide].astype(F32))
            slim = place(rank, ca)
            ends.append(
                keep[prefix:, slim].astype(F32) + got[prefix:, slim].astype(F32)
            )
        action = jnp.concatenate(ends, axis=0)
        action = jnp.concatenate(
            [action, jnp.zeros((action.shape[0], cp - ca), F32)], axis=1
        )
        outs[k][...] = jnp.concatenate(tops + [action], axis=0).astype(BF)


def middle_back_kernel(t_ref, *refs):
    tp = lax.axis_size("tp")
    ds = refs[:tp]
    mp_ref, ma_ref, gp_ref, ga_ref, cp_ref, ca_ref, w_ref = refs[tp : tp + 7]
    bp_ref, ba_ref, own_ref, lp_ref, la_ref, dm_ref, dp_scr, da_scr, rp_scr, ra_scr = refs[tp + 7 :]
    rp, dp = mp_ref.shape
    ra, da = ma_ref.shape
    cp, ca = dp // tp, da // tp
    n = w_ref.shape[0]
    kp = dp // n
    t = t_ref[0]
    for k in range(tp):
        dp_scr[:, place(t ^ k, cp)] = ds[k][:rp, :]
        da_scr[:, place(t ^ k, ca)] = ds[k][rp:, :ca]
    mixes = []
    for d_ref, m_ref, g_ref, c_ref, b_ref, r_ref, l_ref, first, last in (
        (dp_scr, mp_ref, gp_ref, cp_ref, bp_ref, rp_scr, lp_ref, 0, kp),
        (da_scr, ma_ref, ga_ref, ca_ref, ba_ref, ra_scr, la_ref, kp, w_ref.shape[1]),
    ):
        gradient = d_ref[...].astype(F32)
        rows = m_ref[...].astype(F32)
        inverse = inverse_rms(rows)
        centered = rows * inverse
        inner = gradient * g_ref[...]
        dresid = c_ref[...].astype(F32) + inverse * (
            inner - centered * jnp.mean(inner * centered, axis=1, keepdims=True)
        )
        l_ref[...] = jnp.sum(gradient * centered, axis=0, keepdims=True)
        r_ref[...] = dresid
        branch = dresid.astype(BF)
        b_ref[...] = branch
        mixes.append(dot(branch, w_ref[:, first:last, :].reshape(rows.shape[1], -1)))
    dm_ref[...] = jnp.concatenate(mixes, axis=0).astype(BF)
    own_ref[:rp, :] = rp_scr[:, place(t, cp)]
    own_ref[rp:, :] = jnp.concatenate(
        [ra_scr[:, place(t, ca)], jnp.zeros((ra, cp - ca), F32)], axis=1
    )


def out_grad_kernel(bp_ref, ba_ref, mix_ref, out_ref):
    rp, dp = bp_ref.shape
    n = out_ref.shape[0]
    kp = dp // n
    width = mix_ref.shape[1]
    out_ref[:, :kp, :] = t_dot(bp_ref[...], mix_ref[:rp, :]).astype(BF).reshape(n, kp, width)
    out_ref[:, kp:, :] = t_dot(ba_ref[...], mix_ref[rp:, :]).astype(BF).reshape(n, -1, width)


def front_back_kernel(heads_width, s_ref, t_ref, dq_ref, *refs):
    tp = lax.axis_size("tp")
    n = lax.axis_size("seq")
    (ka_ref, ra_ref, kb_ref, rb_ref, xp_ref, xa_ref, inv_ref, gp_ref, ga_ref, w_ref, lp_ref,
     la_ref) = refs[:12]
    groups = refs[12:16]
    pieces = refs[16 : 16 + tp]
    gwp_scr, gwa_scr, gain_scr, dp_scr, da_scr = refs[16 + tp :]
    rp, dp = xp_ref.shape
    ra, da = xa_ref.shape
    kp, ka = dp // n, da // n
    cp, ca = dp // tp, da // tp
    width = heads_width
    dkv = jnp.concatenate(
        [
            ka_ref[...].astype(F32) + ra_ref[...].astype(F32),
            kb_ref[...].astype(F32) + rb_ref[...].astype(F32),
        ],
        axis=0,
    )
    dqkv = jnp.concatenate([dq_ref[...].astype(F32), dkv], axis=1)
    gain_scr[...] = jnp.zeros(gain_scr.shape, F32)
    dots = []
    for x_ref, g_ref, d_scr, gw_scr, l_ref, begin, end, first, last, size, at in (
        (xp_ref, gp_ref, dp_scr, gwp_scr, lp_ref, 0, rp, 0, kp, kp, 0),
        (xa_ref, ga_ref, da_scr, gwa_scr, la_ref, rp, rp + ra, kp, kp + ka, ka, 256),
    ):
        grad_rows = dqkv[begin:end].astype(BF)
        centered = x_ref[...].astype(F32) * inv_ref[begin:end, :1]
        normed = (centered * g_ref[...]).astype(BF)
        gw_scr[...] = t_dot(normed, grad_rows).astype(BF)
        weights = w_ref[:, first:last, :].reshape(x_ref.shape[1], -1)
        partial = dot_t(grad_rows, weights)
        d_scr[...] = partial
        product = partial * centered
        gains = jnp.sum(product, axis=0, keepdims=True)
        mlp_gains = l_ref[...]
        for d in range(n):
            gain_scr[d, 0:1, at : at + size] = gains[:, d * size : (d + 1) * size]
            gain_scr[d, 0:1, at + 512 : at + 512 + size] = mlp_gains[
                :, d * size : (d + 1) * size
            ]
        dots.append(jnp.sum(product * g_ref[...], axis=1, keepdims=True))
    column = jnp.concatenate(dots, axis=0)
    lanes = lax.broadcasted_iota(jnp.int32, (rp + ra, cp), 1)
    rows = lax.broadcasted_iota(jnp.int32, (rp + ra, cp), 0)
    row = jnp.sum(jnp.where(lanes == rows, column, 0.0), axis=0, keepdims=True)
    high = row.astype(BF).astype(F32)
    tail = jnp.concatenate([high, row - high, jnp.zeros((6, cp), F32)], axis=0)
    for k in range(tp):
        rank = t_ref[0] ^ k
        action = jnp.concatenate(
            [da_scr[:, place(rank, ca)], jnp.zeros((ra, cp - ca), F32)], axis=1
        )
        pieces[k][...] = jnp.concatenate([dp_scr[:, place(rank, cp)], action, tail], axis=0).astype(
            BF
        )
    for odd in range(2):
        for number in range(2):
            out = groups[2 * odd + number]
            for i, k in enumerate(block_order(number)):
                d = s_ref[0] ^ (k ^ odd)
                hp, ha = kp // 2, ka // 2
                out[i, :hp, :] = gwp_scr[
                    pl.ds(pl.multiple_of(d * kp + number * hp, hp), hp), :
                ]
                out[i, hp : hp + ha, :] = gwa_scr[
                    pl.ds(pl.multiple_of(d * ka + number * ha, ha), ha), :
                ]
                out[i, hp + ha :, :] = gain_scr[d].astype(BF) * BF(1 - number)


def grad_x_kernel(t_ref, *refs):
    tp = lax.axis_size("tp")
    ds = refs[:tp]
    x_ref, inv_ref, gp_ref, ga_ref, r_ref, op_ref, oa_ref = refs[tp:]
    rp, cp = op_ref.shape
    ra, ca = oa_ref.shape
    t = t_ref[0]
    total = ds[0][...].astype(F32)
    for k in range(1, tp):
        total = total + ds[k][...].astype(F32)
    row = total[rp + ra : rp + ra + 1] + total[rp + ra + 1 : rp + ra + 2]
    lanes = lax.broadcasted_iota(jnp.int32, (rp + ra, cp), 1)
    rows = lax.broadcasted_iota(jnp.int32, (rp + ra, cp), 0)
    column = jnp.sum(jnp.where(lanes == rows, row, 0.0), axis=1, keepdims=True)
    for o_ref, g_ref, begin, end, wide in (
        (op_ref, gp_ref, 0, rp, cp),
        (oa_ref, ga_ref, rp, rp + ra, ca),
    ):
        inverse = inv_ref[begin:end, :1]
        centered = x_ref[begin:end, :wide].astype(F32) * inverse
        mean = column[begin:end] / (wide * tp)
        moved = inverse * (
            total[begin:end, :wide] * g_ref[:, place(t, wide)] - centered * mean
        )
        o_ref[...] = (r_ref[begin:end, :wide] + moved).astype(BF)


def home_kernel(in_ref, gate_ref, up_ref):
    f = gate_ref.shape[1]
    gate_ref[...] = in_ref[0, :, :f].astype(F32)
    up_ref[...] = in_ref[0, :, f:].astype(F32)


def home(got):
    n, kp, both = got.shape
    f = both // 2
    out = pl.BlockSpec((kp, f), lambda j: (0, j))
    return pl.pallas_call(
        home_kernel,
        grid=(n,),
        in_specs=[pl.BlockSpec((1, kp, both), lambda j: (j, 0, 0))],
        out_specs=(out, out),
        out_shape=(jax.ShapeDtypeStruct((kp, n * f), F32),) * 2,
        cost_estimate=pl.CostEstimate(
            flops=0, bytes_accessed=6 * n * kp * both, transcendentals=0
        ),
    )(got)


def shards(
    x_prefix,
    x_action,
    prefix_segment,
    prefix_attn_gain,
    prefix_query,
    prefix_key,
    prefix_value,
    prefix_out,
    prefix_mlp_gain,
    prefix_gate,
    prefix_up,
    prefix_down,
    action_attn_gain,
    action_query,
    action_key,
    action_value,
    action_out,
    action_mlp_gain,
    action_gate,
    action_up,
    action_down,
    cot_prefix,
    cot_action,
):
    n = lax.axis_size("seq")
    tp = lax.axis_size("tp")
    s = lax.axis_index("seq")
    t = lax.axis_index("tp")
    rank_t = t.astype(jnp.int32).reshape(1)
    rank_s = s.astype(jnp.int32).reshape(1)
    rp, cp = x_prefix.shape
    ra, ca = x_action.shape
    rows = rp + ra
    half = rows // 2
    dp, da = cp * tp, ca * tp
    kp, ka = dp // n, da // n
    width = prefix_query.shape[1]
    qkv_width = width + 2 * HD
    fp, fa = prefix_gate.shape[1] // n, action_gate.shape[1] // n

    x_pack = jnp.concatenate(
        [x_prefix, jnp.pad(x_action, ((0, 0), (0, cp - ca)))], axis=0
    )
    x_pieces = gather_tp(x_pack)
    gains = jnp.concatenate(
        [prefix_attn_gain, prefix_mlp_gain, action_attn_gain, action_mlp_gain]
    )
    gain_rows = -(-gains.shape[0] // qkv_width)
    gains = jnp.pad(gains, (0, 8 * qkv_width - gains.shape[0])).reshape(8, qkv_width)
    pack_qkv = jnp.concatenate(
        [
            jnp.concatenate([prefix_query, prefix_key, prefix_value], axis=1),
            jnp.concatenate([action_query, action_key, action_value], axis=1),
            gains,
        ],
        axis=0,
    )
    got_qkv = lax.all_gather(pack_qkv, "seq", axis=0)
    got_gains = got_qkv[:, kp + ka : kp + ka + gain_rows].reshape(n, -1).astype(F32)
    attn_gain_p = got_gains[:, :kp].reshape(1, dp)
    mlp_gain_p = got_gains[:, kp : 2 * kp].reshape(1, dp)
    attn_gain_a = got_gains[:, 2 * kp : 2 * kp + ka].reshape(1, da)
    mlp_gain_a = got_gains[:, 2 * kp + ka : 2 * kp + 2 * ka].reshape(1, da)
    pack_out = jnp.concatenate([prefix_out.T, action_out.T], axis=0)
    cot_wide = jnp.pad(cot_action, ((0, 0), (0, dp - da)))
    cot_far = gather_far(
        [
            jnp.concatenate(
                [
                    cot_prefix[i * (rp // 2) : (i + 1) * (rp // 2)],
                    cot_wide[i * (ra // 2) : (i + 1) * (ra // 2)],
                ],
                axis=0,
            )
            for i in range(2)
        ]
    )
    cot_odd, cot_even = near_rows(cot_far)

    def by_units(w, f):
        return w.reshape(w.shape[0], n, f).transpose(1, 0, 2)

    gate_up_sent = jnp.concatenate([by_units(prefix_gate, fp), by_units(prefix_up, fp)], axis=2)
    action_sent = jnp.concatenate(
        [
            by_units(action_gate, fa),
            by_units(action_up, fa),
            action_down.reshape(n, fa, ka).transpose(0, 2, 1),
        ],
        axis=2,
    ).reshape(n, -1, kp)
    extra = action_sent.shape[1]
    down_sent = jnp.concatenate([prefix_down.reshape(n, fp, kp), action_sent], axis=1)

    queries, kv_a, kv_b, x_full_p, x_full_a, inverse1 = whole_call(
        front_kernel,
        (
            ((rows, width), BF),
            ((half, 2 * HD), BF),
            ((half, 2 * HD), BF),
            ((rp, dp), BF),
            ((ra, da), BF),
            ((rows, 128), F32),
        ),
        [after(rank_t, cot_far[0][1], cot_far[1][1]), *x_pieces, got_qkv, attn_gain_p, attn_gain_a],
        2 * rp * dp * qkv_width,
    )
    kv_even = [jnp.concatenate(blocks, axis=0) for blocks in gather_far([kv_a, kv_b])]
    kv_odd = [swap(e, "seq", 1) for e in kv_even]
    keys_values = jnp.concatenate([kv_even[0], kv_odd[0], kv_even[1], kv_odd[1]], axis=0)
    codes = token_codes(prefix_segment, n, ra)
    query_code = lax.dynamic_slice_in_dim(codes, s, 1, 0).reshape(rows, 1)
    key_code = jnp.concatenate(
        [
            lax.dynamic_slice(codes, (s ^ k ^ odd, number * half), (1, half))
            for number in range(2)
            for odd in range(2)
            for k in block_order(number)
        ],
        axis=1,
    )
    attended, mixed, log_sum = whole_call(
        attend_kernel,
        (
            ((rows, width), F32),
            ((rows, width), BF),
            ((rows, width // HD * 128), F32),
        ),
        [queries, keys_values, query_code, key_code],
        4 * rows * width * n * rows,
        transcendentals=rows * width // HD * n * rows,
    )
    got_out = lax.all_gather(after(pack_out, queries), "seq", axis=0)
    down_got = lax.all_to_all(after(down_sent, keys_values), "seq", 0, 0)

    piece = (((rows, cp), BF),)
    branch = sum_tp(
        whole_call(
            branch_kernel, piece * tp, [after(rank_t, cot_far[0][-1], cot_far[1][-1]), mixed, got_out], 2 * rows * dp * width
        )
    )
    residual = x_pack.astype(F32) + branch
    mid_own = after(residual.astype(BF), down_got)
    gate_up = lax.all_to_all(after(gate_up_sent, branch), "seq", 0, 0).reshape(dp, 2 * fp)
    block = (((half, dp), BF),)
    mid_p, mid_a, normed_a, normed_b = whole_call(
        middle_kernel,
        (((rp, dp), BF), ((ra, da), BF)) + block * 2,
        [after(rank_t, gate_up), *gather_tp(mid_own), mlp_gain_p, mlp_gain_a],
        rp * dp,
    )

    normed_odd, normed_even = near_rows(gather_far([normed_a, normed_b]))
    down = down_got[:, :fp].transpose(1, 0, 2).reshape(fp, dp)
    action_got = down_got[:, fp:].reshape(da, 3 * fa)
    gate_up_action = action_got[:, : 2 * fa]
    down_action = action_got[:, 2 * fa :].T

    def action_rows(blocks):
        return blocks.reshape(n, half, dp)[:, rp // 2 :, :da].reshape(-1, da)

    normed_action = jnp.concatenate([action_rows(normed_odd), action_rows(normed_even)], axis=0)
    cot_action_all = jnp.concatenate([action_rows(cot_odd), action_rows(cot_even)], axis=0)
    tokens = n * ra
    dn_action, lifted_action, grad_gu_action, grad_down_action = whole_call(
        feed_action_kernel,
        (
            ((tokens, da), F32),
            ((tokens, da), F32),
            ((da, 2 * fa), BF),
            ((fa, da), BF),
        ),
        [normed_action, cot_action_all, gate_up_action, down_action],
        18 * tokens * da * fa,
    )
    h_odd, g_odd, dn_odd = feed(
        normed_odd, cot_odd, gate_up, down, dn_action[: tokens // 2], half
    )
    h_even, g_even, dn_even = feed(
        normed_even, cot_even, gate_up, down, dn_action[tokens // 2 :], half
    )
    dn_blocks = [
        d.reshape(2, n // 2, half, dp) for d in (dn_even, swap(dn_odd, "seq", 1))
    ]

    action_grads = jnp.concatenate(
        [
            grad_gu_action.reshape(n, ka, 2 * fa),
            grad_down_action.reshape(fa, n, ka).transpose(1, 2, 0),
        ],
        axis=2,
    ).reshape(n, extra, kp)
    grad_gu, grad_down = weight_grads(
        normed_odd, normed_even, cot_odd, cot_even, h_odd, h_even, g_odd, g_even, action_grads
    )
    ranks = s ^ jnp.arange(n, dtype=jnp.int32)
    odd_bits = ranks & 1
    places = []
    for number in range(2):
        table = [0] * n
        for i, k in enumerate(block_order(number)):
            table[k] = table[k ^ 1] = number * (n // 2) + i
        places.append(jnp.array(table, jnp.int32)[ranks])
    lift_places = [p + (1 - odd_bits) * n for p in places]
    lifted = lift(
        odd_bits, *places, *lift_places, h_odd, h_even, lifted_action, down, half, ra
    )
    (keep_a, got_a), (keep_b, got_b) = scatter_rows(
        [(dn_blocks[0][i], dn_blocks[1][i]) for i in range(2)], grad_gu
    )
    dn_own = sum_tp(
        whole_call(
            pieces_kernel,
            piece * tp,
            [after(rank_t, lifted), keep_a, got_a, keep_b, got_b],
            rp * dp,
        )
    )
    dn_pieces = gather_tp(dn_own.astype(BF))
    lifted_home = lax.psum_scatter(after(lifted, got_a, got_b), "seq", scatter_dimension=0)
    grad_gu, grad_down = after((grad_gu, grad_down), got_a, got_b)
    grad_gu_home = lax.all_to_all(grad_gu.reshape(n, kp, 2 * fp), "seq", 0, 0)
    grad_down_home = lax.all_to_all(grad_down, "seq", 0, 0)

    row = ((1, dp), F32)
    row_a = ((1, da), F32)
    dbranch_p, dbranch_a, dresid, mlp_gains_p, mlp_gains_a, dmixed = whole_call(
        middle_back_kernel,
        (((rp, dp), BF), ((ra, da), BF), ((rows, cp), F32), row, row_a, ((rows, width), BF)),
        [after(rank_t, grad_down_home), *dn_pieces, mid_p, mid_a, mlp_gain_p, mlp_gain_a, cot_prefix, cot_action, got_out],
        2 * rows * dp * width,
        scratch=(
            pltpu.VMEM((rp, dp), BF),
            pltpu.VMEM((ra, da), BF),
            pltpu.VMEM((rp, dp), F32),
            pltpu.VMEM((ra, da), F32),
        ),
    )
    dquery, *dkv_parts = whole_call(
        attend_back_kernel,
        (((rows, width), BF),) + (((n * rows // 4, 2 * HD), BF),) * 4,
        [queries, keys_values, query_code, key_code, attended, log_sum, dmixed],
        10 * rows * width * n * rows,
        limit=56,
        transcendentals=rows * width // HD * n * rows,
    )
    dkv_halves = [
        [d.reshape(n // 2, half, 2 * HD) for d in (e, swap(o, "seq", 1))]
        for e, o in ((dkv_parts[0], dkv_parts[1]), (dkv_parts[2], dkv_parts[3]))
    ]
    dkv = [part for pair in scatter_rows(dkv_halves) for part in pair]
    (out_grads,) = whole_call(
        out_grad_kernel,
        (((n, kp + ka, width), BF),),
        [dbranch_p, dbranch_a, after(mixed, dquery)],
        2 * rows * dp * width,
    )
    out_home = lax.psum_scatter(out_grads, "seq", scatter_dimension=0).astype(F32)
    tall = (kp + ka) // 2 + 8
    *groups_and_pieces, = whole_call(
        lambda *refs: front_back_kernel(width, *refs),
        (((n // 2, tall, qkv_width), BF),) * 4 + (((rows + 8, cp), BF),) * tp,
        [
            after(rank_s, grad_gu_home), rank_t, dquery, *dkv, x_full_p, x_full_a, inverse1, attn_gain_p, attn_gain_a,
            got_qkv, mlp_gains_p, mlp_gains_a,
        ],
        4 * rows * dp * qkv_width,
        scratch=(
            pltpu.VMEM((dp, qkv_width), BF),
            pltpu.VMEM((da, qkv_width), BF),
            pltpu.VMEM((n, 8, qkv_width), F32),
            pltpu.VMEM((rp, dp), F32),
            pltpu.VMEM((ra, da), F32),
        ),
    )
    groups, pieces = groups_and_pieces[:4], groups_and_pieces[4:]
    grad_x_p, grad_x_a = whole_call(
        grad_x_kernel,
        (((rp, cp), BF), ((ra, ca), BF)),
        [
            rank_t, pieces[0], *[swap(pieces[k], "tp", k) for k in range(1, tp)], x_pack,
            inverse1, attn_gain_p, attn_gain_a, dresid,
        ],
        rp * dp,
    )
    def own_piece(rank):
        return jnp.concatenate(
            [
                lax.dynamic_slice(lifted_home, (0, rank * cp), (rp, cp)),
                jnp.pad(
                    lax.dynamic_slice(lifted_home, (rp, rank * ca), (ra, ca)),
                    ((0, 0), (0, cp - ca)),
                ),
            ],
            axis=0,
        )

    output = (residual + sum_tp([own_piece(t ^ k) for k in range(tp)])).astype(BF)
    qkv_a, qkv_b = [
        add(keep, got)
        for keep, got in scatter_rows(
            [(e, swap(o, "seq", 1)) for e, o in ((groups[0], groups[2]), (groups[1], groups[3]))],
            output,
        )
    ]
    hp, ha = kp // 2, ka // 2
    qkv_home_p = jnp.concatenate([qkv_a[:hp], qkv_b[:hp]], axis=0)
    qkv_home_a = jnp.concatenate([qkv_a[hp : hp + ha], qkv_b[hp : hp + ha]], axis=0)
    gains_home = qkv_a[hp + ha :]
    qp, qa = kp // tp, ka // tp

    attn_gains = jnp.pad(gains_home[:1, :512], ((0, 7), (0, 0)))

    def shared_piece(rank):
        return jnp.concatenate(
            [
                lax.dynamic_slice_in_dim(qkv_home_p[:, width:], rank * qp, qp, 0),
                lax.dynamic_slice_in_dim(qkv_home_a[:, width:], rank * qa, qa, 0),
                attn_gains,
            ],
            axis=0,
        )

    shared_home = sum_tp([shared_piece(t ^ k) for k in range(tp)])
    attn_gains_home = shared_home[qp + qa]
    grad_gate_p, grad_up_p = home(grad_gu_home)
    grad_down_p = grad_down_home[:, :fp].astype(F32).reshape(n * fp, kp)
    action_home = grad_down_home[:, fp:].reshape(n, ka, 3 * fa).astype(F32)

    def units(part):
        return part.transpose(1, 0, 2).reshape(ka, n * fa)

    grad_gate_a = units(action_home[:, :, :fa])
    grad_up_a = units(action_home[:, :, fa : 2 * fa])
    grad_down_a = action_home[:, :, 2 * fa :].transpose(0, 2, 1).reshape(n * fa, ka)
    return (
        output[:rp],
        output[rp:, :ca],
        grad_x_p,
        grad_x_a,
        attn_gains_home[:kp],
        qkv_home_p[:, :width],
        shared_home[:qp, :HD],
        shared_home[:qp, HD:],
        out_home[:kp].T,
        gains_home[0, 512 : 512 + kp],
        grad_gate_p,
        grad_up_p,
        grad_down_p,
        attn_gains_home[256 : 256 + ka],
        qkv_home_a[:, :width],
        shared_home[qp : qp + qa, :HD],
        shared_home[qp : qp + qa, HD:],
        out_home[kp:].T,
        gains_home[0, 768 : 768 + ka],
        grad_gate_a,
        grad_up_a,
        grad_down_a,
    )


def solution(mesh):
    split = P("seq", "tp")
    turned = P("tp", "seq")
    both = P(("seq", "tp"), None)
    one = P("seq")
    rows = P("seq", None)
    stream_in = (one, split, rows, rows, turned, one, split, split, turned)
    stream_out = (one, split, both, both, turned, one, split, split, turned)
    return jax.shard_map(
        shards,
        mesh=mesh,
        in_specs=(split, split, P()) + stream_in + stream_in + (rows, rows),
        out_specs=(split, split, split, split) + stream_out + stream_out,
        check_vma=False,
    )
```

```python
import jax
import jax.numpy as jnp
from jax import lax
from jax.experimental import pallas as pl
from jax.experimental.pallas import tpu as pltpu
from jax.sharding import PartitionSpec as P

HD = 256
IMG = 768
TXT = 48
ACT = 50
EPS = 1e-06
NEG = -1e30
BF = jnp.bfloat16
F32 = jnp.float32
MIB = 1 << 20


def swap(value, axis, mask):
    count = lax.axis_size(axis)
    return lax.ppermute(value, axis, [(i, i ^ mask) for i in range(count)])


def after(values, *tokens):
    return lax.optimization_barrier((values, tokens))[0]


def far_masks():
    count = lax.axis_size("seq")
    masks = [1 << b for b in range(1, count.bit_length() - 1)]
    return masks, masks[::-1]


def block_order(number):
    order = [0]
    for mask in far_masks()[number]:
        order = order + [k ^ mask for k in order]
    return order


def gather_far(halves):
    results = []
    for half, masks in zip(halves, far_masks()):
        blocks = [half]
        for mask in masks:
            blocks = blocks + [swap(b, "seq", mask) for b in blocks]
        results.append(blocks)
    return results


def gather_stacked(halves):
    stages = [list(halves)]
    for step in range(len(far_masks()[0])):
        got = [swap(b, "seq", masks[step]) for b, masks in zip(stages[-1], far_masks())]
        got = lax.optimization_barrier(got)
        stages.append([jnp.concatenate(pair, axis=0) for pair in zip(stages[-1], got)])
    return stages[1:]


def near_rows(blocks):
    even = jnp.concatenate(blocks, axis=0)
    return swap(even, "seq", 1), even


def add(left, right):
    return left.astype(F32) + right.astype(F32)


def scatter_rows(halves, token=None):
    results = []
    firsts = []
    for (mine, other), masks in zip(halves, far_masks()):
        for mask in masks[:0:-1]:
            keep = mine.shape[0] // 2
            sent = add(mine[keep:], other[keep:]).astype(BF)
            firsts.append(sent)
            got = swap(sent, "seq", mask)
            mine, other = add(mine[:keep], other[:keep]), got
        sent = add(mine[1], other[1]).astype(BF)
        if token is not None:
            sent = after(sent, token)
        got = swap(sent, "seq", masks[0])
        results.append((add(mine[0], other[0]), got))
    return results, firsts[:: max(1, len(firsts) // 2)]


def gather_tp(piece):
    return [piece] + [swap(piece, "tp", k) for k in range(1, lax.axis_size("tp"))]


def sum_tp(pieces):
    total = pieces[0].astype(F32)
    for k in range(1, len(pieces)):
        total = total + swap(pieces[k].astype(BF), "tp", k).astype(F32)
    return total


def dot(left, right):
    return jnp.dot(left, right, preferred_element_type=F32)


def dot_t(left, right):
    return lax.dot_general(left, right, (((1,), (1,)), ((), ())), preferred_element_type=F32)


def t_dot(left, right):
    return lax.dot_general(left, right, (((0,), (0,)), ((), ())), preferred_element_type=F32)


def whole_call(kernel, outs, args, flops, scratch=(), limit=48, transcendentals=0):
    specs = [
        pl.BlockSpec(memory_space=pltpu.SMEM if a.ndim == 1 else pltpu.VMEM) for a in args
    ]
    outs = tuple(jax.ShapeDtypeStruct(shape, dtype) for shape, dtype in outs)
    moved = sum(a.size * a.dtype.itemsize for a in args)
    moved += sum(o.size * o.dtype.itemsize for o in outs)
    return pl.pallas_call(
        kernel,
        out_shape=outs,
        in_specs=specs,
        out_specs=tuple(pl.BlockSpec(memory_space=pltpu.VMEM) for _ in outs),
        scratch_shapes=list(scratch),
        compiler_params=pltpu.CompilerParams(vmem_limit_bytes=limit * MIB),
        cost_estimate=pl.CostEstimate(
            flops=int(flops), bytes_accessed=int(moved), transcendentals=int(transcendentals)
        ),
    )(*args)


def inverse_rms(values):
    return lax.rsqrt(jnp.mean(values * values, axis=1, keepdims=True) + EPS)


def place(rank, width):
    return pl.ds(pl.multiple_of(rank * width, width), width)


def token_codes(prefix_segment, seq_count, suf_rows):
    items_all = prefix_segment.shape[0] // (IMG + TXT)
    places = jnp.arange(seq_count * suf_rows, dtype=jnp.int32)
    items_of = places // (ACT + 1)
    suffix_seg = jnp.where(items_of < items_all, items_of, items_all)
    suffix_lvl = jnp.where((items_of < items_all) & (places % (ACT + 1) == 0), 1, 2)
    suffix = (suffix_seg * 4 + suffix_lvl).astype(jnp.int32)
    return jnp.concatenate(
        [(prefix_segment * 4).reshape(seq_count, -1), suffix.reshape(seq_count, -1)], axis=1
    )


def front_kernel(t_ref, *refs):
    tp = lax.axis_size("tp")
    xs = refs[:tp]
    w_ref, gp_ref, ga_ref, q_ref, kva_ref, kvb_ref, xp_ref, xa_ref, inv_ref = refs[tp:]
    rp, dp = xp_ref.shape
    ra, da = xa_ref.shape
    cp, ca = dp // tp, da // tp
    kp, ka = dp // w_ref.shape[0], da // w_ref.shape[0]
    width = q_ref.shape[1]
    half = kva_ref.shape[0]
    for k in range(tp):
        xp_ref[:, place(t_ref[0] ^ k, cp)] = xs[k][:rp, :]
        xa_ref[:, place(t_ref[0] ^ k, ca)] = xs[k][rp:, :ca]
    parts = []
    inverses = []
    for x_ref, g_ref, first, last, size in (
        (xp_ref, gp_ref, 0, kp, dp),
        (xa_ref, ga_ref, kp, kp + ka, da),
    ):
        rows = x_ref[...].astype(F32)
        inverse = inverse_rms(rows)
        normed = (rows * inverse * g_ref[...]).astype(BF)
        parts.append(dot(normed, w_ref[:, first:last, :].reshape(size, -1)))
        inverses.append(inverse)
    qkv = jnp.concatenate(parts, axis=0)
    q_ref[...] = qkv[:, :width].astype(BF)
    kva_ref[...] = qkv[:half, width:].astype(BF)
    kvb_ref[...] = qkv[half:, width:].astype(BF)
    inv_ref[...] = jnp.broadcast_to(jnp.concatenate(inverses, axis=0), inv_ref.shape)


def key_step(count):
    for step in (2176, 1088, 544, 272):
        if count % step == 0:
            return step
    return count


def attend_kernel(q_ref, kv_ref, qc_ref, kc_ref, att_ref, mix_ref, lse_ref):
    rows = q_ref.shape[0]
    heads = q_ref.shape[1] // HD
    count = kv_ref.shape[0]
    step = key_step(count)
    code = qc_ref[...]
    low = code - code % 4
    for h in range(heads):
        query = q_ref[:, h * HD : (h + 1) * HD] * BF(HD**-0.5)
        top = jnp.full((rows, 1), NEG, F32)
        mass = jnp.zeros((rows, 1), F32)
        total = jnp.zeros((rows, HD), F32)
        for begin in range(0, count, step):
            keys = kv_ref[begin : begin + step, :HD]
            marks = kc_ref[:, begin : begin + step]
            allowed = (marks >= low) & (marks <= code)
            scores = jnp.where(allowed, dot_t(query, keys), NEG)
            new_top = jnp.maximum(top, jnp.max(scores, axis=1, keepdims=True))
            expo = jnp.where(allowed, jnp.exp(scores - new_top), 0.0)
            shrink = jnp.exp(top - new_top)
            mass = mass * shrink + jnp.sum(expo, axis=1, keepdims=True)
            total = total * shrink + dot(expo.astype(BF), kv_ref[begin : begin + step, HD:])
            top = new_top
        attended = total / mass
        att_ref[:, h * HD : (h + 1) * HD] = attended
        mix_ref[:, h * HD : (h + 1) * HD] = attended.astype(BF)
        lse_ref[:, h * 128 : (h + 1) * 128] = jnp.broadcast_to(top + jnp.log(mass), (rows, 128))


def attend_back_kernel(
    q_ref, kv_ref, qc_ref, kc_ref, att_ref, lse_ref, dm_ref, dq_ref, *dkv_refs
):
    rows = q_ref.shape[0]
    heads = q_ref.shape[1] // HD
    count = kv_ref.shape[0]
    step = key_step(count)
    each = dkv_refs[0].shape[0]
    code = qc_ref[...]
    low = code - code % 4
    dq = [jnp.zeros((rows, HD), F32) for _ in range(heads)]
    for begin in range(0, count, step):
        keys = kv_ref[begin : begin + step, :HD]
        vals = kv_ref[begin : begin + step, HD:]
        marks = kc_ref[:, begin : begin + step]
        allowed = (marks >= low) & (marks <= code)
        dk = jnp.zeros((step, HD), F32)
        dv = jnp.zeros((step, HD), F32)
        for h in range(heads):
            span = slice(h * HD, (h + 1) * HD)
            query = q_ref[:, span] * BF(HD**-0.5)
            dmix = dm_ref[:, span]
            delta = jnp.sum(dmix.astype(F32) * att_ref[:, span], axis=1, keepdims=True)
            scores = dot_t(query, keys)
            probs = jnp.where(allowed, jnp.exp(scores - lse_ref[:, h * 128 : h * 128 + 1]), 0.0)
            dscores = (probs * (dot_t(dmix, vals) - delta)).astype(BF)
            dq[h] = dq[h] + dot(dscores, keys)
            dk = dk + t_dot(dscores, query)
            dv = dv + t_dot(probs.astype(BF), dmix)
        dkv = jnp.concatenate([dk, dv], axis=1).astype(BF)
        for part in range(len(dkv_refs)):
            first, last = max(begin, part * each), min(begin + step, (part + 1) * each)
            if first < last:
                dkv_refs[part][first - part * each : last - part * each, :] = dkv[
                    first - begin : last - begin
                ]
    for h in range(heads):
        dq_ref[:, h * HD : (h + 1) * HD] = (dq[h] * HD**-0.5).astype(BF)


def branch_kernel(t_ref, mix_ref, w_ref, *outs):
    tp = len(outs)
    n = w_ref.shape[0]
    cp = outs[0].shape[1]
    ra = mix_ref.shape[0] - (outs[0].shape[0] - 16)
    rp = mix_ref.shape[0] - ra
    kp = cp * tp // n
    for k in range(tp):
        rank = t_ref[0] ^ k
        blocks = w_ref[pl.ds(rank * (n // tp), n // tp)]
        prefix = dot_t(mix_ref[:rp, :], blocks[:, :kp].reshape(cp, -1))
        action = dot_t(mix_ref[rp:, :], blocks[:, kp:].reshape(-1, mix_ref.shape[1]))
        outs[k][:rp, :] = prefix.astype(BF)
        outs[k][rp:, :] = jnp.concatenate(
            [action, jnp.zeros((ra, cp - action.shape[1]), F32)], axis=1
        ).astype(BF)


def middle_kernel(t_ref, *refs):
    tp = lax.axis_size("tp")
    mids = refs[:tp]
    gp_ref, ga_ref, mp_ref, ma_ref, a_ref, b_ref = refs[tp:]
    rp, dp = mp_ref.shape
    ra, da = ma_ref.shape
    cp, ca = dp // tp, da // tp
    for k in range(tp):
        mp_ref[:, place(t_ref[0] ^ k, cp)] = mids[k][:rp, :]
        ma_ref[:, place(t_ref[0] ^ k, ca)] = mids[k][rp:, :ca]
    rows = mp_ref[...].astype(F32)
    prefix = rows * inverse_rms(rows) * gp_ref[...]
    rows = ma_ref[...].astype(F32)
    action = rows * inverse_rms(rows) * ga_ref[...]
    action = jnp.concatenate([action, jnp.zeros((ra, dp - da), F32)], axis=1)
    for number, out in enumerate((a_ref, b_ref)):
        out[...] = jnp.concatenate(
            [
                prefix[number * (rp // 2) : (number + 1) * (rp // 2)],
                action[number * (ra // 2) : (number + 1) * (ra // 2)],
            ],
            axis=0,
        ).astype(BF)


def gelu_parts(value):
    scale = 0.7978845608028654
    square = value * value
    bent = jnp.tanh(scale * (value + 0.044715 * value * square))
    gelu = 0.5 * value * (1.0 + bent)
    slope = 0.5 * (1.0 + bent) + 0.5 * value * (1.0 - bent * bent) * scale * (
        1.0 + 3.0 * 0.044715 * square
    )
    return gelu, slope


def forward_back(rows, cot_rows, gate_up, down):
    f = down.shape[0]
    both = dot(rows, gate_up)
    gelu, slope = gelu_parts(both[:, :f])
    up = both[:, f:]
    dhidden = dot_t(cot_rows, down)
    return gelu * up, jnp.concatenate([dhidden * up * slope, dhidden * gelu], axis=1)


def feed_kernel(pair, x_ref, c_ref, w_ref, d_ref, act_ref, h_ref, g_ref, dn_ref):
    rows, dp = x_ref.shape
    each = rows // pair
    prefix = each - act_ref.shape[0] // pair
    hidden, dgate_up = forward_back(x_ref[...], c_ref[...], w_ref[...], d_ref[...])
    inside = lax.broadcasted_iota(jnp.int32, (rows, 1), 0) % each < prefix
    dgate_up = jnp.where(inside, dgate_up, 0.0).astype(BF)
    h_ref[...] = jnp.where(inside, hidden, 0.0).astype(BF)
    g_ref[...] = dgate_up
    dn = dot_t(dgate_up, w_ref[...])
    action = act_ref[...]
    action = jnp.concatenate(
        [action, jnp.zeros((action.shape[0], dp - action.shape[1]), F32)], axis=1
    )
    pieces = []
    for i in range(pair):
        pieces.append(dn[i * each : i * each + prefix])
        pieces.append(action[i * (each - prefix) : (i + 1) * (each - prefix)])
    dn_ref[...] = jnp.concatenate(pieces, axis=0).astype(BF)


def feed(rows_in, cot_rows, gate_up, down, dn_action, each):
    total, dp = rows_in.shape
    pair = 2
    step = pair * each
    f = down.shape[0]
    act_step = dn_action.shape[0] * step // total
    row_spec = pl.BlockSpec((step, dp), lambda i: (i, 0))
    in_specs = [
        row_spec,
        row_spec,
        pl.BlockSpec(gate_up.shape, lambda i: (0, 0)),
        pl.BlockSpec(down.shape, lambda i: (0, 0)),
        pl.BlockSpec((act_step, dn_action.shape[1]), lambda i: (i, 0)),
    ]
    return pl.pallas_call(
        lambda *refs: feed_kernel(pair, *refs),
        grid=(total // step,),
        in_specs=in_specs,
        out_specs=(
            pl.BlockSpec((step, f), lambda i: (i, 0)),
            pl.BlockSpec((step, 2 * f), lambda i: (i, 0)),
            row_spec,
        ),
        out_shape=(
            jax.ShapeDtypeStruct((total, f), BF),
            jax.ShapeDtypeStruct((total, 2 * f), BF),
            jax.ShapeDtypeStruct((total, dp), BF),
        ),
        compiler_params=pltpu.CompilerParams(vmem_limit_bytes=58 * MIB),
        cost_estimate=pl.CostEstimate(
            flops=10 * total * dp * f,
            bytes_accessed=8 * total * dp + 6 * f * dp,
            transcendentals=total * f,
        ),
    )(rows_in, cot_rows, gate_up, down, dn_action)


def feed_action_kernel(x_ref, c_ref, w_ref, d_ref, dn_ref, lift_ref, gw_ref, gd_ref):
    rows, cot_rows = x_ref[...], c_ref[...]
    hidden, dgate_up = forward_back(rows, cot_rows, w_ref[...], d_ref[...])
    hidden, dgate_up = hidden.astype(BF), dgate_up.astype(BF)
    dn_ref[...] = dot_t(dgate_up, w_ref[...])
    lift_ref[...] = dot(hidden, d_ref[...])
    gw_ref[...] = t_dot(rows, dgate_up).astype(BF)
    gd_ref[...] = t_dot(hidden, cot_rows).astype(BF)


def weights_kernel(
    xo_ref, xe_ref, co_ref, ce_ref, ho_ref, he_ref, go_ref, ge_ref, act_ref, gw_ref, gd_ref
):
    f = ho_ref.shape[1]
    kp = gd_ref.shape[2]
    gw_ref[...] = (t_dot(xo_ref[...], go_ref[...]) + t_dot(xe_ref[...], ge_ref[...])).astype(BF)
    down = (t_dot(ho_ref[...], co_ref[...]) + t_dot(he_ref[...], ce_ref[...])).astype(BF)
    for i in range(gd_ref.shape[0]):
        gd_ref[i, :f, :] = down[:, i * kp : (i + 1) * kp]
        gd_ref[i, f:, :] = act_ref[i]


def weight_grads(x_odd, x_even, c_odd, c_even, h_odd, h_even, g_odd, g_even, action):
    total, dp = x_odd.shape
    f = h_odd.shape[1]
    n, extra, kp = action.shape
    wide = 256
    cols = pl.BlockSpec((total, wide), lambda i: (0, i))
    h_spec = pl.BlockSpec((total, f), lambda i: (0, 0))
    g_spec = pl.BlockSpec((total, 2 * f), lambda i: (0, 0))
    return pl.pallas_call(
        weights_kernel,
        grid=(dp // wide,),
        in_specs=[
            cols,
            cols,
            cols,
            cols,
            h_spec,
            h_spec,
            g_spec,
            g_spec,
            pl.BlockSpec((wide // kp, extra, kp), lambda i: (i, 0, 0)),
        ],
        out_specs=(
            pl.BlockSpec((wide, 2 * f), lambda i: (i, 0)),
            pl.BlockSpec((wide // kp, f + extra, kp), lambda i: (i, 0, 0)),
        ),
        out_shape=(
            jax.ShapeDtypeStruct((dp, 2 * f), BF),
            jax.ShapeDtypeStruct((n, f + extra, kp), BF),
        ),
        compiler_params=pltpu.CompilerParams(vmem_limit_bytes=48 * MIB),
        cost_estimate=pl.CostEstimate(
            flops=12 * total * dp * f, bytes_accessed=8 * total * dp, transcendentals=0
        ),
    )(x_odd, x_even, c_odd, c_even, h_odd, h_even, g_odd, g_even, action)


def lift_kernel(
    odd_ref, pa_ref, pb_ref, la_ref, lb_ref,
    oa_ref, ea_ref, ob_ref, eb_ref, aa_ref, ab_ref, d_ref, out_ref,
):
    odd = odd_ref[pl.program_id(0)] == 1
    dp = out_ref.shape[2]
    prefix = oa_ref.shape[0] - aa_ref.shape[0]
    outs = []
    for o_ref, e_ref in ((oa_ref, ea_ref), (ob_ref, eb_ref)):
        hidden = jnp.where(odd, o_ref[...].astype(F32), e_ref[...].astype(F32)).astype(BF)
        outs.append(dot(hidden, d_ref[...])[:prefix])
    action = jnp.concatenate([aa_ref[...], ab_ref[...]], axis=0)
    action = jnp.concatenate(
        [action, jnp.zeros((action.shape[0], dp - action.shape[1]), F32)], axis=1
    )
    out_ref[0] = jnp.concatenate(outs + [action], axis=0).astype(BF)


def lift(odd, place_a, place_b, lift_a, lift_b, h_odd, h_even, lifted_action, down, each, ra):
    n = odd.shape[0]
    f, dp = down.shape
    da = lifted_action.shape[1]
    a_spec = pl.BlockSpec((each, f), lambda j, o, a, b, la, lb: (a[j], 0))
    b_spec = pl.BlockSpec((each, f), lambda j, o, a, b, la, lb: (b[j], 0))
    rows = 2 * each
    return pl.pallas_call(
        lift_kernel,
        grid_spec=pltpu.PrefetchScalarGridSpec(
            num_scalar_prefetch=5,
            grid=(n,),
            in_specs=[
                a_spec,
                a_spec,
                b_spec,
                b_spec,
                pl.BlockSpec((ra // 2, da), lambda j, o, a, b, la, lb: (la[j], 0)),
                pl.BlockSpec((ra // 2, da), lambda j, o, a, b, la, lb: (lb[j], 0)),
                pl.BlockSpec((f, dp), lambda j, o, a, b, la, lb: (0, 0)),
            ],
            out_specs=pl.BlockSpec((1, rows, dp), lambda j, o, a, b, la, lb: (j, 0, 0)),
        ),
        out_shape=jax.ShapeDtypeStruct((n, rows, dp), BF),
        compiler_params=pltpu.CompilerParams(vmem_limit_bytes=32 * MIB),
        cost_estimate=pl.CostEstimate(
            flops=2 * n * rows * dp * f, bytes_accessed=2 * n * rows * dp, transcendentals=0
        ),
    )(odd, place_a, place_b, lift_a, lift_b, h_odd, h_even, h_odd, h_even,
      lifted_action, lifted_action, down)


def pieces_kernel(t_ref, ka_ref, ga_ref, kb_ref, gb_ref, *outs):
    tp = len(outs)
    each, dp = ka_ref.shape
    cp = dp // tp
    rp = outs[0].shape[0] * 2 * each // (2 * each)
    extra = 8
    prefix = each - extra
    ca = outs[0].shape[1] // 2
    del rp
    for k in range(tp):
        rank = t_ref[0] ^ k
        tops, ends = [], []
        for keep, got in ((ka_ref, ga_ref), (kb_ref, gb_ref)):
            wide = place(rank, cp)
            tops.append(keep[:prefix, wide].astype(F32) + got[:prefix, wide].astype(F32))
            slim = place(rank, ca)
            ends.append(
                keep[prefix:, slim].astype(F32) + got[prefix:, slim].astype(F32)
            )
        action = jnp.concatenate(ends, axis=0)
        action = jnp.concatenate(
            [action, jnp.zeros((action.shape[0], cp - ca), F32)], axis=1
        )
        outs[k][...] = jnp.concatenate(tops + [action], axis=0).astype(BF)


def middle_back_kernel(t_ref, *refs):
    tp = lax.axis_size("tp")
    ds = refs[:tp]
    mp_ref, ma_ref, gp_ref, ga_ref, cp_ref, ca_ref, w_ref = refs[tp : tp + 7]
    bp_ref, ba_ref, own_ref, lp_ref, la_ref, dm_ref, dp_scr, da_scr, rp_scr, ra_scr = refs[tp + 7 :]
    rp, dp = mp_ref.shape
    ra, da = ma_ref.shape
    cp, ca = dp // tp, da // tp
    n = w_ref.shape[0]
    kp = dp // n
    t = t_ref[0]
    for k in range(tp):
        dp_scr[:, place(t ^ k, cp)] = ds[k][:rp, :]
        da_scr[:, place(t ^ k, ca)] = ds[k][rp:, :ca]
    mixes = []
    for d_ref, m_ref, g_ref, c_ref, b_ref, r_ref, l_ref, first, last in (
        (dp_scr, mp_ref, gp_ref, cp_ref, bp_ref, rp_scr, lp_ref, 0, kp),
        (da_scr, ma_ref, ga_ref, ca_ref, ba_ref, ra_scr, la_ref, kp, w_ref.shape[1]),
    ):
        gradient = d_ref[...].astype(F32)
        rows = m_ref[...].astype(F32)
        inverse = inverse_rms(rows)
        centered = rows * inverse
        inner = gradient * g_ref[...]
        dresid = c_ref[...].astype(F32) + inverse * (
            inner - centered * jnp.mean(inner * centered, axis=1, keepdims=True)
        )
        l_ref[...] = jnp.sum(gradient * centered, axis=0, keepdims=True)
        r_ref[...] = dresid
        branch = dresid.astype(BF)
        b_ref[...] = branch
        mixes.append(dot(branch, w_ref[:, first:last, :].reshape(rows.shape[1], -1)))
    dm_ref[...] = jnp.concatenate(mixes, axis=0).astype(BF)
    own_ref[:rp, :] = rp_scr[:, place(t, cp)]
    own_ref[rp:, :] = jnp.concatenate(
        [ra_scr[:, place(t, ca)], jnp.zeros((ra, cp - ca), F32)], axis=1
    )


def out_grad_kernel(bp_ref, ba_ref, mix_ref, out_ref):
    rp, dp = bp_ref.shape
    n = out_ref.shape[0]
    kp = dp // n
    width = mix_ref.shape[1]
    out_ref[:, :kp, :] = t_dot(bp_ref[...], mix_ref[:rp, :]).astype(BF).reshape(n, kp, width)
    out_ref[:, kp:, :] = t_dot(ba_ref[...], mix_ref[rp:, :]).astype(BF).reshape(n, -1, width)


def front_back_kernel(heads_width, s_ref, t_ref, dq_ref, *refs):
    tp = lax.axis_size("tp")
    n = lax.axis_size("seq")
    (ka_ref, ra_ref, kb_ref, rb_ref, xp_ref, xa_ref, inv_ref, gp_ref, ga_ref, w_ref, lp_ref,
     la_ref) = refs[:12]
    groups = refs[12:16]
    pieces = refs[16 : 16 + tp]
    gwp_scr, gwa_scr, gain_scr, dp_scr, da_scr = refs[16 + tp :]
    rp, dp = xp_ref.shape
    ra, da = xa_ref.shape
    kp, ka = dp // n, da // n
    cp, ca = dp // tp, da // tp
    width = heads_width
    dkv = jnp.concatenate(
        [
            ka_ref[...].astype(F32) + ra_ref[...].astype(F32),
            kb_ref[...].astype(F32) + rb_ref[...].astype(F32),
        ],
        axis=0,
    )
    dqkv = jnp.concatenate([dq_ref[...].astype(F32), dkv], axis=1)
    gain_scr[...] = jnp.zeros(gain_scr.shape, F32)
    dots = []
    for x_ref, g_ref, d_scr, gw_scr, l_ref, begin, end, first, last, size, at in (
        (xp_ref, gp_ref, dp_scr, gwp_scr, lp_ref, 0, rp, 0, kp, kp, 0),
        (xa_ref, ga_ref, da_scr, gwa_scr, la_ref, rp, rp + ra, kp, kp + ka, ka, 256),
    ):
        grad_rows = dqkv[begin:end].astype(BF)
        centered = x_ref[...].astype(F32) * inv_ref[begin:end, :1]
        normed = (centered * g_ref[...]).astype(BF)
        gw_scr[...] = t_dot(normed, grad_rows).astype(BF)
        weights = w_ref[:, first:last, :].reshape(x_ref.shape[1], -1)
        partial = dot_t(grad_rows, weights)
        d_scr[...] = partial
        product = partial * centered
        gains = jnp.sum(product, axis=0, keepdims=True)
        mlp_gains = l_ref[...]
        for d in range(n):
            gain_scr[d, 0:1, at : at + size] = gains[:, d * size : (d + 1) * size]
            gain_scr[d, 0:1, at + 512 : at + 512 + size] = mlp_gains[
                :, d * size : (d + 1) * size
            ]
        dots.append(jnp.sum(product * g_ref[...], axis=1, keepdims=True))
    column = jnp.concatenate(dots, axis=0)
    lanes = lax.broadcasted_iota(jnp.int32, (rp + ra, cp), 1)
    rows = lax.broadcasted_iota(jnp.int32, (rp + ra, cp), 0)
    row = jnp.sum(jnp.where(lanes == rows, column, 0.0), axis=0, keepdims=True)
    high = row.astype(BF).astype(F32)
    tail = jnp.concatenate([high, row - high, jnp.zeros((6, cp), F32)], axis=0)
    for k in range(tp):
        rank = t_ref[0] ^ k
        action = jnp.concatenate(
            [da_scr[:, place(rank, ca)], jnp.zeros((ra, cp - ca), F32)], axis=1
        )
        pieces[k][...] = jnp.concatenate([dp_scr[:, place(rank, cp)], action, tail], axis=0).astype(
            BF
        )
    for odd in range(2):
        for number in range(2):
            out = groups[2 * odd + number]
            for i, k in enumerate(block_order(number)):
                d = s_ref[0] ^ (k ^ odd)
                hp, ha = kp // 2, ka // 2
                out[i, :hp, :] = gwp_scr[
                    pl.ds(pl.multiple_of(d * kp + number * hp, hp), hp), :
                ]
                out[i, hp : hp + ha, :] = gwa_scr[
                    pl.ds(pl.multiple_of(d * ka + number * ha, ha), ha), :
                ]
                out[i, hp + ha :, :] = gain_scr[d].astype(BF) * BF(1 - number)


def grad_x_kernel(t_ref, *refs):
    tp = lax.axis_size("tp")
    ds = refs[:tp]
    x_ref, inv_ref, gp_ref, ga_ref, r_ref, op_ref, oa_ref = refs[tp:]
    rp, cp = op_ref.shape
    ra, ca = oa_ref.shape
    t = t_ref[0]
    total = ds[0][...].astype(F32)
    for k in range(1, tp):
        total = total + ds[k][...].astype(F32)
    row = total[rp + ra : rp + ra + 1] + total[rp + ra + 1 : rp + ra + 2]
    lanes = lax.broadcasted_iota(jnp.int32, (rp + ra, cp), 1)
    rows = lax.broadcasted_iota(jnp.int32, (rp + ra, cp), 0)
    column = jnp.sum(jnp.where(lanes == rows, row, 0.0), axis=1, keepdims=True)
    for o_ref, g_ref, begin, end, wide in (
        (op_ref, gp_ref, 0, rp, cp),
        (oa_ref, ga_ref, rp, rp + ra, ca),
    ):
        inverse = inv_ref[begin:end, :1]
        centered = x_ref[begin:end, :wide].astype(F32) * inverse
        mean = column[begin:end] / (wide * tp)
        moved = inverse * (
            total[begin:end, :wide] * g_ref[:, place(t, wide)] - centered * mean
        )
        o_ref[...] = (r_ref[begin:end, :wide] + moved).astype(BF)


def home_kernel(token_ref, gu_ref, down_in_ref, gate_ref, up_ref, down_ref, act_ref):
    del token_ref
    f = gate_ref.shape[1]
    gate_ref[...] = gu_ref[0, :, :f].astype(F32)
    up_ref[...] = gu_ref[0, :, f:].astype(F32)
    down_ref[...] = down_in_ref[0, :f, :].astype(F32)
    act_ref[0] = down_in_ref[0, f:, :].astype(F32)


def home(token, got_gu, got_down):
    n, kp, both = got_gu.shape
    f = both // 2
    tall = got_down.shape[1]
    out = pl.BlockSpec((kp, f), lambda j: (0, j))
    return pl.pallas_call(
        home_kernel,
        grid=(n,),
        in_specs=[
            pl.BlockSpec(memory_space=pltpu.SMEM),
            pl.BlockSpec((1, kp, both), lambda j: (j, 0, 0)),
            pl.BlockSpec((1, tall, kp), lambda j: (j, 0, 0)),
        ],
        out_specs=(
            out,
            out,
            pl.BlockSpec((f, kp), lambda j: (j, 0)),
            pl.BlockSpec((1, tall - f, kp), lambda j: (j, 0, 0)),
        ),
        out_shape=(
            jax.ShapeDtypeStruct((kp, n * f), F32),
            jax.ShapeDtypeStruct((kp, n * f), F32),
            jax.ShapeDtypeStruct((n * f, kp), F32),
            jax.ShapeDtypeStruct((n, tall - f, kp), F32),
        ),
        cost_estimate=pl.CostEstimate(
            flops=0, bytes_accessed=6 * n * kp * (both + tall), transcendentals=0
        ),
    )(token, got_gu, got_down)


def shards(
    x_prefix,
    x_action,
    prefix_segment,
    prefix_attn_gain,
    prefix_query,
    prefix_key,
    prefix_value,
    prefix_out,
    prefix_mlp_gain,
    prefix_gate,
    prefix_up,
    prefix_down,
    action_attn_gain,
    action_query,
    action_key,
    action_value,
    action_out,
    action_mlp_gain,
    action_gate,
    action_up,
    action_down,
    cot_prefix,
    cot_action,
):
    n = lax.axis_size("seq")
    tp = lax.axis_size("tp")
    s = lax.axis_index("seq")
    t = lax.axis_index("tp")
    rank_t = t.astype(jnp.int32).reshape(1)
    rank_s = s.astype(jnp.int32).reshape(1)
    rp, cp = x_prefix.shape
    ra, ca = x_action.shape
    rows = rp + ra
    half = rows // 2
    dp, da = cp * tp, ca * tp
    kp, ka = dp // n, da // n
    width = prefix_query.shape[1]
    qkv_width = width + 2 * HD
    fp, fa = prefix_gate.shape[1] // n, action_gate.shape[1] // n

    x_pack = jnp.concatenate(
        [x_prefix, jnp.pad(x_action, ((0, 0), (0, cp - ca)))], axis=0
    )
    x_pieces = gather_tp(x_pack)
    gains = jnp.concatenate(
        [prefix_attn_gain, prefix_mlp_gain, action_attn_gain, action_mlp_gain]
    )
    gain_rows = -(-gains.shape[0] // qkv_width)
    gains = jnp.pad(gains, (0, 8 * qkv_width - gains.shape[0])).reshape(8, qkv_width)
    pack_qkv = jnp.concatenate(
        [
            jnp.concatenate([prefix_query, prefix_key, prefix_value], axis=1),
            jnp.concatenate([action_query, action_key, action_value], axis=1),
            gains,
        ],
        axis=0,
    )
    got_qkv = lax.all_gather(pack_qkv, "seq", axis=0)
    got_gains = got_qkv[:, kp + ka : kp + ka + gain_rows].reshape(n, -1).astype(F32)
    attn_gain_p = got_gains[:, :kp].reshape(1, dp)
    mlp_gain_p = got_gains[:, kp : 2 * kp].reshape(1, dp)
    attn_gain_a = got_gains[:, 2 * kp : 2 * kp + ka].reshape(1, da)
    mlp_gain_a = got_gains[:, 2 * kp + ka : 2 * kp + 2 * ka].reshape(1, da)
    pack_out = jnp.concatenate([prefix_out.T, action_out.T], axis=0)
    cot_wide = jnp.pad(cot_action, ((0, 0), (0, dp - da)))
    cot_stages = gather_stacked(
        [
            jnp.concatenate(
                [
                    cot_prefix[i * (rp // 2) : (i + 1) * (rp // 2)],
                    cot_wide[i * (ra // 2) : (i + 1) * (ra // 2)],
                ],
                axis=0,
            )
            for i in range(2)
        ]
    )
    cot_odd, cot_even = near_rows(cot_stages[-1])

    def by_units(w, f):
        return w.reshape(w.shape[0], n, f).transpose(1, 0, 2)

    gate_up_sent = jnp.concatenate([by_units(prefix_gate, fp), by_units(prefix_up, fp)], axis=2)
    action_sent = jnp.concatenate(
        [
            by_units(action_gate, fa),
            by_units(action_up, fa),
            action_down.reshape(n, fa, ka).transpose(0, 2, 1),
        ],
        axis=2,
    ).reshape(n, -1, kp)
    extra = action_sent.shape[1]
    down_sent = jnp.concatenate([prefix_down.reshape(n, fp, kp), action_sent], axis=1)

    queries, kv_a, kv_b, x_full_p, x_full_a, inverse1 = whole_call(
        front_kernel,
        (
            ((rows, width), BF),
            ((half, 2 * HD), BF),
            ((half, 2 * HD), BF),
            ((rp, dp), BF),
            ((ra, da), BF),
            ((rows, 128), F32),
        ),
        [after(rank_t, cot_even), *x_pieces, got_qkv, attn_gain_p, attn_gain_a],
        2 * rp * dp * qkv_width,
    )
    kv_even = [jnp.concatenate(blocks, axis=0) for blocks in gather_far([kv_a, kv_b])]
    kv_odd = [swap(e, "seq", 1) for e in kv_even]
    keys_values = jnp.concatenate([kv_even[0], kv_odd[0], kv_even[1], kv_odd[1]], axis=0)
    codes = token_codes(prefix_segment, n, ra)
    query_code = lax.dynamic_slice_in_dim(codes, s, 1, 0).reshape(rows, 1)
    key_code = jnp.concatenate(
        [
            lax.dynamic_slice(codes, (s ^ k ^ odd, number * half), (1, half))
            for number in range(2)
            for odd in range(2)
            for k in block_order(number)
        ],
        axis=1,
    )
    attended, mixed, log_sum = whole_call(
        attend_kernel,
        (
            ((rows, width), F32),
            ((rows, width), BF),
            ((rows, width // HD * 128), F32),
        ),
        [queries, keys_values, query_code, key_code],
        4 * rows * width * n * rows,
        transcendentals=rows * width // HD * n * rows,
    )
    got_out = lax.all_gather(after(pack_out, queries), "seq", axis=0)
    down_got = lax.all_to_all(after(down_sent, keys_values), "seq", 0, 0)

    piece = (((rows, cp), BF),)
    branch = sum_tp(
        whole_call(
            branch_kernel, piece * tp, [rank_t, mixed, got_out], 2 * rows * dp * width
        )
    )
    residual = x_pack.astype(F32) + branch
    mid_own = after(residual.astype(BF), down_got)
    gate_up = lax.all_to_all(after(gate_up_sent, branch), "seq", 0, 0).reshape(dp, 2 * fp)
    down = down_got[:, :fp].transpose(1, 0, 2).reshape(fp, dp)
    action_got = down_got[:, fp:].reshape(da, 3 * fa)
    gate_up_action = action_got[:, : 2 * fa]
    down_action = action_got[:, 2 * fa :].T


    def action_rows(blocks):
        return blocks.reshape(n, half, dp)[:, rp // 2 :, :da].reshape(-1, da)

    cot_action_all = jnp.concatenate([action_rows(cot_odd), action_rows(cot_even)], axis=0)
    block = (((half, dp), BF),)
    mid_p, mid_a, normed_a, normed_b = whole_call(
        middle_kernel,
        (((rp, dp), BF), ((ra, da), BF)) + block * 2,
        [after(rank_t, gate_up, down, gate_up_action, down_action, cot_action_all), *gather_tp(mid_own), mlp_gain_p, mlp_gain_a],
        rp * dp,
    )

    normed_odd, normed_even = near_rows(
        [b for blocks in gather_far([normed_a, normed_b]) for b in blocks]
    )
    normed_action = jnp.concatenate([action_rows(normed_odd), action_rows(normed_even)], axis=0)
    tokens = n * ra
    dn_action, lifted_action, grad_gu_action, grad_down_action = whole_call(
        feed_action_kernel,
        (
            ((tokens, da), F32),
            ((tokens, da), F32),
            ((da, 2 * fa), BF),
            ((fa, da), BF),
        ),
        [normed_action, cot_action_all, gate_up_action, down_action],
        18 * tokens * da * fa,
    )
    h_odd, g_odd, dn_odd = feed(
        normed_odd, cot_odd, gate_up, down, dn_action[: tokens // 2], half
    )
    h_even, g_even, dn_even = feed(
        normed_even, cot_even, gate_up, down, dn_action[tokens // 2 :], half
    )
    dn_blocks = [
        d.reshape(2, n // 2, half, dp) for d in (dn_even, swap(dn_odd, "seq", 1))
    ]

    grad_gu_action, grad_down_action = after((grad_gu_action, grad_down_action), dn_even)
    action_grads = jnp.concatenate(
        [
            grad_gu_action.reshape(n, ka, 2 * fa),
            grad_down_action.reshape(fa, n, ka).transpose(1, 2, 0),
        ],
        axis=2,
    ).reshape(n, extra, kp)
    grad_gu, grad_down = weight_grads(
        normed_odd, normed_even, cot_odd, cot_even, h_odd, h_even, g_odd, g_even, action_grads
    )
    ranks = s ^ jnp.arange(n, dtype=jnp.int32)
    odd_bits = ranks & 1
    places = []
    for number in range(2):
        table = [0] * n
        for i, k in enumerate(block_order(number)):
            table[k] = table[k ^ 1] = number * (n // 2) + i
        places.append(jnp.array(table, jnp.int32)[ranks])
    lift_places = [p + (1 - odd_bits) * n for p in places]
    lifted = lift(
        odd_bits, *places, *lift_places, h_odd, h_even, lifted_action, down, half, ra
    )
    ((keep_a, got_a), (keep_b, got_b)), _ = scatter_rows(
        [(dn_blocks[0][i], dn_blocks[1][i]) for i in range(2)], grad_gu
    )
    sent_pieces = whole_call(
        pieces_kernel,
        piece * tp,
        [after(rank_t, lifted), keep_a, got_a, keep_b, got_b],
        rp * dp,
    )
    dn_own = sum_tp(sent_pieces)
    dn_pieces = gather_tp(dn_own.astype(BF))
    lifted_home = lax.psum_scatter(after(lifted, got_a, got_b), "seq", scatter_dimension=0)
    grad_down_home = lax.all_to_all(after(grad_down, sent_pieces[0]), "seq", 0, 0)

    row = ((1, dp), F32)
    row_a = ((1, da), F32)
    dbranch_p, dbranch_a, dresid, mlp_gains_p, mlp_gains_a, dmixed = whole_call(
        middle_back_kernel,
        (((rp, dp), BF), ((ra, da), BF), ((rows, cp), F32), row, row_a, ((rows, width), BF)),
        [after(rank_t, grad_down_home), *dn_pieces, mid_p, mid_a, mlp_gain_p, mlp_gain_a, cot_prefix, cot_action, got_out],
        2 * rows * dp * width,
        scratch=(
            pltpu.VMEM((rp, dp), BF),
            pltpu.VMEM((ra, da), BF),
            pltpu.VMEM((rp, dp), F32),
            pltpu.VMEM((ra, da), F32),
        ),
    )
    grad_gu_home = lax.all_to_all(
        after(grad_gu, grad_down_home, dbranch_a).reshape(n, kp, 2 * fp), "seq", 0, 0
    )
    dquery, *dkv_parts = whole_call(
        attend_back_kernel,
        (((rows, width), BF),) + (((n * rows // 4, 2 * HD), BF),) * 4,
        [queries, keys_values, query_code, key_code, attended, log_sum, dmixed],
        10 * rows * width * n * rows,
        limit=56,
        transcendentals=rows * width // HD * n * rows,
    )
    dkv_halves = [
        [d.reshape(n // 2, half, 2 * HD) for d in (e, swap(o, "seq", 1))]
        for e, o in ((dkv_parts[0], dkv_parts[1]), (dkv_parts[2], dkv_parts[3]))
    ]
    dkv = [part for pair in scatter_rows(dkv_halves)[0] for part in pair]
    (out_grads,) = whole_call(
        out_grad_kernel,
        (((n, kp + ka, width), BF),),
        [dbranch_p, dbranch_a, after(mixed, dquery)],
        2 * rows * dp * width,
    )
    out_home = lax.psum_scatter(out_grads, "seq", scatter_dimension=0).astype(F32)
    def own_piece(rank):
        return jnp.concatenate(
            [
                lax.dynamic_slice(lifted_home, (0, rank * cp), (rp, cp)),
                jnp.pad(
                    lax.dynamic_slice(lifted_home, (rp, rank * ca), (ra, ca)),
                    ((0, 0), (0, cp - ca)),
                ),
            ],
            axis=0,
        )

    output = (residual + sum_tp([own_piece(t ^ k) for k in range(tp)])).astype(BF)
    tall = (kp + ka) // 2 + 8
    *groups_and_pieces, = whole_call(
        lambda *refs: front_back_kernel(width, *refs),
        (((n // 2, tall, qkv_width), BF),) * 4 + (((rows + 8, cp), BF),) * tp,
        [
            after(rank_s, output), rank_t, dquery, *dkv, x_full_p, x_full_a, inverse1, attn_gain_p, attn_gain_a,
            got_qkv, mlp_gains_p, mlp_gains_a,
        ],
        4 * rows * dp * qkv_width,
        scratch=(
            pltpu.VMEM((dp, qkv_width), BF),
            pltpu.VMEM((da, qkv_width), BF),
            pltpu.VMEM((n, 8, qkv_width), F32),
            pltpu.VMEM((rp, dp), F32),
            pltpu.VMEM((ra, da), F32),
        ),
    )
    groups, pieces = groups_and_pieces[:4], groups_and_pieces[4:]
    tree, first_sent = scatter_rows(
        [(e, swap(o, "seq", 1)) for e, o in ((groups[0], groups[2]), (groups[1], groups[3]))]
    )
    qkv_a, qkv_b = [add(keep, got) for keep, got in tree]
    grad_x_p, grad_x_a = whole_call(
        grad_x_kernel,
        (((rp, cp), BF), ((ra, ca), BF)),
        [
            after(rank_t, first_sent), pieces[0], *[swap(pieces[k], "tp", k) for k in range(1, tp)], x_pack,
            inverse1, attn_gain_p, attn_gain_a, dresid,
        ],
        rp * dp,
    )
    hp, ha = kp // 2, ka // 2
    qkv_home_p = jnp.concatenate([qkv_a[:hp], qkv_b[:hp]], axis=0)
    qkv_home_a = jnp.concatenate([qkv_a[hp : hp + ha], qkv_b[hp : hp + ha]], axis=0)
    gains_home = qkv_a[hp + ha :]
    qp, qa = kp // tp, ka // tp

    attn_gains = jnp.pad(gains_home[:1, :512], ((0, 7), (0, 0)))

    def shared_piece(rank):
        return jnp.concatenate(
            [
                lax.dynamic_slice_in_dim(qkv_home_p[:, width:], rank * qp, qp, 0),
                lax.dynamic_slice_in_dim(qkv_home_a[:, width:], rank * qa, qa, 0),
                attn_gains,
            ],
            axis=0,
        )

    shared_home = sum_tp([shared_piece(t ^ k) for k in range(tp)])
    attn_gains_home = shared_home[qp + qa]
    grad_gate_p, grad_up_p, grad_down_p, action_home = home(
        after(rank_t, first_sent), grad_gu_home, grad_down_home
    )
    action_home = action_home.reshape(n, ka, 3 * fa)

    def units(part):
        return part.transpose(1, 0, 2).reshape(ka, n * fa)

    grad_gate_a = units(action_home[:, :, :fa])
    grad_up_a = units(action_home[:, :, fa : 2 * fa])
    grad_down_a = action_home[:, :, 2 * fa :].transpose(0, 2, 1).reshape(n * fa, ka)
    return (
        output[:rp],
        output[rp:, :ca],
        grad_x_p,
        grad_x_a,
        attn_gains_home[:kp],
        qkv_home_p[:, :width],
        shared_home[:qp, :HD],
        shared_home[:qp, HD:],
        out_home[:kp].T,
        gains_home[0, 512 : 512 + kp],
        grad_gate_p,
        grad_up_p,
        grad_down_p,
        attn_gains_home[256 : 256 + ka],
        qkv_home_a[:, :width],
        shared_home[qp : qp + qa, :HD],
        shared_home[qp : qp + qa, HD:],
        out_home[kp:].T,
        gains_home[0, 768 : 768 + ka],
        grad_gate_a,
        grad_up_a,
        grad_down_a,
    )


def solution(mesh):
    split = P("seq", "tp")
    turned = P("tp", "seq")
    both = P(("seq", "tp"), None)
    one = P("seq")
    rows = P("seq", None)
    stream_in = (one, split, rows, rows, turned, one, split, split, turned)
    stream_out = (one, split, both, both, turned, one, split, split, turned)
    return jax.shard_map(
        shards,
        mesh=mesh,
        in_specs=(split, split, P()) + stream_in + stream_in + (rows, rows),
        out_specs=(split, split, split, split) + stream_out + stream_out,
        check_vma=False,
    )
```

```python
import jax
import jax.numpy as jnp
from jax import lax
from jax.experimental import pallas as pl
from jax.experimental.pallas import tpu as pltpu
from jax.sharding import PartitionSpec as P

HD = 256
IMG = 768
TXT = 48
ACT = 50
EPS = 1e-06
NEG = -1e30
BF = jnp.bfloat16
F32 = jnp.float32
MIB = 1 << 20


def swap(value, axis, mask):
    count = lax.axis_size(axis)
    return lax.ppermute(value, axis, [(i, i ^ mask) for i in range(count)])


def after(values, *tokens):
    return lax.optimization_barrier((values, tokens))[0]


def far_masks():
    count = lax.axis_size("seq")
    masks = [1 << b for b in range(1, count.bit_length() - 1)]
    return masks, masks[::-1]


def block_order(number):
    order = [0]
    for mask in far_masks()[number]:
        order = order + [k ^ mask for k in order]
    return order


def gather_far(halves):
    results = []
    for half, masks in zip(halves, far_masks()):
        blocks = [half]
        for mask in masks:
            blocks = blocks + [swap(b, "seq", mask) for b in blocks]
        results.append(blocks)
    return results


def gather_stacked(halves):
    stages = [list(halves)]
    for step in range(len(far_masks()[0])):
        got = [swap(b, "seq", masks[step]) for b, masks in zip(stages[-1], far_masks())]
        got = lax.optimization_barrier(got)
        stages.append([jnp.concatenate(pair, axis=0) for pair in zip(stages[-1], got)])
    return stages[1:], got


def near_rows(blocks):
    even = jnp.concatenate(blocks, axis=0)
    return swap(even, "seq", 1), even


def add(left, right):
    return left.astype(F32) + right.astype(F32)


def scatter_rows(halves, token=None, beside=((), ())):
    parts = [list(half) for half in halves]
    orders = [masks[::-1] for masks in far_masks()]
    steps = len(orders[0])
    history = []
    beside = list(beside)
    for step in range(steps):
        keep = parts[0][0].shape[0] // 2
        sent = [total_of([p[keep:] for p in part]).astype(BF) for part in parts]
        if token is not None and step == steps - 1:
            sent = after(sent, token)
        got = [swap(part, "seq", order[step]) for part, order in zip(sent, orders)]
        for place, when in enumerate((0, steps - 1)):
            if step == when and beside[place]:
                got, beside[place] = lax.optimization_barrier((got, beside[place]))
        parts = [[p[:keep] for p in part] + [g] for part, g in zip(parts, got)]
        history.append(sent)
    return [(total_of([p[0] for p in part[:-1]]), part[-1][0]) for part in parts], history, beside


def gather_tp(piece):
    return [piece] + [swap(piece, "tp", k) for k in range(1, lax.axis_size("tp"))]


def trade_tp(pieces):
    return [pieces[0]] + [swap(pieces[k].astype(BF), "tp", k) for k in range(1, len(pieces))]


def total_of(addends):
    total = addends[0].astype(F32)
    for part in addends[1:]:
        total = total + part.astype(F32)
    return total


def sum_tp(pieces):
    return total_of(trade_tp(pieces))


def dot(left, right):
    return jnp.dot(left, right, preferred_element_type=F32)


def dot_t(left, right):
    return lax.dot_general(left, right, (((1,), (1,)), ((), ())), preferred_element_type=F32)


def t_dot(left, right):
    return lax.dot_general(left, right, (((0,), (0,)), ((), ())), preferred_element_type=F32)


def whole_call(kernel, outs, args, flops, scratch=(), limit=48, transcendentals=0):
    specs = [
        pl.BlockSpec(memory_space=pltpu.SMEM if a.ndim == 1 else pltpu.VMEM) for a in args
    ]
    outs = tuple(jax.ShapeDtypeStruct(shape, dtype) for shape, dtype in outs)
    moved = sum(a.size * a.dtype.itemsize for a in args)
    moved += sum(o.size * o.dtype.itemsize for o in outs)
    return pl.pallas_call(
        kernel,
        out_shape=outs,
        in_specs=specs,
        out_specs=tuple(pl.BlockSpec(memory_space=pltpu.VMEM) for _ in outs),
        scratch_shapes=list(scratch),
        compiler_params=pltpu.CompilerParams(vmem_limit_bytes=limit * MIB),
        cost_estimate=pl.CostEstimate(
            flops=int(flops), bytes_accessed=int(moved), transcendentals=int(transcendentals)
        ),
    )(*args)


def inverse_rms(values):
    return lax.rsqrt(jnp.mean(values * values, axis=1, keepdims=True) + EPS)


def place(rank, width):
    return pl.ds(pl.multiple_of(rank * width, width), width)


def token_codes(prefix_segment, seq_count, suf_rows):
    items_all = prefix_segment.shape[0] // (IMG + TXT)
    places = jnp.arange(seq_count * suf_rows, dtype=jnp.int32)
    items_of = places // (ACT + 1)
    suffix_seg = jnp.where(items_of < items_all, items_of, items_all)
    suffix_lvl = jnp.where((items_of < items_all) & (places % (ACT + 1) == 0), 1, 2)
    suffix = (suffix_seg * 4 + suffix_lvl).astype(jnp.int32)
    return jnp.concatenate(
        [(prefix_segment * 4).reshape(seq_count, -1), suffix.reshape(seq_count, -1)], axis=1
    )


def front_kernel(t_ref, *refs):
    tp = lax.axis_size("tp")
    xs = refs[:tp]
    w_ref, gp_ref, ga_ref, q_ref, kva_ref, kvb_ref, xp_ref, xa_ref, inv_ref = refs[tp:]
    rp, dp = xp_ref.shape
    ra, da = xa_ref.shape
    cp, ca = dp // tp, da // tp
    kp, ka = dp // w_ref.shape[0], da // w_ref.shape[0]
    width = q_ref.shape[1]
    half = kva_ref.shape[0]
    for k in range(tp):
        xp_ref[:, place(t_ref[0] ^ k, cp)] = xs[k][:rp, :]
        xa_ref[:, place(t_ref[0] ^ k, ca)] = xs[k][rp:, :ca]
    parts = []
    inverses = []
    for x_ref, g_ref, first, last, size in (
        (xp_ref, gp_ref, 0, kp, dp),
        (xa_ref, ga_ref, kp, kp + ka, da),
    ):
        rows = x_ref[...].astype(F32)
        inverse = inverse_rms(rows)
        normed = (rows * inverse * g_ref[...]).astype(BF)
        parts.append(dot(normed, w_ref[:, first:last, :].reshape(size, -1)))
        inverses.append(inverse)
    qkv = jnp.concatenate(parts, axis=0)
    q_ref[...] = qkv[:, :width].astype(BF)
    kva_ref[...] = qkv[:half, width:].astype(BF)
    kvb_ref[...] = qkv[half:, width:].astype(BF)
    inv_ref[...] = jnp.broadcast_to(jnp.concatenate(inverses, axis=0), inv_ref.shape)


def key_step(count):
    for step in (2176, 1088, 544, 272):
        if count % step == 0:
            return step
    return count


def attend_kernel(q_ref, kv_ref, qc_ref, kc_ref, att_ref, mix_ref, lse_ref):
    rows = q_ref.shape[0]
    heads = q_ref.shape[1] // HD
    count = kv_ref.shape[0]
    step = key_step(count)
    code = qc_ref[...]
    low = code - code % 4
    for h in range(heads):
        query = q_ref[:, h * HD : (h + 1) * HD] * BF(HD**-0.5)
        top = jnp.full((rows, 1), NEG, F32)
        mass = jnp.zeros((rows, 1), F32)
        total = jnp.zeros((rows, HD), F32)
        for begin in range(0, count, step):
            keys = kv_ref[begin : begin + step, :HD]
            marks = kc_ref[:, begin : begin + step]
            allowed = (marks >= low) & (marks <= code)
            scores = jnp.where(allowed, dot_t(query, keys), NEG)
            new_top = jnp.maximum(top, jnp.max(scores, axis=1, keepdims=True))
            expo = jnp.where(allowed, jnp.exp(scores - new_top), 0.0)
            shrink = jnp.exp(top - new_top)
            mass = mass * shrink + jnp.sum(expo, axis=1, keepdims=True)
            total = total * shrink + dot(expo.astype(BF), kv_ref[begin : begin + step, HD:])
            top = new_top
        attended = total / mass
        att_ref[:, h * HD : (h + 1) * HD] = attended
        mix_ref[:, h * HD : (h + 1) * HD] = attended.astype(BF)
        lse_ref[:, h * 128 : (h + 1) * 128] = jnp.broadcast_to(top + jnp.log(mass), (rows, 128))


def attend_back_kernel(
    q_ref, kv_ref, qc_ref, kc_ref, att_ref, lse_ref, dm_ref, dq_ref, *dkv_refs
):
    rows = q_ref.shape[0]
    heads = q_ref.shape[1] // HD
    count = kv_ref.shape[0]
    step = key_step(count)
    each = dkv_refs[0].shape[0]
    code = qc_ref[...]
    low = code - code % 4
    dq = [jnp.zeros((rows, HD), F32) for _ in range(heads)]
    for begin in range(0, count, step):
        keys = kv_ref[begin : begin + step, :HD]
        vals = kv_ref[begin : begin + step, HD:]
        marks = kc_ref[:, begin : begin + step]
        allowed = (marks >= low) & (marks <= code)
        dk = jnp.zeros((step, HD), F32)
        dv = jnp.zeros((step, HD), F32)
        for h in range(heads):
            span = slice(h * HD, (h + 1) * HD)
            query = q_ref[:, span] * BF(HD**-0.5)
            dmix = dm_ref[:, span]
            delta = jnp.sum(dmix.astype(F32) * att_ref[:, span], axis=1, keepdims=True)
            scores = dot_t(query, keys)
            probs = jnp.where(allowed, jnp.exp(scores - lse_ref[:, h * 128 : h * 128 + 1]), 0.0)
            dscores = (probs * (dot_t(dmix, vals) - delta)).astype(BF)
            dq[h] = dq[h] + dot(dscores, keys)
            dk = dk + t_dot(dscores, query)
            dv = dv + t_dot(probs.astype(BF), dmix)
        dkv = jnp.concatenate([dk, dv], axis=1).astype(BF)
        for part in range(len(dkv_refs)):
            first, last = max(begin, part * each), min(begin + step, (part + 1) * each)
            if first < last:
                dkv_refs[part][first - part * each : last - part * each, :] = dkv[
                    first - begin : last - begin
                ]
    for h in range(heads):
        dq_ref[:, h * HD : (h + 1) * HD] = (dq[h] * HD**-0.5).astype(BF)


def branch_kernel(t_ref, mix_ref, w_ref, *outs):
    tp = len(outs)
    n = w_ref.shape[0]
    cp = outs[0].shape[1]
    ra = mix_ref.shape[0] - (outs[0].shape[0] - 16)
    rp = mix_ref.shape[0] - ra
    kp = cp * tp // n
    for k in range(tp):
        rank = t_ref[0] ^ k
        prefix, action = [], []
        for i in range(n // tp):
            block = w_ref[rank * (n // tp) + i]
            prefix.append(dot(mix_ref[:rp, :], block[:, :kp]))
            action.append(dot(mix_ref[rp:, :], block[:, kp:]))
        action = jnp.concatenate(action, axis=1)
        outs[k][:rp, :] = jnp.concatenate(prefix, axis=1).astype(BF)
        outs[k][rp:, :] = jnp.concatenate(
            [action, jnp.zeros((ra, cp - action.shape[1]), F32)], axis=1
        ).astype(BF)


def middle_kernel(t_ref, *refs):
    tp = lax.axis_size("tp")
    mids = refs[:tp]
    gp_ref, ga_ref, mp_ref, ma_ref, a_ref, b_ref = refs[tp:]
    rp, dp = mp_ref.shape
    ra, da = ma_ref.shape
    cp, ca = dp // tp, da // tp
    for k in range(tp):
        mp_ref[:, place(t_ref[0] ^ k, cp)] = mids[k][:rp, :]
        ma_ref[:, place(t_ref[0] ^ k, ca)] = mids[k][rp:, :ca]
    rows = mp_ref[...].astype(F32)
    prefix = rows * inverse_rms(rows) * gp_ref[...]
    rows = ma_ref[...].astype(F32)
    action = rows * inverse_rms(rows) * ga_ref[...]
    action = jnp.concatenate([action, jnp.zeros((ra, dp - da), F32)], axis=1)
    for number, out in enumerate((a_ref, b_ref)):
        out[...] = jnp.concatenate(
            [
                prefix[number * (rp // 2) : (number + 1) * (rp // 2)],
                action[number * (ra // 2) : (number + 1) * (ra // 2)],
            ],
            axis=0,
        ).astype(BF)


def gelu_parts(value):
    scale = 0.7978845608028654
    square = value * value
    bent = jnp.tanh(scale * (value + 0.044715 * value * square))
    gelu = 0.5 * value * (1.0 + bent)
    slope = 0.5 * (1.0 + bent) + 0.5 * value * (1.0 - bent * bent) * scale * (
        1.0 + 3.0 * 0.044715 * square
    )
    return gelu, slope


def forward_back(rows, cot_rows, gate_up, down):
    f = down.shape[0]
    both = dot(rows, gate_up)
    gelu, slope = gelu_parts(both[:, :f])
    up = both[:, f:]
    dhidden = dot_t(cot_rows, down)
    return gelu * up, jnp.concatenate([dhidden * up * slope, dhidden * gelu], axis=1)


def feed_kernel(pair, x_ref, c_ref, w_ref, d_ref, act_ref, h_ref, g_ref, dn_ref):
    rows, dp = x_ref.shape
    each = rows // pair
    prefix = each - act_ref.shape[0] // pair
    hidden, dgate_up = forward_back(x_ref[...], c_ref[...], w_ref[...], d_ref[...])
    inside = lax.broadcasted_iota(jnp.int32, (rows, 1), 0) % each < prefix
    dgate_up = jnp.where(inside, dgate_up, 0.0).astype(BF)
    h_ref[...] = jnp.where(inside, hidden, 0.0).astype(BF)
    g_ref[...] = dgate_up
    dn = dot_t(dgate_up, w_ref[...])
    action = act_ref[...]
    action = jnp.concatenate(
        [action, jnp.zeros((action.shape[0], dp - action.shape[1]), F32)], axis=1
    )
    begin = 0
    for i in range(pair):
        first, last = i * each + prefix, (i + 1) * each
        low, high = first // 16 * 16, -(-last // 16) * 16
        dn_ref[begin:low, :] = dn[begin:low].astype(BF)
        piece = [dn[low:first], action[i * (each - prefix) : (i + 1) * (each - prefix)]]
        piece = [p for p in piece + [dn[last:high]] if p.shape[0]]
        dn_ref[low:high, :] = jnp.concatenate(piece, axis=0).astype(BF)
        begin = high


def feed(rows_in, cot_rows, gate_up, down, dn_action, each):
    total, dp = rows_in.shape
    pair = 2
    step = pair * each
    f = down.shape[0]
    act_step = dn_action.shape[0] * step // total
    row_spec = pl.BlockSpec((step, dp), lambda i: (i, 0))
    in_specs = [
        row_spec,
        row_spec,
        pl.BlockSpec(gate_up.shape, lambda i: (0, 0)),
        pl.BlockSpec(down.shape, lambda i: (0, 0)),
        pl.BlockSpec((act_step, dn_action.shape[1]), lambda i: (i, 0)),
    ]
    return pl.pallas_call(
        lambda *refs: feed_kernel(pair, *refs),
        grid=(total // step,),
        in_specs=in_specs,
        out_specs=(
            pl.BlockSpec((step, f), lambda i: (i, 0)),
            pl.BlockSpec((step, 2 * f), lambda i: (i, 0)),
            row_spec,
        ),
        out_shape=(
            jax.ShapeDtypeStruct((total, f), BF),
            jax.ShapeDtypeStruct((total, 2 * f), BF),
            jax.ShapeDtypeStruct((total, dp), BF),
        ),
        compiler_params=pltpu.CompilerParams(vmem_limit_bytes=58 * MIB),
        cost_estimate=pl.CostEstimate(
            flops=10 * total * dp * f,
            bytes_accessed=8 * total * dp + 6 * f * dp,
            transcendentals=total * f,
        ),
    )(rows_in, cot_rows, gate_up, down, dn_action)


def feed_action_kernel(x_ref, c_ref, w_ref, d_ref, dn_ref, lift_ref, gw_ref, gd_ref):
    rows, cot_rows = x_ref[...], c_ref[...]
    hidden, dgate_up = forward_back(rows, cot_rows, w_ref[...], d_ref[...])
    hidden, dgate_up = hidden.astype(BF), dgate_up.astype(BF)
    dn_ref[...] = dot_t(dgate_up, w_ref[...])
    lift_ref[...] = dot(hidden, d_ref[...])
    gw_ref[...] = t_dot(rows, dgate_up).astype(BF)
    gd_ref[...] = t_dot(hidden, cot_rows).astype(BF)


def weights_kernel(
    xo_ref, xe_ref, co_ref, ce_ref, ho_ref, he_ref, go_ref, ge_ref, act_ref, gg_ref, gu_ref,
    gd_ref,
):
    f = ho_ref.shape[1]
    kp = gd_ref.shape[2]
    both = t_dot(xo_ref[...], go_ref[...]) + t_dot(xe_ref[...], ge_ref[...])
    gg_ref[...] = both[:, :f].astype(BF)
    gu_ref[...] = both[:, f:].astype(BF)
    down = (t_dot(ho_ref[...], co_ref[...]) + t_dot(he_ref[...], ce_ref[...])).astype(BF)
    for i in range(gd_ref.shape[0]):
        gd_ref[i, :f, :] = down[:, i * kp : (i + 1) * kp]
        gd_ref[i, f:, :] = act_ref[i]


def weight_grads(x_odd, x_even, c_odd, c_even, h_odd, h_even, g_odd, g_even, action):
    total, dp = x_odd.shape
    f = h_odd.shape[1]
    n, extra, kp = action.shape
    wide = 256
    cols = pl.BlockSpec((total, wide), lambda i: (0, i))
    h_spec = pl.BlockSpec((total, f), lambda i: (0, 0))
    g_spec = pl.BlockSpec((total, 2 * f), lambda i: (0, 0))
    return pl.pallas_call(
        weights_kernel,
        grid=(dp // wide,),
        in_specs=[
            cols,
            cols,
            cols,
            cols,
            h_spec,
            h_spec,
            g_spec,
            g_spec,
            pl.BlockSpec((wide // kp, extra, kp), lambda i: (i, 0, 0)),
        ],
        out_specs=(
            pl.BlockSpec((wide, f), lambda i: (i, 0)),
            pl.BlockSpec((wide, f), lambda i: (i, 0)),
            pl.BlockSpec((wide // kp, f + extra, kp), lambda i: (i, 0, 0)),
        ),
        out_shape=(
            jax.ShapeDtypeStruct((dp, f), BF),
            jax.ShapeDtypeStruct((dp, f), BF),
            jax.ShapeDtypeStruct((n, f + extra, kp), BF),
        ),
        compiler_params=pltpu.CompilerParams(vmem_limit_bytes=48 * MIB),
        cost_estimate=pl.CostEstimate(
            flops=12 * total * dp * f, bytes_accessed=8 * total * dp, transcendentals=0
        ),
    )(x_odd, x_even, c_odd, c_even, h_odd, h_even, g_odd, g_even, action)


def lift_kernel(
    odd_ref, pa_ref, pb_ref, la_ref, lb_ref,
    oa_ref, ea_ref, ob_ref, eb_ref, aa_ref, ab_ref, d_ref, out_ref,
):
    odd = odd_ref[pl.program_id(0)] == 1
    dp = out_ref.shape[2]
    prefix = oa_ref.shape[0] - aa_ref.shape[0]
    outs = []
    for o_ref, e_ref in ((oa_ref, ea_ref), (ob_ref, eb_ref)):
        hidden = jnp.where(odd, o_ref[...].astype(F32), e_ref[...].astype(F32)).astype(BF)
        outs.append(dot(hidden, d_ref[...])[:prefix])
    action = jnp.concatenate([aa_ref[...], ab_ref[...]], axis=0)
    action = jnp.concatenate(
        [action, jnp.zeros((action.shape[0], dp - action.shape[1]), F32)], axis=1
    )
    out_ref[0] = jnp.concatenate(outs + [action], axis=0).astype(BF)


def lift(odd, place_a, place_b, lift_a, lift_b, h_odd, h_even, lifted_action, down, each, ra):
    n = odd.shape[0]
    f, dp = down.shape
    da = lifted_action.shape[1]
    a_spec = pl.BlockSpec((each, f), lambda j, o, a, b, la, lb: (a[j], 0))
    b_spec = pl.BlockSpec((each, f), lambda j, o, a, b, la, lb: (b[j], 0))
    rows = 2 * each
    return pl.pallas_call(
        lift_kernel,
        grid_spec=pltpu.PrefetchScalarGridSpec(
            num_scalar_prefetch=5,
            grid=(n,),
            in_specs=[
                a_spec,
                a_spec,
                b_spec,
                b_spec,
                pl.BlockSpec((ra // 2, da), lambda j, o, a, b, la, lb: (la[j], 0)),
                pl.BlockSpec((ra // 2, da), lambda j, o, a, b, la, lb: (lb[j], 0)),
                pl.BlockSpec((f, dp), lambda j, o, a, b, la, lb: (0, 0)),
            ],
            out_specs=pl.BlockSpec((1, rows, dp), lambda j, o, a, b, la, lb: (j, 0, 0)),
        ),
        out_shape=jax.ShapeDtypeStruct((n, rows, dp), BF),
        compiler_params=pltpu.CompilerParams(vmem_limit_bytes=32 * MIB),
        cost_estimate=pl.CostEstimate(
            flops=2 * n * rows * dp * f, bytes_accessed=2 * n * rows * dp, transcendentals=0
        ),
    )(odd, place_a, place_b, lift_a, lift_b, h_odd, h_even, h_odd, h_even,
      lifted_action, lifted_action, down)


def pieces_kernel(t_ref, ka_ref, ga_ref, kb_ref, gb_ref, *outs):
    tp = len(outs)
    each, dp = ka_ref.shape
    cp = dp // tp
    rp = outs[0].shape[0] * 2 * each // (2 * each)
    extra = 8
    prefix = each - extra
    ca = outs[0].shape[1] // 2
    del rp
    for k in range(tp):
        rank = t_ref[0] ^ k
        tops, ends = [], []
        for keep, got in ((ka_ref, ga_ref), (kb_ref, gb_ref)):
            wide = place(rank, cp)
            tops.append(keep[:prefix, wide].astype(F32) + got[:prefix, wide].astype(F32))
            slim = place(rank, ca)
            ends.append(
                keep[prefix:, slim].astype(F32) + got[prefix:, slim].astype(F32)
            )
        action = jnp.concatenate(ends, axis=0)
        action = jnp.concatenate(
            [action, jnp.zeros((action.shape[0], cp - ca), F32)], axis=1
        )
        outs[k][...] = jnp.concatenate(tops + [action], axis=0).astype(BF)


def middle_back_kernel(t_ref, *refs):
    tp = lax.axis_size("tp")
    ds = refs[:tp]
    mp_ref, ma_ref, gp_ref, ga_ref, cp_ref, ca_ref, w_ref = refs[tp : tp + 7]
    bp_ref, ba_ref, own_ref, lp_ref, la_ref, dm_ref, dp_scr, da_scr, rp_scr, ra_scr = refs[tp + 7 :]
    rp, dp = mp_ref.shape
    ra, da = ma_ref.shape
    cp, ca = dp // tp, da // tp
    n = w_ref.shape[0]
    kp = dp // n
    t = t_ref[0]
    for k in range(tp):
        dp_scr[:, place(t ^ k, cp)] = ds[k][:rp, :]
        da_scr[:, place(t ^ k, ca)] = ds[k][rp:, :ca]
    mixes = []
    for d_ref, m_ref, g_ref, c_ref, b_ref, r_ref, l_ref, first, last in (
        (dp_scr, mp_ref, gp_ref, cp_ref, bp_ref, rp_scr, lp_ref, 0, kp),
        (da_scr, ma_ref, ga_ref, ca_ref, ba_ref, ra_scr, la_ref, kp, w_ref.shape[2]),
    ):
        gradient = d_ref[...].astype(F32)
        rows = m_ref[...].astype(F32)
        inverse = inverse_rms(rows)
        centered = rows * inverse
        inner = gradient * g_ref[...]
        dresid = c_ref[...].astype(F32) + inverse * (
            inner - centered * jnp.mean(inner * centered, axis=1, keepdims=True)
        )
        l_ref[...] = jnp.sum(gradient * centered, axis=0, keepdims=True)
        r_ref[...] = dresid
        branch = dresid.astype(BF)
        b_ref[...] = branch
        size = last - first
        mix = jnp.zeros((rows.shape[0], dm_ref.shape[1]), F32)
        for d in range(n):
            mix = mix + dot_t(branch[:, d * size : (d + 1) * size], w_ref[d, :, first:last])
        mixes.append(mix)
    dm_ref[...] = jnp.concatenate(mixes, axis=0).astype(BF)
    own_ref[:rp, :] = rp_scr[:, place(t, cp)]
    own_ref[rp:, :] = jnp.concatenate(
        [ra_scr[:, place(t, ca)], jnp.zeros((ra, cp - ca), F32)], axis=1
    )


def out_grad_kernel(bp_ref, ba_ref, mix_ref, out_ref):
    rp, dp = bp_ref.shape
    n = out_ref.shape[0]
    kp = dp // n
    ka = ba_ref.shape[1] // n
    for d in range(n):
        out_ref[d, :, :kp] = t_dot(mix_ref[:rp, :], bp_ref[:, d * kp : (d + 1) * kp]).astype(BF)
        out_ref[d, :, kp:] = t_dot(mix_ref[rp:, :], ba_ref[:, d * ka : (d + 1) * ka]).astype(BF)


def front_back_kernel(heads_width, s_ref, t_ref, dq_ref, *refs):
    tp = lax.axis_size("tp")
    n = lax.axis_size("seq")
    (ka_ref, ra_ref, kb_ref, rb_ref, xp_ref, xa_ref, inv_ref, gp_ref, ga_ref, w_ref, lp_ref,
     la_ref, lifted_ref) = refs[:13]
    groups = refs[13:17]
    pieces = refs[17 : 17 + tp]
    gwp_scr, gwa_scr, gain_scr, dp_scr, da_scr = refs[17 + tp :]
    rp, dp = xp_ref.shape
    ra, da = xa_ref.shape
    kp, ka = dp // n, da // n
    cp, ca = dp // tp, da // tp
    width = heads_width
    dkv = jnp.concatenate(
        [
            ka_ref[...].astype(F32) + ra_ref[...].astype(F32),
            kb_ref[...].astype(F32) + rb_ref[...].astype(F32),
        ],
        axis=0,
    )
    dqkv = jnp.concatenate([dq_ref[...].astype(F32), dkv], axis=1)
    gain_scr[...] = jnp.zeros(gain_scr.shape, F32)
    dots = []
    for x_ref, g_ref, d_scr, gw_scr, l_ref, begin, end, first, last, size, at in (
        (xp_ref, gp_ref, dp_scr, gwp_scr, lp_ref, 0, rp, 0, kp, kp, 0),
        (xa_ref, ga_ref, da_scr, gwa_scr, la_ref, rp, rp + ra, kp, kp + ka, ka, 256),
    ):
        grad_rows = dqkv[begin:end].astype(BF)
        centered = x_ref[...].astype(F32) * inv_ref[begin:end, :1]
        normed = (centered * g_ref[...]).astype(BF)
        gw_scr[...] = t_dot(normed, grad_rows).astype(BF)
        weights = w_ref[:, first:last, :].reshape(x_ref.shape[1], -1)
        partial = dot_t(grad_rows, weights)
        d_scr[...] = partial
        product = partial * centered
        gains = jnp.sum(product, axis=0, keepdims=True)
        mlp_gains = l_ref[...]
        for d in range(n):
            gain_scr[d, 0:1, at : at + size] = gains[:, d * size : (d + 1) * size]
            gain_scr[d, 0:1, at + 512 : at + 512 + size] = mlp_gains[
                :, d * size : (d + 1) * size
            ]
        dots.append(jnp.sum(product * g_ref[...], axis=1, keepdims=True))
    column = jnp.concatenate(dots, axis=0)
    lanes = lax.broadcasted_iota(jnp.int32, (rp + ra, cp), 1)
    rows = lax.broadcasted_iota(jnp.int32, (rp + ra, cp), 0)
    row = jnp.sum(jnp.where(lanes == rows, column, 0.0), axis=0, keepdims=True)
    high = row.astype(BF).astype(F32)
    tail = jnp.concatenate([high, row - high, jnp.zeros((6, cp), F32)], axis=0)
    for k in range(tp):
        rank = t_ref[0] ^ k
        action = jnp.concatenate(
            [da_scr[:, place(rank, ca)], jnp.zeros((ra, cp - ca), F32)], axis=1
        )
        lifted_action = jnp.concatenate(
            [lifted_ref[rp:, place(rank, ca)].astype(F32), jnp.zeros((ra, cp - ca), F32)], axis=1
        )
        lifted = lifted_ref[:rp, place(rank, cp)].astype(F32)
        pieces[k][...] = jnp.concatenate(
            [dp_scr[:, place(rank, cp)], action, tail, lifted, lifted_action], axis=0
        ).astype(BF)
    for odd in range(2):
        for number in range(2):
            out = groups[2 * odd + number]
            for i, k in enumerate(block_order(number)):
                d = s_ref[0] ^ (k ^ odd)
                hp, ha = kp // 2, ka // 2
                out[i, :hp, :] = gwp_scr[
                    pl.ds(pl.multiple_of(d * kp + number * hp, hp), hp), :
                ]
                out[i, hp : hp + ha, :] = gwa_scr[
                    pl.ds(pl.multiple_of(d * ka + number * ha, ha), ha), :
                ]
                out[i, hp + ha :, :] = gain_scr[d].astype(BF) * BF(1 - number)


def grad_x_kernel(t_ref, *refs):
    tp = lax.axis_size("tp")
    ds = refs[:tp]
    x_ref, inv_ref, gp_ref, ga_ref, r_ref, op_ref, oa_ref = refs[tp:]
    rp, cp = op_ref.shape
    ra, ca = oa_ref.shape
    t = t_ref[0]
    total = ds[0][...].astype(F32)
    for k in range(1, tp):
        total = total + ds[k][...].astype(F32)
    row = total[rp + ra : rp + ra + 1] + total[rp + ra + 1 : rp + ra + 2]
    lanes = lax.broadcasted_iota(jnp.int32, (rp + ra, cp), 1)
    rows = lax.broadcasted_iota(jnp.int32, (rp + ra, cp), 0)
    column = jnp.sum(jnp.where(lanes == rows, row, 0.0), axis=1, keepdims=True)
    for o_ref, g_ref, begin, end, wide in (
        (op_ref, gp_ref, 0, rp, cp),
        (oa_ref, ga_ref, rp, rp + ra, ca),
    ):
        inverse = inv_ref[begin:end, :1]
        centered = x_ref[begin:end, :wide].astype(F32) * inverse
        mean = column[begin:end] / (wide * tp)
        moved = inverse * (
            total[begin:end, :wide] * g_ref[:, place(t, wide)] - centered * mean
        )
        o_ref[...] = (r_ref[begin:end, :wide] + moved).astype(BF)


def home_kernel(token_ref, g_ref, d_ref, gate_ref, down_ref, act_ref):
    del token_ref
    f = gate_ref.shape[1]
    gate_ref[...] = g_ref[0].astype(F32)
    down_ref[...] = d_ref[0, :f, :].astype(F32)
    act_ref[0] = d_ref[0, f:, :].astype(F32)


def home(token, got_gate, got_down):
    n, kp, f = got_gate.shape
    tall = got_down.shape[1]
    return pl.pallas_call(
        home_kernel,
        grid=(n,),
        in_specs=[
            pl.BlockSpec(memory_space=pltpu.SMEM),
            pl.BlockSpec((1, kp, f), lambda j: (j, 0, 0)),
            pl.BlockSpec((1, tall, kp), lambda j: (j, 0, 0)),
        ],
        out_specs=(
            pl.BlockSpec((kp, f), lambda j: (0, j)),
            pl.BlockSpec((f, kp), lambda j: (j, 0)),
            pl.BlockSpec((1, tall - f, kp), lambda j: (j, 0, 0)),
        ),
        out_shape=(
            jax.ShapeDtypeStruct((kp, n * f), F32),
            jax.ShapeDtypeStruct((n * f, kp), F32),
            jax.ShapeDtypeStruct((n, tall - f, kp), F32),
        ),
        cost_estimate=pl.CostEstimate(
            flops=0, bytes_accessed=6 * n * kp * (f + tall), transcendentals=0
        ),
    )(token, got_gate, got_down)


def home_up_kernel(u_ref, up_ref):
    up_ref[...] = u_ref[0].astype(F32)


def home_up(got):
    n, kp, f = got.shape
    return pl.pallas_call(
        home_up_kernel,
        grid=(n,),
        in_specs=[pl.BlockSpec((1, kp, f), lambda j: (j, 0, 0))],
        out_specs=pl.BlockSpec((kp, f), lambda j: (0, j)),
        out_shape=jax.ShapeDtypeStruct((kp, n * f), F32),
        cost_estimate=pl.CostEstimate(
            flops=0, bytes_accessed=6 * n * kp * f, transcendentals=0
        ),
    )(got)


def shards(
    x_prefix,
    x_action,
    prefix_segment,
    prefix_attn_gain,
    prefix_query,
    prefix_key,
    prefix_value,
    prefix_out,
    prefix_mlp_gain,
    prefix_gate,
    prefix_up,
    prefix_down,
    action_attn_gain,
    action_query,
    action_key,
    action_value,
    action_out,
    action_mlp_gain,
    action_gate,
    action_up,
    action_down,
    cot_prefix,
    cot_action,
):
    n = lax.axis_size("seq")
    tp = lax.axis_size("tp")
    s = lax.axis_index("seq")
    t = lax.axis_index("tp")
    rank_t = t.astype(jnp.int32).reshape(1)
    rank_s = s.astype(jnp.int32).reshape(1)
    rp, cp = x_prefix.shape
    ra, ca = x_action.shape
    rows = rp + ra
    half = rows // 2
    dp, da = cp * tp, ca * tp
    kp, ka = dp // n, da // n
    width = prefix_query.shape[1]
    qkv_width = width + 2 * HD
    fp, fa = prefix_gate.shape[1] // n, action_gate.shape[1] // n

    x_pack = jnp.concatenate(
        [x_prefix, jnp.pad(x_action, ((0, 0), (0, cp - ca)))], axis=0
    )
    x_pieces = gather_tp(x_pack)
    gains = jnp.concatenate(
        [prefix_attn_gain, prefix_mlp_gain, action_attn_gain, action_mlp_gain]
    )
    gain_rows = -(-gains.shape[0] // qkv_width)
    gains = jnp.pad(gains, (0, 8 * qkv_width - gains.shape[0])).reshape(8, qkv_width)
    pack_qkv = jnp.concatenate(
        [
            jnp.concatenate([prefix_query, prefix_key, prefix_value], axis=1),
            jnp.concatenate([action_query, action_key, action_value], axis=1),
            gains,
        ],
        axis=0,
    )
    got_qkv = lax.all_gather(pack_qkv, "seq", axis=0)
    got_gains = got_qkv[:, kp + ka : kp + ka + gain_rows].reshape(n, -1).astype(F32)
    attn_gain_p = got_gains[:, :kp].reshape(1, dp)
    mlp_gain_p = got_gains[:, kp : 2 * kp].reshape(1, dp)
    attn_gain_a = got_gains[:, 2 * kp : 2 * kp + ka].reshape(1, da)
    mlp_gain_a = got_gains[:, 2 * kp + ka : 2 * kp + 2 * ka].reshape(1, da)
    pack_out = jnp.concatenate([prefix_out, action_out], axis=1)
    cot_wide = jnp.pad(cot_action, ((0, 0), (0, dp - da)))
    cot_stages, cot_last = gather_stacked(
        [
            jnp.concatenate(
                [
                    cot_prefix[i * (rp // 2) : (i + 1) * (rp // 2)],
                    cot_wide[i * (ra // 2) : (i + 1) * (ra // 2)],
                ],
                axis=0,
            )
            for i in range(2)
        ]
    )
    cot_odd, cot_even = near_rows(cot_stages[-1])

    def by_units(w, f):
        return w.reshape(w.shape[0], n, f).transpose(1, 0, 2)

    gate_up_sent = jnp.concatenate([by_units(prefix_gate, fp), by_units(prefix_up, fp)], axis=2)
    action_sent = jnp.concatenate(
        [
            by_units(action_gate, fa),
            by_units(action_up, fa),
            action_down.reshape(n, fa, ka).transpose(0, 2, 1),
        ],
        axis=2,
    ).reshape(n, -1, kp)
    extra = action_sent.shape[1]
    down_sent = jnp.concatenate([prefix_down.reshape(n, fp, kp), action_sent], axis=1)

    queries, kv_a, kv_b, x_full_p, x_full_a, inverse1 = whole_call(
        front_kernel,
        (
            ((rows, width), BF),
            ((half, 2 * HD), BF),
            ((half, 2 * HD), BF),
            ((rp, dp), BF),
            ((ra, da), BF),
            ((rows, 128), F32),
        ),
        [after(rank_t, *cot_last), *x_pieces, got_qkv, attn_gain_p, attn_gain_a],
        2 * rp * dp * qkv_width,
    )
    kv_even = [jnp.concatenate(blocks, axis=0) for blocks in gather_far([kv_a, kv_b])]
    kv_odd = [swap(e, "seq", 1) for e in kv_even]
    keys_values = jnp.concatenate([kv_even[0], kv_odd[0], kv_even[1], kv_odd[1]], axis=0)
    codes = token_codes(prefix_segment, n, ra)
    query_code = lax.dynamic_slice_in_dim(codes, s, 1, 0).reshape(rows, 1)
    key_code = jnp.concatenate(
        [
            lax.dynamic_slice(codes, (s ^ k ^ odd, number * half), (1, half))
            for number in range(2)
            for odd in range(2)
            for k in block_order(number)
        ],
        axis=1,
    )
    attended, mixed, log_sum = whole_call(
        attend_kernel,
        (
            ((rows, width), F32),
            ((rows, width), BF),
            ((rows, width // HD * 128), F32),
        ),
        [queries, keys_values, query_code, key_code],
        4 * rows * width * n * rows,
        transcendentals=rows * width // HD * n * rows,
    )
    got_out = lax.all_gather(after(pack_out, queries), "seq", axis=0)
    down_got = lax.all_to_all(after(down_sent, keys_values), "seq", 0, 0)

    piece = (((rows, cp), BF),)
    branch = sum_tp(
        whole_call(
            branch_kernel, piece * tp, [rank_t, mixed, got_out], 2 * rows * dp * width
        )
    )
    residual = x_pack.astype(F32) + branch
    mid_own = after(residual.astype(BF), down_got)
    gate_up = lax.all_to_all(after(gate_up_sent, branch), "seq", 0, 0).reshape(dp, 2 * fp)
    down = down_got[:, :fp].transpose(1, 0, 2).reshape(fp, dp)
    action_got = down_got[:, fp:].reshape(da, 3 * fa)
    gate_up_action = action_got[:, : 2 * fa]
    down_action = action_got[:, 2 * fa :].T


    def action_rows(blocks):
        return blocks.reshape(n, half, dp)[:, rp // 2 :, :da].reshape(-1, da)

    cot_action_all = jnp.concatenate([action_rows(cot_odd), action_rows(cot_even)], axis=0)
    block = (((half, dp), BF),)
    mid_p, mid_a, normed_a, normed_b = whole_call(
        middle_kernel,
        (((rp, dp), BF), ((ra, da), BF)) + block * 2,
        [after(rank_t, gate_up, down, gate_up_action, down_action, cot_action_all), *gather_tp(mid_own), mlp_gain_p, mlp_gain_a],
        rp * dp,
    )

    normed_odd, normed_even = near_rows(
        [b for blocks in gather_far([normed_a, normed_b]) for b in blocks]
    )
    normed_action = jnp.concatenate([action_rows(normed_odd), action_rows(normed_even)], axis=0)
    tokens = n * ra
    dn_action, lifted_action, grad_gu_action, grad_down_action = whole_call(
        feed_action_kernel,
        (
            ((tokens, da), F32),
            ((tokens, da), F32),
            ((da, 2 * fa), BF),
            ((fa, da), BF),
        ),
        [normed_action, cot_action_all, gate_up_action, down_action],
        18 * tokens * da * fa,
    )
    h_odd, g_odd, dn_odd = feed(
        normed_odd, cot_odd, gate_up, down, dn_action[: tokens // 2], half
    )
    h_even, g_even, dn_even = feed(
        normed_even, cot_even, gate_up, down, dn_action[tokens // 2 :], half
    )
    dn_blocks = [
        d.reshape(2, n // 2, half, dp) for d in (dn_even, swap(dn_odd, "seq", 1))
    ]

    grad_gu_action, grad_down_action = after((grad_gu_action, grad_down_action), dn_even)
    action_grads = jnp.concatenate(
        [
            grad_gu_action.reshape(n, ka, 2 * fa),
            grad_down_action.reshape(fa, n, ka).transpose(1, 2, 0),
        ],
        axis=2,
    ).reshape(n, extra, kp)
    grad_gate, grad_up, grad_down = weight_grads(
        normed_odd, normed_even, cot_odd, cot_even, h_odd, h_even, g_odd, g_even, action_grads
    )
    ranks = s ^ jnp.arange(n, dtype=jnp.int32)
    odd_bits = ranks & 1
    places = []
    for number in range(2):
        table = [0] * n
        for i, k in enumerate(block_order(number)):
            table[k] = table[k ^ 1] = number * (n // 2) + i
        places.append(jnp.array(table, jnp.int32)[ranks])
    lift_places = [p + (1 - odd_bits) * n for p in places]
    lifted = lift(
        odd_bits, *places, *lift_places, h_odd, h_even, lifted_action, down, half, ra
    )
    ((keep_a, got_a), (keep_b, got_b)), *_ = scatter_rows(
        [(dn_blocks[0][i], dn_blocks[1][i]) for i in range(2)], grad_gate
    )
    sent_pieces = whole_call(
        pieces_kernel,
        piece * tp,
        [after(rank_t, lifted), keep_a, got_a, keep_b, got_b],
        rp * dp,
    )
    dn_own = sum_tp(sent_pieces)
    dn_pieces = gather_tp(dn_own.astype(BF))
    lifted_home = lax.psum_scatter(after(lifted, got_a, got_b), "seq", scatter_dimension=0)
    grad_down_home = lax.all_to_all(after(grad_down, sent_pieces[0]), "seq", 0, 0)

    grad_gate_home = lax.all_to_all(
        after(grad_gate, grad_down_home).reshape(n, kp, fp), "seq", 0, 0
    )

    row = ((1, dp), F32)
    row_a = ((1, da), F32)
    dbranch_p, dbranch_a, dresid, mlp_gains_p, mlp_gains_a, dmixed = whole_call(
        middle_back_kernel,
        (((rp, dp), BF), ((ra, da), BF), ((rows, cp), F32), row, row_a, ((rows, width), BF)),
        [after(rank_t, grad_down_home), *dn_pieces, mid_p, mid_a, mlp_gain_p, mlp_gain_a, cot_prefix, cot_action, got_out],
        2 * rows * dp * width,
        scratch=(
            pltpu.VMEM((rp, dp), BF),
            pltpu.VMEM((ra, da), BF),
            pltpu.VMEM((rp, dp), F32),
            pltpu.VMEM((ra, da), F32),
        ),
    )
    dquery, *dkv_parts = whole_call(
        attend_back_kernel,
        (((rows, width), BF),) + (((n * rows // 4, 2 * HD), BF),) * 4,
        [queries, keys_values, query_code, key_code, attended, log_sum, dmixed],
        10 * rows * width * n * rows,
        limit=56,
        transcendentals=rows * width // HD * n * rows,
    )
    dkv_halves = [
        [d.reshape(n // 2, half, 2 * HD) for d in (e, swap(o, "seq", 1))]
        for e, o in ((dkv_parts[0], dkv_parts[1]), (dkv_parts[2], dkv_parts[3]))
    ]
    dkv = [part for pair in scatter_rows(dkv_halves, grad_gate_home)[0] for part in pair]
    (out_grads,) = whole_call(
        out_grad_kernel,
        (((n, width, kp + ka), BF),),
        [dbranch_p, dbranch_a, after(mixed, dquery)],
        2 * rows * dp * width,
    )
    out_home = lax.psum_scatter(out_grads, "seq", scatter_dimension=0)
    tall = (kp + ka) // 2 + 8
    *groups_and_pieces, = whole_call(
        lambda *refs: front_back_kernel(width, *refs),
        (((n // 2, tall, qkv_width), BF),) * 4 + (((2 * rows + 8, cp), BF),) * tp,
        [
            rank_s, rank_t, dquery, *dkv, x_full_p, x_full_a, inverse1, attn_gain_p, attn_gain_a,
            got_qkv, mlp_gains_p, mlp_gains_a, lifted_home,
        ],
        4 * rows * dp * qkv_width,
        scratch=(
            pltpu.VMEM((dp, qkv_width), BF),
            pltpu.VMEM((da, qkv_width), BF),
            pltpu.VMEM((n, 8, qkv_width), F32),
            pltpu.VMEM((rp, dp), F32),
            pltpu.VMEM((ra, da), F32),
        ),
    )
    groups, pieces = groups_and_pieces[:4], groups_and_pieces[4:]
    tree, history, (tp_parts, _) = scatter_rows(
        [(e, swap(o, "seq", 1)) for e, o in ((groups[0], groups[2]), (groups[1], groups[3]))],
        None,
        (trade_tp(pieces), ()),
    )
    lifted_parts = [part[rows + 8 :] for part in tp_parts]
    grad_up_home = lax.all_to_all(
        after(grad_up, grad_gate_home, groups[0]).reshape(n, kp, fp), "seq", 0, 0
    )
    qkv_a, qkv_b = [add(keep, got) for keep, got in tree]
    output = (residual + total_of(lifted_parts)).astype(BF)
    grad_x_p, grad_x_a = whole_call(
        grad_x_kernel,
        (((rp, cp), BF), ((ra, ca), BF)),
        [
            after(rank_t, history[-1]), *tp_parts, x_pack,
            inverse1, attn_gain_p, attn_gain_a, dresid,
        ],
        rp * dp,
    )
    hp, ha = kp // 2, ka // 2
    qkv_home_p = jnp.concatenate([qkv_a[:hp], qkv_b[:hp]], axis=0)
    qkv_home_a = jnp.concatenate([qkv_a[hp : hp + ha], qkv_b[hp : hp + ha]], axis=0)
    gains_home = qkv_a[hp + ha :]
    qp, qa = kp // tp, ka // tp

    attn_gains = jnp.pad(gains_home[:1, :512], ((0, 7), (0, 0)))

    def shared_piece(rank):
        return jnp.concatenate(
            [
                lax.dynamic_slice_in_dim(qkv_home_p[:, width:], rank * qp, qp, 0),
                lax.dynamic_slice_in_dim(qkv_home_a[:, width:], rank * qa, qa, 0),
                attn_gains,
            ],
            axis=0,
        )

    shared_home = sum_tp([shared_piece(t ^ k) for k in range(tp)])
    attn_gains_home = shared_home[qp + qa]
    out_home = after(out_home, *history[-1]).astype(F32)
    grad_gate_p, grad_down_p, action_home = home(
        after(rank_t, history[0]), grad_gate_home, grad_down_home
    )
    grad_up_p = home_up(grad_up_home)
    action_home = action_home.reshape(n, ka, 3 * fa)

    def units(part):
        return part.transpose(1, 0, 2).reshape(ka, n * fa)

    grad_gate_a = units(action_home[:, :, :fa])
    grad_up_a = units(action_home[:, :, fa : 2 * fa])
    grad_down_a = action_home[:, :, 2 * fa :].transpose(0, 2, 1).reshape(n * fa, ka)
    return (
        output[:rp],
        output[rp:, :ca],
        grad_x_p,
        grad_x_a,
        attn_gains_home[:kp],
        qkv_home_p[:, :width],
        shared_home[:qp, :HD],
        shared_home[:qp, HD:],
        out_home[:, :kp],
        gains_home[0, 512 : 512 + kp],
        grad_gate_p,
        grad_up_p,
        grad_down_p,
        attn_gains_home[256 : 256 + ka],
        qkv_home_a[:, :width],
        shared_home[qp : qp + qa, :HD],
        shared_home[qp : qp + qa, HD:],
        out_home[:, kp:],
        gains_home[0, 768 : 768 + ka],
        grad_gate_a,
        grad_up_a,
        grad_down_a,
    )


def solution(mesh):
    split = P("seq", "tp")
    turned = P("tp", "seq")
    both = P(("seq", "tp"), None)
    one = P("seq")
    rows = P("seq", None)
    stream_in = (one, split, rows, rows, turned, one, split, split, turned)
    stream_out = (one, split, both, both, turned, one, split, split, turned)
    return jax.shard_map(
        shards,
        mesh=mesh,
        in_specs=(split, split, P()) + stream_in + stream_in + (rows, rows),
        out_specs=(split, split, split, split) + stream_out + stream_out,
        check_vma=False,
    )
```

```python
import jax
import jax.numpy as jnp
from jax import lax
from jax.experimental import pallas as pl
from jax.experimental.pallas import tpu as pltpu
from jax.sharding import PartitionSpec as P

HD = 256
IMG = 768
TXT = 48
ACT = 50
EPS = 1e-06
NEG = -1e30
BF = jnp.bfloat16
F32 = jnp.float32
MIB = 1 << 20


def swap(value, axis, mask):
    count = lax.axis_size(axis)
    return lax.ppermute(value, axis, [(i, i ^ mask) for i in range(count)])


def after(values, *tokens):
    return lax.optimization_barrier((values, tokens))[0]


def far_masks():
    count = lax.axis_size("seq")
    masks = [1 << b for b in range(1, count.bit_length() - 1)]
    return masks, masks[::-1]


def block_order(number):
    order = [0]
    for mask in far_masks()[number]:
        order = order + [k ^ mask for k in order]
    return order


def gather_far(halves):
    results = []
    for half, masks in zip(halves, far_masks()):
        blocks = [half]
        for mask in masks:
            blocks = blocks + [swap(b, "seq", mask) for b in blocks]
        results.append(blocks)
    return results


def gather_stacked(halves):
    stages = [list(halves)]
    for step in range(len(far_masks()[0])):
        got = [swap(b, "seq", masks[step]) for b, masks in zip(stages[-1], far_masks())]
        got = lax.optimization_barrier(got)
        stages.append([jnp.concatenate(pair, axis=0) for pair in zip(stages[-1], got)])
    return stages[1:], got


def near_rows(blocks):
    even = jnp.concatenate(blocks, axis=0)
    return swap(even, "seq", 1), even


def add(left, right):
    return left.astype(F32) + right.astype(F32)


def scatter_rows(halves, token=None, beside=((), ())):
    parts = [list(half) for half in halves]
    orders = [masks[::-1] for masks in far_masks()]
    steps = len(orders[0])
    history = []
    beside = list(beside)
    for step in range(steps):
        keep = parts[0][0].shape[0] // 2
        sent = [total_of([p[keep:] for p in part]).astype(BF) for part in parts]
        if token is not None and step == steps - 1:
            sent = after(sent, token)
        got = [swap(part, "seq", order[step]) for part, order in zip(sent, orders)]
        for place, when in enumerate((0, steps - 1)):
            if step == when and beside[place]:
                got, beside[place] = lax.optimization_barrier((got, beside[place]))
        parts = [[p[:keep] for p in part] + [g] for part, g in zip(parts, got)]
        history.append(sent)
    return [(total_of([p[0] for p in part[:-1]]), part[-1][0]) for part in parts], history, beside


def gather_tp(piece):
    return [piece] + [swap(piece, "tp", k) for k in range(1, lax.axis_size("tp"))]


def trade_tp(pieces):
    return [pieces[0]] + [swap(pieces[k].astype(BF), "tp", k) for k in range(1, len(pieces))]


def total_of(addends):
    total = addends[0].astype(F32)
    for part in addends[1:]:
        total = total + part.astype(F32)
    return total


def sum_tp(pieces):
    return total_of(trade_tp(pieces))


def dot(left, right):
    return jnp.dot(left, right, preferred_element_type=F32)


def dot_t(left, right):
    return lax.dot_general(left, right, (((1,), (1,)), ((), ())), preferred_element_type=F32)


def t_dot(left, right):
    return lax.dot_general(left, right, (((0,), (0,)), ((), ())), preferred_element_type=F32)


def whole_call(kernel, outs, args, flops, scratch=(), limit=48, transcendentals=0):
    specs = [
        pl.BlockSpec(memory_space=pltpu.SMEM if a.ndim == 1 else pltpu.VMEM) for a in args
    ]
    outs = tuple(jax.ShapeDtypeStruct(shape, dtype) for shape, dtype in outs)
    moved = sum(a.size * a.dtype.itemsize for a in args)
    moved += sum(o.size * o.dtype.itemsize for o in outs)
    return pl.pallas_call(
        kernel,
        out_shape=outs,
        in_specs=specs,
        out_specs=tuple(pl.BlockSpec(memory_space=pltpu.VMEM) for _ in outs),
        scratch_shapes=list(scratch),
        compiler_params=pltpu.CompilerParams(vmem_limit_bytes=limit * MIB),
        cost_estimate=pl.CostEstimate(
            flops=int(flops), bytes_accessed=int(moved), transcendentals=int(transcendentals)
        ),
    )(*args)


def inverse_rms(values):
    return lax.rsqrt(jnp.mean(values * values, axis=1, keepdims=True) + EPS)


def place(rank, width):
    return pl.ds(pl.multiple_of(rank * width, width), width)


def token_codes(prefix_segment, seq_count, suf_rows):
    items_all = prefix_segment.shape[0] // (IMG + TXT)
    places = jnp.arange(seq_count * suf_rows, dtype=jnp.int32)
    items_of = places // (ACT + 1)
    suffix_seg = jnp.where(items_of < items_all, items_of, items_all)
    suffix_lvl = jnp.where((items_of < items_all) & (places % (ACT + 1) == 0), 1, 2)
    suffix = (suffix_seg * 4 + suffix_lvl).astype(jnp.int32)
    return jnp.concatenate(
        [(prefix_segment * 4).reshape(seq_count, -1), suffix.reshape(seq_count, -1)], axis=1
    )


def front_kernel(t_ref, *refs):
    tp = lax.axis_size("tp")
    xs = refs[:tp]
    w_ref, gp_ref, ga_ref, q_ref, kva_ref, kvb_ref, xp_ref, xa_ref, inv_ref = refs[tp:]
    rp, dp = xp_ref.shape
    ra, da = xa_ref.shape
    cp, ca = dp // tp, da // tp
    kp, ka = dp // w_ref.shape[0], da // w_ref.shape[0]
    width = q_ref.shape[1]
    half = kva_ref.shape[0]
    for k in range(tp):
        xp_ref[:, place(t_ref[0] ^ k, cp)] = xs[k][:rp, :]
        xa_ref[:, place(t_ref[0] ^ k, ca)] = xs[k][rp:, :ca]
    parts = []
    inverses = []
    for x_ref, g_ref, first, last, size in (
        (xp_ref, gp_ref, 0, kp, dp),
        (xa_ref, ga_ref, kp, kp + ka, da),
    ):
        rows = x_ref[...].astype(F32)
        inverse = inverse_rms(rows)
        normed = (rows * inverse * g_ref[...]).astype(BF)
        parts.append(dot(normed, w_ref[:, first:last, :].reshape(size, -1)))
        inverses.append(inverse)
    qkv = jnp.concatenate(parts, axis=0)
    q_ref[...] = qkv[:, :width].astype(BF)
    kva_ref[...] = qkv[:half, width:].astype(BF)
    kvb_ref[...] = qkv[half:, width:].astype(BF)
    inv_ref[...] = jnp.broadcast_to(jnp.concatenate(inverses, axis=0), inv_ref.shape)


def key_step(count):
    for step in (2176, 1088, 544, 272):
        if count % step == 0:
            return step
    return count


def attend_kernel(q_ref, kv_ref, qc_ref, kc_ref, att_ref, mix_ref, lse_ref):
    rows = q_ref.shape[0]
    heads = q_ref.shape[1] // HD
    count = kv_ref.shape[0]
    step = key_step(count)
    code = qc_ref[...]
    low = code - code % 4
    for h in range(heads):
        query = q_ref[:, h * HD : (h + 1) * HD] * BF(HD**-0.5)
        top = jnp.full((rows, 1), NEG, F32)
        mass = jnp.zeros((rows, 1), F32)
        total = jnp.zeros((rows, HD), F32)
        for begin in range(0, count, step):
            keys = kv_ref[begin : begin + step, :HD]
            marks = kc_ref[:, begin : begin + step]
            allowed = (marks >= low) & (marks <= code)
            scores = jnp.where(allowed, dot_t(query, keys), NEG)
            new_top = jnp.maximum(top, jnp.max(scores, axis=1, keepdims=True))
            expo = jnp.where(allowed, jnp.exp(scores - new_top), 0.0)
            shrink = jnp.exp(top - new_top)
            mass = mass * shrink + jnp.sum(expo, axis=1, keepdims=True)
            total = total * shrink + dot(expo.astype(BF), kv_ref[begin : begin + step, HD:])
            top = new_top
        attended = total / mass
        att_ref[:, h * HD : (h + 1) * HD] = attended
        mix_ref[:, h * HD : (h + 1) * HD] = attended.astype(BF)
        lse_ref[:, h * 128 : (h + 1) * 128] = jnp.broadcast_to(top + jnp.log(mass), (rows, 128))


def attend_back_kernel(
    q_ref, kv_ref, qc_ref, kc_ref, att_ref, lse_ref, dm_ref, dq_ref, *dkv_refs
):
    rows = q_ref.shape[0]
    heads = q_ref.shape[1] // HD
    count = kv_ref.shape[0]
    step = key_step(count)
    each = dkv_refs[0].shape[0]
    code = qc_ref[...]
    low = code - code % 4
    dq = [jnp.zeros((rows, HD), F32) for _ in range(heads)]
    for begin in range(0, count, step):
        keys = kv_ref[begin : begin + step, :HD]
        vals = kv_ref[begin : begin + step, HD:]
        marks = kc_ref[:, begin : begin + step]
        allowed = (marks >= low) & (marks <= code)
        dk = jnp.zeros((step, HD), F32)
        dv = jnp.zeros((step, HD), F32)
        for h in range(heads):
            span = slice(h * HD, (h + 1) * HD)
            query = q_ref[:, span] * BF(HD**-0.5)
            dmix = dm_ref[:, span]
            delta = jnp.sum(dmix.astype(F32) * att_ref[:, span], axis=1, keepdims=True)
            scores = dot_t(query, keys)
            probs = jnp.where(allowed, jnp.exp(scores - lse_ref[:, h * 128 : h * 128 + 1]), 0.0)
            dscores = (probs * (dot_t(dmix, vals) - delta)).astype(BF)
            dq[h] = dq[h] + dot(dscores, keys)
            dk = dk + t_dot(dscores, query)
            dv = dv + t_dot(probs.astype(BF), dmix)
        dkv = jnp.concatenate([dk, dv], axis=1).astype(BF)
        for part in range(len(dkv_refs)):
            first, last = max(begin, part * each), min(begin + step, (part + 1) * each)
            if first < last:
                dkv_refs[part][first - part * each : last - part * each, :] = dkv[
                    first - begin : last - begin
                ]
    for h in range(heads):
        dq_ref[:, h * HD : (h + 1) * HD] = (dq[h] * HD**-0.5).astype(BF)


def branch_kernel(t_ref, mix_ref, w_ref, *outs):
    tp = len(outs)
    n = w_ref.shape[0]
    cp = outs[0].shape[1]
    ra = mix_ref.shape[0] - (outs[0].shape[0] - 16)
    rp = mix_ref.shape[0] - ra
    kp = cp * tp // n
    for k in range(tp):
        rank = t_ref[0] ^ k
        prefix, action = [], []
        for i in range(n // tp):
            block = w_ref[rank * (n // tp) + i]
            prefix.append(dot(mix_ref[:rp, :], block[:, :kp]))
            action.append(dot(mix_ref[rp:, :], block[:, kp:]))
        action = jnp.concatenate(action, axis=1)
        outs[k][:rp, :] = jnp.concatenate(prefix, axis=1).astype(BF)
        outs[k][rp:, :] = jnp.concatenate(
            [action, jnp.zeros((ra, cp - action.shape[1]), F32)], axis=1
        ).astype(BF)


def middle_kernel(t_ref, *refs):
    tp = lax.axis_size("tp")
    mids = refs[:tp]
    gp_ref, ga_ref, mp_ref, ma_ref, a_ref, b_ref = refs[tp:]
    rp, dp = mp_ref.shape
    ra, da = ma_ref.shape
    cp, ca = dp // tp, da // tp
    for k in range(tp):
        mp_ref[:, place(t_ref[0] ^ k, cp)] = mids[k][:rp, :]
        ma_ref[:, place(t_ref[0] ^ k, ca)] = mids[k][rp:, :ca]
    rows = mp_ref[...].astype(F32)
    prefix = rows * inverse_rms(rows) * gp_ref[...]
    rows = ma_ref[...].astype(F32)
    action = rows * inverse_rms(rows) * ga_ref[...]
    action = jnp.concatenate([action, jnp.zeros((ra, dp - da), F32)], axis=1)
    for number, out in enumerate((a_ref, b_ref)):
        out[...] = jnp.concatenate(
            [
                prefix[number * (rp // 2) : (number + 1) * (rp // 2)],
                action[number * (ra // 2) : (number + 1) * (ra // 2)],
            ],
            axis=0,
        ).astype(BF)


def gelu_parts(value):
    scale = 0.7978845608028654
    square = value * value
    bent = jnp.tanh(scale * (value + 0.044715 * value * square))
    gelu = 0.5 * value * (1.0 + bent)
    slope = 0.5 * (1.0 + bent) + 0.5 * value * (1.0 - bent * bent) * scale * (
        1.0 + 3.0 * 0.044715 * square
    )
    return gelu, slope


def forward_back(rows, cot_rows, gate_up, down):
    f = down.shape[0]
    both = dot(rows, gate_up)
    gelu, slope = gelu_parts(both[:, :f])
    up = both[:, f:]
    dhidden = dot_t(cot_rows, down)
    return gelu * up, jnp.concatenate([dhidden * up * slope, dhidden * gelu], axis=1)


def feed_kernel(pair, x_ref, c_ref, w_ref, d_ref, act_ref, h_ref, g_ref, dn_ref):
    rows, dp = x_ref.shape
    each = rows // pair
    prefix = each - act_ref.shape[0] // pair
    hidden, dgate_up = forward_back(x_ref[...], c_ref[...], w_ref[...], d_ref[...])
    inside = lax.broadcasted_iota(jnp.int32, (rows, 1), 0) % each < prefix
    dgate_up = jnp.where(inside, dgate_up, 0.0).astype(BF)
    h_ref[...] = jnp.where(inside, hidden, 0.0).astype(BF)
    g_ref[...] = dgate_up
    dn = dot_t(dgate_up, w_ref[...])
    action = act_ref[...]
    action = jnp.concatenate(
        [action, jnp.zeros((action.shape[0], dp - action.shape[1]), F32)], axis=1
    )
    begin = 0
    for i in range(pair):
        first, last = i * each + prefix, (i + 1) * each
        low, high = first // 16 * 16, -(-last // 16) * 16
        dn_ref[begin:low, :] = dn[begin:low].astype(BF)
        piece = [dn[low:first], action[i * (each - prefix) : (i + 1) * (each - prefix)]]
        piece = [p for p in piece + [dn[last:high]] if p.shape[0]]
        dn_ref[low:high, :] = jnp.concatenate(piece, axis=0).astype(BF)
        begin = high


def feed(rows_in, cot_rows, gate_up, down, dn_action, each):
    total, dp = rows_in.shape
    pair = 2
    step = pair * each
    f = down.shape[0]
    act_step = dn_action.shape[0] * step // total
    row_spec = pl.BlockSpec((step, dp), lambda i: (i, 0))
    in_specs = [
        row_spec,
        row_spec,
        pl.BlockSpec(gate_up.shape, lambda i: (0, 0)),
        pl.BlockSpec(down.shape, lambda i: (0, 0)),
        pl.BlockSpec((act_step, dn_action.shape[1]), lambda i: (i, 0)),
    ]
    return pl.pallas_call(
        lambda *refs: feed_kernel(pair, *refs),
        grid=(total // step,),
        in_specs=in_specs,
        out_specs=(
            pl.BlockSpec((step, f), lambda i: (i, 0)),
            pl.BlockSpec((step, 2 * f), lambda i: (i, 0)),
            row_spec,
        ),
        out_shape=(
            jax.ShapeDtypeStruct((total, f), BF),
            jax.ShapeDtypeStruct((total, 2 * f), BF),
            jax.ShapeDtypeStruct((total, dp), BF),
        ),
        compiler_params=pltpu.CompilerParams(vmem_limit_bytes=58 * MIB),
        cost_estimate=pl.CostEstimate(
            flops=10 * total * dp * f,
            bytes_accessed=8 * total * dp + 6 * f * dp,
            transcendentals=total * f,
        ),
    )(rows_in, cot_rows, gate_up, down, dn_action)


def feed_action_kernel(x_ref, c_ref, w_ref, d_ref, dn_ref, lift_ref, gw_ref, gd_ref):
    rows, cot_rows = x_ref[...], c_ref[...]
    hidden, dgate_up = forward_back(rows, cot_rows, w_ref[...], d_ref[...])
    hidden, dgate_up = hidden.astype(BF), dgate_up.astype(BF)
    dn_ref[...] = dot_t(dgate_up, w_ref[...])
    lift_ref[...] = dot(hidden, d_ref[...])
    gw_ref[...] = t_dot(rows, dgate_up).astype(BF)
    gd_ref[...] = t_dot(hidden, cot_rows).astype(BF)


def weights_kernel(
    xo_ref, xe_ref, co_ref, ce_ref, ho_ref, he_ref, go_ref, ge_ref, act_ref, gg_ref, gu_ref,
    gd_ref,
):
    f = ho_ref.shape[1]
    kp = gd_ref.shape[2]
    both = t_dot(xo_ref[...], go_ref[...]) + t_dot(xe_ref[...], ge_ref[...])
    gg_ref[...] = both[:, :f].astype(BF)
    gu_ref[...] = both[:, f:].astype(BF)
    down = (t_dot(ho_ref[...], co_ref[...]) + t_dot(he_ref[...], ce_ref[...])).astype(BF)
    for i in range(gd_ref.shape[0]):
        gd_ref[i, :f, :] = down[:, i * kp : (i + 1) * kp]
        gd_ref[i, f:, :] = act_ref[i]


def weight_grads(x_odd, x_even, c_odd, c_even, h_odd, h_even, g_odd, g_even, action):
    total, dp = x_odd.shape
    f = h_odd.shape[1]
    n, extra, kp = action.shape
    wide = 256
    cols = pl.BlockSpec((total, wide), lambda i: (0, i))
    h_spec = pl.BlockSpec((total, f), lambda i: (0, 0))
    g_spec = pl.BlockSpec((total, 2 * f), lambda i: (0, 0))
    return pl.pallas_call(
        weights_kernel,
        grid=(dp // wide,),
        in_specs=[
            cols,
            cols,
            cols,
            cols,
            h_spec,
            h_spec,
            g_spec,
            g_spec,
            pl.BlockSpec((wide // kp, extra, kp), lambda i: (i, 0, 0)),
        ],
        out_specs=(
            pl.BlockSpec((wide, f), lambda i: (i, 0)),
            pl.BlockSpec((wide, f), lambda i: (i, 0)),
            pl.BlockSpec((wide // kp, f + extra, kp), lambda i: (i, 0, 0)),
        ),
        out_shape=(
            jax.ShapeDtypeStruct((dp, f), BF),
            jax.ShapeDtypeStruct((dp, f), BF),
            jax.ShapeDtypeStruct((n, f + extra, kp), BF),
        ),
        compiler_params=pltpu.CompilerParams(vmem_limit_bytes=48 * MIB),
        cost_estimate=pl.CostEstimate(
            flops=12 * total * dp * f, bytes_accessed=8 * total * dp, transcendentals=0
        ),
    )(x_odd, x_even, c_odd, c_even, h_odd, h_even, g_odd, g_even, action)


def lift_kernel(
    odd_ref, pa_ref, pb_ref, la_ref, lb_ref,
    oa_ref, ea_ref, ob_ref, eb_ref, aa_ref, ab_ref, d_ref, out_ref,
):
    odd = odd_ref[pl.program_id(0)] == 1
    dp = out_ref.shape[2]
    prefix = oa_ref.shape[0] - aa_ref.shape[0]
    outs = []
    for o_ref, e_ref in ((oa_ref, ea_ref), (ob_ref, eb_ref)):
        hidden = jnp.where(odd, o_ref[...].astype(F32), e_ref[...].astype(F32)).astype(BF)
        outs.append(dot(hidden, d_ref[...])[:prefix])
    action = jnp.concatenate([aa_ref[...], ab_ref[...]], axis=0)
    action = jnp.concatenate(
        [action, jnp.zeros((action.shape[0], dp - action.shape[1]), F32)], axis=1
    )
    out_ref[0] = jnp.concatenate(outs + [action], axis=0).astype(BF)


def lift(odd, place_a, place_b, lift_a, lift_b, h_odd, h_even, lifted_action, down, each, ra):
    n = odd.shape[0]
    f, dp = down.shape
    da = lifted_action.shape[1]
    a_spec = pl.BlockSpec((each, f), lambda j, o, a, b, la, lb: (a[j], 0))
    b_spec = pl.BlockSpec((each, f), lambda j, o, a, b, la, lb: (b[j], 0))
    rows = 2 * each
    return pl.pallas_call(
        lift_kernel,
        grid_spec=pltpu.PrefetchScalarGridSpec(
            num_scalar_prefetch=5,
            grid=(n,),
            in_specs=[
                a_spec,
                a_spec,
                b_spec,
                b_spec,
                pl.BlockSpec((ra // 2, da), lambda j, o, a, b, la, lb: (la[j], 0)),
                pl.BlockSpec((ra // 2, da), lambda j, o, a, b, la, lb: (lb[j], 0)),
                pl.BlockSpec((f, dp), lambda j, o, a, b, la, lb: (0, 0)),
            ],
            out_specs=pl.BlockSpec((1, rows, dp), lambda j, o, a, b, la, lb: (j, 0, 0)),
        ),
        out_shape=pltpu.HBM((n, rows, dp), BF),
        compiler_params=pltpu.CompilerParams(vmem_limit_bytes=32 * MIB),
        cost_estimate=pl.CostEstimate(
            flops=2 * n * rows * dp * f, bytes_accessed=2 * n * rows * dp, transcendentals=0
        ),
    )(odd, place_a, place_b, lift_a, lift_b, h_odd, h_even, h_odd, h_even,
      lifted_action, lifted_action, down)


def pieces_kernel(t_ref, ka_ref, ga_ref, kb_ref, gb_ref, *outs):
    tp = len(outs)
    each, dp = ka_ref.shape
    cp = dp // tp
    rp = outs[0].shape[0] * 2 * each // (2 * each)
    extra = 8
    prefix = each - extra
    ca = outs[0].shape[1] // 2
    del rp
    for k in range(tp):
        rank = t_ref[0] ^ k
        tops, ends = [], []
        for keep, got in ((ka_ref, ga_ref), (kb_ref, gb_ref)):
            wide = place(rank, cp)
            tops.append(keep[:prefix, wide].astype(F32) + got[:prefix, wide].astype(F32))
            slim = place(rank, ca)
            ends.append(
                keep[prefix:, slim].astype(F32) + got[prefix:, slim].astype(F32)
            )
        action = jnp.concatenate(ends, axis=0)
        action = jnp.concatenate(
            [action, jnp.zeros((action.shape[0], cp - ca), F32)], axis=1
        )
        outs[k][...] = jnp.concatenate(tops + [action], axis=0).astype(BF)


def middle_back_kernel(t_ref, *refs):
    tp = lax.axis_size("tp")
    ds = refs[:tp]
    mp_ref, ma_ref, gp_ref, ga_ref, cp_ref, ca_ref, w_ref = refs[tp : tp + 7]
    bp_ref, ba_ref, own_ref, lp_ref, la_ref, dm_ref, dp_scr, da_scr, rp_scr, ra_scr = refs[tp + 7 :]
    rp, dp = mp_ref.shape
    ra, da = ma_ref.shape
    cp, ca = dp // tp, da // tp
    n = w_ref.shape[0]
    kp = dp // n
    t = t_ref[0]
    for k in range(tp):
        dp_scr[:, place(t ^ k, cp)] = ds[k][:rp, :]
        da_scr[:, place(t ^ k, ca)] = ds[k][rp:, :ca]
    mixes = []
    for d_ref, m_ref, g_ref, c_ref, b_ref, r_ref, l_ref, first, last in (
        (dp_scr, mp_ref, gp_ref, cp_ref, bp_ref, rp_scr, lp_ref, 0, kp),
        (da_scr, ma_ref, ga_ref, ca_ref, ba_ref, ra_scr, la_ref, kp, w_ref.shape[2]),
    ):
        gradient = d_ref[...].astype(F32)
        rows = m_ref[...].astype(F32)
        inverse = inverse_rms(rows)
        centered = rows * inverse
        inner = gradient * g_ref[...]
        dresid = c_ref[...].astype(F32) + inverse * (
            inner - centered * jnp.mean(inner * centered, axis=1, keepdims=True)
        )
        l_ref[...] = jnp.sum(gradient * centered, axis=0, keepdims=True)
        r_ref[...] = dresid
        branch = dresid.astype(BF)
        b_ref[...] = branch
        size = last - first
        mix = jnp.zeros((rows.shape[0], dm_ref.shape[1]), F32)
        for d in range(n):
            mix = mix + dot_t(branch[:, d * size : (d + 1) * size], w_ref[d, :, first:last])
        mixes.append(mix)
    dm_ref[...] = jnp.concatenate(mixes, axis=0).astype(BF)
    own_ref[:rp, :] = rp_scr[:, place(t, cp)]
    own_ref[rp:, :] = jnp.concatenate(
        [ra_scr[:, place(t, ca)], jnp.zeros((ra, cp - ca), F32)], axis=1
    )


def out_grad_kernel(bp_ref, ba_ref, mix_ref, out_ref):
    rp, dp = bp_ref.shape
    n = out_ref.shape[0]
    kp = dp // n
    ka = ba_ref.shape[1] // n
    for d in range(n):
        out_ref[d, :, :kp] = t_dot(mix_ref[:rp, :], bp_ref[:, d * kp : (d + 1) * kp]).astype(BF)
        out_ref[d, :, kp:] = t_dot(mix_ref[rp:, :], ba_ref[:, d * ka : (d + 1) * ka]).astype(BF)


def front_back_kernel(heads_width, s_ref, t_ref, dq_ref, *refs):
    tp = lax.axis_size("tp")
    n = lax.axis_size("seq")
    (ka_ref, ra_ref, kb_ref, rb_ref, xp_ref, xa_ref, inv_ref, gp_ref, ga_ref, w_ref, lp_ref,
     la_ref, lifted_ref) = refs[:13]
    groups = refs[13:17]
    pieces = refs[17 : 17 + tp]
    gwp_scr, gwa_scr, gain_scr, dp_scr, da_scr = refs[17 + tp :]
    rp, dp = xp_ref.shape
    ra, da = xa_ref.shape
    kp, ka = dp // n, da // n
    cp, ca = dp // tp, da // tp
    width = heads_width
    dkv = jnp.concatenate(
        [
            ka_ref[...].astype(F32) + ra_ref[...].astype(F32),
            kb_ref[...].astype(F32) + rb_ref[...].astype(F32),
        ],
        axis=0,
    )
    dqkv = jnp.concatenate([dq_ref[...].astype(F32), dkv], axis=1)
    gain_scr[...] = jnp.zeros(gain_scr.shape, F32)
    dots = []
    for x_ref, g_ref, d_scr, gw_scr, l_ref, begin, end, first, last, size, at in (
        (xp_ref, gp_ref, dp_scr, gwp_scr, lp_ref, 0, rp, 0, kp, kp, 0),
        (xa_ref, ga_ref, da_scr, gwa_scr, la_ref, rp, rp + ra, kp, kp + ka, ka, 256),
    ):
        grad_rows = dqkv[begin:end].astype(BF)
        centered = x_ref[...].astype(F32) * inv_ref[begin:end, :1]
        normed = (centered * g_ref[...]).astype(BF)
        gw_scr[...] = t_dot(normed, grad_rows).astype(BF)
        weights = w_ref[:, first:last, :].reshape(x_ref.shape[1], -1)
        partial = dot_t(grad_rows, weights)
        d_scr[...] = partial
        product = partial * centered
        gains = jnp.sum(product, axis=0, keepdims=True)
        mlp_gains = l_ref[...]
        for d in range(n):
            gain_scr[d, 0:1, at : at + size] = gains[:, d * size : (d + 1) * size]
            gain_scr[d, 0:1, at + 512 : at + 512 + size] = mlp_gains[
                :, d * size : (d + 1) * size
            ]
        dots.append(jnp.sum(product * g_ref[...], axis=1, keepdims=True))
    column = jnp.concatenate(dots, axis=0)
    lanes = lax.broadcasted_iota(jnp.int32, (rp + ra, cp), 1)
    rows = lax.broadcasted_iota(jnp.int32, (rp + ra, cp), 0)
    row = jnp.sum(jnp.where(lanes == rows, column, 0.0), axis=0, keepdims=True)
    high = row.astype(BF).astype(F32)
    tail = jnp.concatenate([high, row - high, jnp.zeros((6, cp), F32)], axis=0)
    for k in range(tp):
        rank = t_ref[0] ^ k
        action = jnp.concatenate(
            [da_scr[:, place(rank, ca)], jnp.zeros((ra, cp - ca), F32)], axis=1
        )
        lifted_action = jnp.concatenate(
            [lifted_ref[rp:, place(rank, ca)].astype(F32), jnp.zeros((ra, cp - ca), F32)], axis=1
        )
        lifted = lifted_ref[:rp, place(rank, cp)].astype(F32)
        pieces[k][...] = jnp.concatenate(
            [dp_scr[:, place(rank, cp)], action, tail, lifted, lifted_action], axis=0
        ).astype(BF)
    for odd in range(2):
        for number in range(2):
            out = groups[2 * odd + number]
            for i, k in enumerate(block_order(number)):
                d = s_ref[0] ^ (k ^ odd)
                hp, ha = kp // 2, ka // 2
                out[i, :hp, :] = gwp_scr[
                    pl.ds(pl.multiple_of(d * kp + number * hp, hp), hp), :
                ]
                out[i, hp : hp + ha, :] = gwa_scr[
                    pl.ds(pl.multiple_of(d * ka + number * ha, ha), ha), :
                ]
                out[i, hp + ha :, :] = gain_scr[d].astype(BF) * BF(1 - number)


def grad_x_kernel(t_ref, *refs):
    tp = lax.axis_size("tp")
    ds = refs[:tp]
    x_ref, inv_ref, gp_ref, ga_ref, r_ref, op_ref, oa_ref = refs[tp:]
    rp, cp = op_ref.shape
    ra, ca = oa_ref.shape
    t = t_ref[0]
    total = ds[0][...].astype(F32)
    for k in range(1, tp):
        total = total + ds[k][...].astype(F32)
    row = total[rp + ra : rp + ra + 1] + total[rp + ra + 1 : rp + ra + 2]
    lanes = lax.broadcasted_iota(jnp.int32, (rp + ra, cp), 1)
    rows = lax.broadcasted_iota(jnp.int32, (rp + ra, cp), 0)
    column = jnp.sum(jnp.where(lanes == rows, row, 0.0), axis=1, keepdims=True)
    for o_ref, g_ref, begin, end, wide in (
        (op_ref, gp_ref, 0, rp, cp),
        (oa_ref, ga_ref, rp, rp + ra, ca),
    ):
        inverse = inv_ref[begin:end, :1]
        centered = x_ref[begin:end, :wide].astype(F32) * inverse
        mean = column[begin:end] / (wide * tp)
        moved = inverse * (
            total[begin:end, :wide] * g_ref[:, place(t, wide)] - centered * mean
        )
        o_ref[...] = (r_ref[begin:end, :wide] + moved).astype(BF)


def home_kernel(token_ref, g_ref, d_ref, gate_ref, down_ref, act_ref):
    del token_ref
    f = gate_ref.shape[1]
    gate_ref[...] = g_ref[0].astype(F32)
    down_ref[...] = d_ref[0, :f, :].astype(F32)
    act_ref[0] = d_ref[0, f:, :].astype(F32)


def home(token, got_gate, got_down):
    n, kp, f = got_gate.shape
    tall = got_down.shape[1]
    return pl.pallas_call(
        home_kernel,
        grid=(n,),
        in_specs=[
            pl.BlockSpec(memory_space=pltpu.SMEM),
            pl.BlockSpec((1, kp, f), lambda j: (j, 0, 0)),
            pl.BlockSpec((1, tall, kp), lambda j: (j, 0, 0)),
        ],
        out_specs=(
            pl.BlockSpec((kp, f), lambda j: (0, j)),
            pl.BlockSpec((f, kp), lambda j: (j, 0)),
            pl.BlockSpec((1, tall - f, kp), lambda j: (j, 0, 0)),
        ),
        out_shape=(
            jax.ShapeDtypeStruct((kp, n * f), F32),
            jax.ShapeDtypeStruct((n * f, kp), F32),
            jax.ShapeDtypeStruct((n, tall - f, kp), F32),
        ),
        cost_estimate=pl.CostEstimate(
            flops=0, bytes_accessed=6 * n * kp * (f + tall), transcendentals=0
        ),
    )(token, got_gate, got_down)


def home_up_kernel(u_ref, up_ref):
    up_ref[...] = u_ref[0].astype(F32)


def home_up(got):
    n, kp, f = got.shape
    return pl.pallas_call(
        home_up_kernel,
        grid=(n,),
        in_specs=[pl.BlockSpec((1, kp, f), lambda j: (j, 0, 0))],
        out_specs=pl.BlockSpec((kp, f), lambda j: (0, j)),
        out_shape=jax.ShapeDtypeStruct((kp, n * f), F32),
        cost_estimate=pl.CostEstimate(
            flops=0, bytes_accessed=6 * n * kp * f, transcendentals=0
        ),
    )(got)


def shards(
    x_prefix,
    x_action,
    prefix_segment,
    prefix_attn_gain,
    prefix_query,
    prefix_key,
    prefix_value,
    prefix_out,
    prefix_mlp_gain,
    prefix_gate,
    prefix_up,
    prefix_down,
    action_attn_gain,
    action_query,
    action_key,
    action_value,
    action_out,
    action_mlp_gain,
    action_gate,
    action_up,
    action_down,
    cot_prefix,
    cot_action,
):
    n = lax.axis_size("seq")
    tp = lax.axis_size("tp")
    s = lax.axis_index("seq")
    t = lax.axis_index("tp")
    rank_t = t.astype(jnp.int32).reshape(1)
    rank_s = s.astype(jnp.int32).reshape(1)
    rp, cp = x_prefix.shape
    ra, ca = x_action.shape
    rows = rp + ra
    half = rows // 2
    dp, da = cp * tp, ca * tp
    kp, ka = dp // n, da // n
    width = prefix_query.shape[1]
    qkv_width = width + 2 * HD
    fp, fa = prefix_gate.shape[1] // n, action_gate.shape[1] // n

    x_pack = jnp.concatenate(
        [x_prefix, jnp.pad(x_action, ((0, 0), (0, cp - ca)))], axis=0
    )
    x_pieces = gather_tp(x_pack)
    gains = jnp.concatenate(
        [prefix_attn_gain, prefix_mlp_gain, action_attn_gain, action_mlp_gain]
    )
    gain_rows = -(-gains.shape[0] // qkv_width)
    gains = jnp.pad(gains, (0, 8 * qkv_width - gains.shape[0])).reshape(8, qkv_width)
    pack_qkv = jnp.concatenate(
        [
            jnp.concatenate([prefix_query, prefix_key, prefix_value], axis=1),
            jnp.concatenate([action_query, action_key, action_value], axis=1),
            gains,
        ],
        axis=0,
    )
    got_qkv = lax.all_gather(pack_qkv, "seq", axis=0)
    got_gains = got_qkv[:, kp + ka : kp + ka + gain_rows].reshape(n, -1).astype(F32)
    attn_gain_p = got_gains[:, :kp].reshape(1, dp)
    mlp_gain_p = got_gains[:, kp : 2 * kp].reshape(1, dp)
    attn_gain_a = got_gains[:, 2 * kp : 2 * kp + ka].reshape(1, da)
    mlp_gain_a = got_gains[:, 2 * kp + ka : 2 * kp + 2 * ka].reshape(1, da)
    pack_out = jnp.concatenate([prefix_out, action_out], axis=1)
    cot_wide = jnp.pad(cot_action, ((0, 0), (0, dp - da)))
    cot_stages, cot_last = gather_stacked(
        [
            jnp.concatenate(
                [
                    cot_prefix[i * (rp // 2) : (i + 1) * (rp // 2)],
                    cot_wide[i * (ra // 2) : (i + 1) * (ra // 2)],
                ],
                axis=0,
            )
            for i in range(2)
        ]
    )
    cot_odd, cot_even = near_rows(cot_stages[-1])

    def by_units(w, f):
        return w.reshape(w.shape[0], n, f).transpose(1, 0, 2)

    gate_up_sent = jnp.concatenate([by_units(prefix_gate, fp), by_units(prefix_up, fp)], axis=2)
    action_sent = jnp.concatenate(
        [
            by_units(action_gate, fa),
            by_units(action_up, fa),
            action_down.reshape(n, fa, ka).transpose(0, 2, 1),
        ],
        axis=2,
    ).reshape(n, -1, kp)
    extra = action_sent.shape[1]
    down_sent = jnp.concatenate([prefix_down.reshape(n, fp, kp), action_sent], axis=1)

    queries, kv_a, kv_b, x_full_p, x_full_a, inverse1 = whole_call(
        front_kernel,
        (
            ((rows, width), BF),
            ((half, 2 * HD), BF),
            ((half, 2 * HD), BF),
            ((rp, dp), BF),
            ((ra, da), BF),
            ((rows, 128), F32),
        ),
        [after(rank_t, *cot_last), *x_pieces, got_qkv, attn_gain_p, attn_gain_a],
        2 * rp * dp * qkv_width,
    )
    kv_even = [jnp.concatenate(blocks, axis=0) for blocks in gather_far([kv_a, kv_b])]
    kv_odd = [swap(e, "seq", 1) for e in kv_even]
    keys_values = jnp.concatenate([kv_even[0], kv_odd[0], kv_even[1], kv_odd[1]], axis=0)
    codes = token_codes(prefix_segment, n, ra)
    query_code = lax.dynamic_slice_in_dim(codes, s, 1, 0).reshape(rows, 1)
    key_code = jnp.concatenate(
        [
            lax.dynamic_slice(codes, (s ^ k ^ odd, number * half), (1, half))
            for number in range(2)
            for odd in range(2)
            for k in block_order(number)
        ],
        axis=1,
    )
    attended, mixed, log_sum = whole_call(
        attend_kernel,
        (
            ((rows, width), F32),
            ((rows, width), BF),
            ((rows, width // HD * 128), F32),
        ),
        [queries, keys_values, query_code, key_code],
        4 * rows * width * n * rows,
        transcendentals=rows * width // HD * n * rows,
    )
    got_out = lax.all_gather(after(pack_out, queries), "seq", axis=0)
    down_got = lax.all_to_all(after(down_sent, keys_values), "seq", 0, 0)

    piece = (((rows, cp), BF),)
    branch = sum_tp(
        whole_call(
            branch_kernel, piece * tp, [rank_t, mixed, got_out], 2 * rows * dp * width
        )
    )
    residual = x_pack.astype(F32) + branch
    mid_own = after(residual.astype(BF), down_got)
    gate_up = lax.all_to_all(after(gate_up_sent, branch), "seq", 0, 0).reshape(dp, 2 * fp)
    down = down_got[:, :fp].transpose(1, 0, 2).reshape(fp, dp)
    action_got = down_got[:, fp:].reshape(da, 3 * fa)
    gate_up_action = action_got[:, : 2 * fa]
    down_action = action_got[:, 2 * fa :].T


    def action_rows(blocks):
        return blocks.reshape(n, half, dp)[:, rp // 2 :, :da].reshape(-1, da)

    cot_action_all = jnp.concatenate([action_rows(cot_odd), action_rows(cot_even)], axis=0)
    block = (((half, dp), BF),)
    mid_p, mid_a, normed_a, normed_b = whole_call(
        middle_kernel,
        (((rp, dp), BF), ((ra, da), BF)) + block * 2,
        [after(rank_t, gate_up, down, gate_up_action, down_action, cot_action_all), *gather_tp(mid_own), mlp_gain_p, mlp_gain_a],
        rp * dp,
    )

    normed_odd, normed_even = near_rows(
        [b for blocks in gather_far([normed_a, normed_b]) for b in blocks]
    )
    normed_action = jnp.concatenate([action_rows(normed_odd), action_rows(normed_even)], axis=0)
    tokens = n * ra
    dn_action, lifted_action, grad_gu_action, grad_down_action = whole_call(
        feed_action_kernel,
        (
            ((tokens, da), F32),
            ((tokens, da), F32),
            ((da, 2 * fa), BF),
            ((fa, da), BF),
        ),
        [normed_action, cot_action_all, gate_up_action, down_action],
        18 * tokens * da * fa,
    )
    h_odd, g_odd, dn_odd = feed(
        normed_odd, cot_odd, gate_up, down, dn_action[: tokens // 2], half
    )
    h_even, g_even, dn_even = feed(
        normed_even, cot_even, gate_up, down, dn_action[tokens // 2 :], half
    )
    dn_blocks = [
        d.reshape(2, n // 2, half, dp) for d in (dn_even, swap(dn_odd, "seq", 1))
    ]

    grad_gu_action, grad_down_action = after((grad_gu_action, grad_down_action), dn_even)
    action_grads = jnp.concatenate(
        [
            grad_gu_action.reshape(n, ka, 2 * fa),
            grad_down_action.reshape(fa, n, ka).transpose(1, 2, 0),
        ],
        axis=2,
    ).reshape(n, extra, kp)
    grad_gate, grad_up, grad_down = weight_grads(
        normed_odd, normed_even, cot_odd, cot_even, h_odd, h_even, g_odd, g_even, action_grads
    )
    ranks = s ^ jnp.arange(n, dtype=jnp.int32)
    odd_bits = ranks & 1
    places = []
    for number in range(2):
        table = [0] * n
        for i, k in enumerate(block_order(number)):
            table[k] = table[k ^ 1] = number * (n // 2) + i
        places.append(jnp.array(table, jnp.int32)[ranks])
    lift_places = [p + (1 - odd_bits) * n for p in places]
    lifted = lift(
        odd_bits, *places, *lift_places, h_odd, h_even, lifted_action, down, half, ra
    )
    ((keep_a, got_a), (keep_b, got_b)), *_ = scatter_rows(
        [(dn_blocks[0][i], dn_blocks[1][i]) for i in range(2)], grad_gate
    )
    sent_pieces = whole_call(
        pieces_kernel,
        piece * tp,
        [after(rank_t, lifted), keep_a, got_a, keep_b, got_b],
        rp * dp,
    )
    dn_own = sum_tp(sent_pieces)
    dn_pieces = gather_tp(dn_own.astype(BF))
    lifted_home = lax.psum_scatter(after(lifted, got_a, got_b), "seq", scatter_dimension=0)
    grad_down_home = lax.all_to_all(after(grad_down, sent_pieces[0]), "seq", 0, 0)

    grad_gate_home = lax.all_to_all(
        after(grad_gate, grad_down_home).reshape(n, kp, fp), "seq", 0, 0
    )

    row = ((1, dp), F32)
    row_a = ((1, da), F32)
    dbranch_p, dbranch_a, dresid, mlp_gains_p, mlp_gains_a, dmixed = whole_call(
        middle_back_kernel,
        (((rp, dp), BF), ((ra, da), BF), ((rows, cp), F32), row, row_a, ((rows, width), BF)),
        [after(rank_t, grad_down_home), *dn_pieces, mid_p, mid_a, mlp_gain_p, mlp_gain_a, cot_prefix, cot_action, got_out],
        2 * rows * dp * width,
        scratch=(
            pltpu.VMEM((rp, dp), BF),
            pltpu.VMEM((ra, da), BF),
            pltpu.VMEM((rp, dp), F32),
            pltpu.VMEM((ra, da), F32),
        ),
    )
    dquery, *dkv_parts = whole_call(
        attend_back_kernel,
        (((rows, width), BF),) + (((n * rows // 4, 2 * HD), BF),) * 4,
        [queries, keys_values, query_code, key_code, attended, log_sum, dmixed],
        10 * rows * width * n * rows,
        limit=56,
        transcendentals=rows * width // HD * n * rows,
    )
    dkv_halves = [
        [d.reshape(n // 2, half, 2 * HD) for d in (e, swap(o, "seq", 1))]
        for e, o in ((dkv_parts[0], dkv_parts[1]), (dkv_parts[2], dkv_parts[3]))
    ]
    dkv = [part for pair in scatter_rows(dkv_halves, grad_gate_home)[0] for part in pair]
    (out_grads,) = whole_call(
        out_grad_kernel,
        (((n, width, kp + ka), BF),),
        [dbranch_p, dbranch_a, after(mixed, dquery)],
        2 * rows * dp * width,
    )
    out_home = lax.psum_scatter(out_grads, "seq", scatter_dimension=0)
    tall = (kp + ka) // 2 + 8
    *groups_and_pieces, = whole_call(
        lambda *refs: front_back_kernel(width, *refs),
        (((n // 2, tall, qkv_width), BF),) * 4 + (((2 * rows + 8, cp), BF),) * tp,
        [
            rank_s, rank_t, dquery, *dkv, x_full_p, x_full_a, inverse1, attn_gain_p, attn_gain_a,
            got_qkv, mlp_gains_p, mlp_gains_a, lifted_home,
        ],
        4 * rows * dp * qkv_width,
        scratch=(
            pltpu.VMEM((dp, qkv_width), BF),
            pltpu.VMEM((da, qkv_width), BF),
            pltpu.VMEM((n, 8, qkv_width), F32),
            pltpu.VMEM((rp, dp), F32),
            pltpu.VMEM((ra, da), F32),
        ),
    )
    groups, pieces = groups_and_pieces[:4], groups_and_pieces[4:]
    tree, history, (tp_parts, _) = scatter_rows(
        [(e, swap(o, "seq", 1)) for e, o in ((groups[0], groups[2]), (groups[1], groups[3]))],
        None,
        (trade_tp(pieces), ()),
    )
    lifted_parts = [part[rows + 8 :] for part in tp_parts]
    grad_up_home = lax.all_to_all(
        after(grad_up, grad_gate_home, groups[0]).reshape(n, kp, fp), "seq", 0, 0
    )
    qkv_a, qkv_b = [add(keep, got) for keep, got in tree]
    output = (residual + total_of(lifted_parts)).astype(BF)
    grad_x_p, grad_x_a = whole_call(
        grad_x_kernel,
        (((rp, cp), BF), ((ra, ca), BF)),
        [
            after(rank_t, history[-1]), *tp_parts, x_pack,
            inverse1, attn_gain_p, attn_gain_a, dresid,
        ],
        rp * dp,
    )
    hp, ha = kp // 2, ka // 2
    qkv_home_p = jnp.concatenate([qkv_a[:hp], qkv_b[:hp]], axis=0)
    qkv_home_a = jnp.concatenate([qkv_a[hp : hp + ha], qkv_b[hp : hp + ha]], axis=0)
    gains_home = qkv_a[hp + ha :]
    qp, qa = kp // tp, ka // tp

    attn_gains = jnp.pad(gains_home[:1, :512], ((0, 7), (0, 0)))

    def shared_piece(rank):
        return jnp.concatenate(
            [
                lax.dynamic_slice_in_dim(qkv_home_p[:, width:], rank * qp, qp, 0),
                lax.dynamic_slice_in_dim(qkv_home_a[:, width:], rank * qa, qa, 0),
                attn_gains,
            ],
            axis=0,
        )

    shared_home = sum_tp([shared_piece(t ^ k) for k in range(tp)])
    attn_gains_home = shared_home[qp + qa]
    out_home = after(out_home, *history[-1]).astype(F32)
    grad_gate_p, grad_down_p, action_home = home(
        after(rank_t, history[0]), grad_gate_home, grad_down_home
    )
    grad_up_p = home_up(grad_up_home)
    action_home = action_home.reshape(n, ka, 3 * fa)

    def units(part):
        return part.transpose(1, 0, 2).reshape(ka, n * fa)

    grad_gate_a = units(action_home[:, :, :fa])
    grad_up_a = units(action_home[:, :, fa : 2 * fa])
    grad_down_a = action_home[:, :, 2 * fa :].transpose(0, 2, 1).reshape(n * fa, ka)
    return (
        output[:rp],
        output[rp:, :ca],
        grad_x_p,
        grad_x_a,
        attn_gains_home[:kp],
        qkv_home_p[:, :width],
        shared_home[:qp, :HD],
        shared_home[:qp, HD:],
        out_home[:, :kp],
        gains_home[0, 512 : 512 + kp],
        grad_gate_p,
        grad_up_p,
        grad_down_p,
        attn_gains_home[256 : 256 + ka],
        qkv_home_a[:, :width],
        shared_home[qp : qp + qa, :HD],
        shared_home[qp : qp + qa, HD:],
        out_home[:, kp:],
        gains_home[0, 768 : 768 + ka],
        grad_gate_a,
        grad_up_a,
        grad_down_a,
    )


def solution(mesh):
    split = P("seq", "tp")
    turned = P("tp", "seq")
    both = P(("seq", "tp"), None)
    one = P("seq")
    rows = P("seq", None)
    stream_in = (one, split, rows, rows, turned, one, split, split, turned)
    stream_out = (one, split, both, both, turned, one, split, split, turned)
    return jax.shard_map(
        shards,
        mesh=mesh,
        in_specs=(split, split, P()) + stream_in + stream_in + (rows, rows),
        out_specs=(split, split, split, split) + stream_out + stream_out,
        check_vma=False,
    )
```

```python
import jax
import jax.numpy as jnp
from jax import lax
from jax.experimental import pallas as pl
from jax.experimental.pallas import tpu as pltpu
from jax.sharding import PartitionSpec as P

HD = 256
IMG = 768
TXT = 48
ACT = 50
EPS = 1e-06
NEG = -1e30
BF = jnp.bfloat16
F32 = jnp.float32
MIB = 1 << 20


def swap(value, axis, mask):
    count = lax.axis_size(axis)
    return lax.ppermute(value, axis, [(i, i ^ mask) for i in range(count)])


def after(values, *tokens):
    return lax.optimization_barrier((values, tokens))[0]


def far_masks():
    count = lax.axis_size("seq")
    masks = [1 << b for b in range(1, count.bit_length() - 1)]
    return masks, masks[::-1]


def block_order(number):
    order = [0]
    for mask in far_masks()[number]:
        order = order + [k ^ mask for k in order]
    return order


def gather_far(halves):
    results = []
    for half, masks in zip(halves, far_masks()):
        blocks = [half]
        for mask in masks:
            blocks = blocks + [swap(b, "seq", mask) for b in blocks]
        results.append(blocks)
    return results


def gather_stacked(halves):
    stages = [list(halves)]
    for step in range(len(far_masks()[0])):
        got = [swap(b, "seq", masks[step]) for b, masks in zip(stages[-1], far_masks())]
        got = lax.optimization_barrier(got)
        stages.append([jnp.concatenate(pair, axis=0) for pair in zip(stages[-1], got)])
    return stages[1:], got


def near_rows(blocks):
    even = jnp.concatenate(blocks, axis=0)
    return swap(even, "seq", 1), even


def add(left, right):
    return left.astype(F32) + right.astype(F32)


def scatter_rows(halves, token=None, beside=((), ())):
    parts = [list(half) for half in halves]
    orders = [masks[::-1] for masks in far_masks()]
    steps = len(orders[0])
    history = []
    beside = list(beside)
    for step in range(steps):
        keep = parts[0][0].shape[0] // 2
        sent = [total_of([p[keep:] for p in part]).astype(BF) for part in parts]
        if token is not None and step == steps - 1:
            sent = after(sent, token)
        got = [swap(part, "seq", order[step]) for part, order in zip(sent, orders)]
        for place, when in enumerate((0, steps - 1)):
            if step == when and beside[place]:
                got, beside[place] = lax.optimization_barrier((got, beside[place]))
        parts = [[p[:keep] for p in part] + [g] for part, g in zip(parts, got)]
        history.append(sent)
    return [(total_of([p[0] for p in part[:-1]]), part[-1][0]) for part in parts], history, beside


def gather_tp(piece):
    return [piece] + [swap(piece, "tp", k) for k in range(1, lax.axis_size("tp"))]


def trade_tp(pieces):
    return [pieces[0]] + [swap(pieces[k].astype(BF), "tp", k) for k in range(1, len(pieces))]


def total_of(addends):
    total = addends[0].astype(F32)
    for part in addends[1:]:
        total = total + part.astype(F32)
    return total


def sum_tp(pieces):
    return total_of(trade_tp(pieces))


def dot(left, right):
    return jnp.dot(left, right, preferred_element_type=F32)


def dot_t(left, right):
    return lax.dot_general(left, right, (((1,), (1,)), ((), ())), preferred_element_type=F32)


def t_dot(left, right):
    return lax.dot_general(left, right, (((0,), (0,)), ((), ())), preferred_element_type=F32)


def whole_call(kernel, outs, args, flops, scratch=(), limit=48, transcendentals=0):
    specs = [
        pl.BlockSpec(memory_space=pltpu.SMEM if a.ndim == 1 else pltpu.VMEM) for a in args
    ]
    outs = tuple(jax.ShapeDtypeStruct(shape, dtype) for shape, dtype in outs)
    moved = sum(a.size * a.dtype.itemsize for a in args)
    moved += sum(o.size * o.dtype.itemsize for o in outs)
    return pl.pallas_call(
        kernel,
        out_shape=outs,
        in_specs=specs,
        out_specs=tuple(pl.BlockSpec(memory_space=pltpu.VMEM) for _ in outs),
        scratch_shapes=list(scratch),
        compiler_params=pltpu.CompilerParams(vmem_limit_bytes=limit * MIB),
        cost_estimate=pl.CostEstimate(
            flops=int(flops), bytes_accessed=int(moved), transcendentals=int(transcendentals)
        ),
    )(*args)


def inverse_rms(values):
    return lax.rsqrt(jnp.mean(values * values, axis=1, keepdims=True) + EPS)


def place(rank, width):
    return pl.ds(pl.multiple_of(rank * width, width), width)


def token_codes(prefix_segment, seq_count, suf_rows):
    items_all = prefix_segment.shape[0] // (IMG + TXT)
    places = jnp.arange(seq_count * suf_rows, dtype=jnp.int32)
    items_of = places // (ACT + 1)
    suffix_seg = jnp.where(items_of < items_all, items_of, items_all)
    suffix_lvl = jnp.where((items_of < items_all) & (places % (ACT + 1) == 0), 1, 2)
    suffix = (suffix_seg * 4 + suffix_lvl).astype(jnp.int32)
    return jnp.concatenate(
        [(prefix_segment * 4).reshape(seq_count, -1), suffix.reshape(seq_count, -1)], axis=1
    )


def front_kernel(t_ref, *refs):
    tp = lax.axis_size("tp")
    xs = refs[:tp]
    w_ref, gp_ref, ga_ref, q_ref, kva_ref, kvb_ref, xp_ref, xa_ref, inv_ref = refs[tp:]
    rp, dp = xp_ref.shape
    ra, da = xa_ref.shape
    cp, ca = dp // tp, da // tp
    kp, ka = dp // w_ref.shape[0], da // w_ref.shape[0]
    width = q_ref.shape[1]
    half = kva_ref.shape[0]
    for k in range(tp):
        xp_ref[:, place(t_ref[0] ^ k, cp)] = xs[k][:rp, :]
        xa_ref[:, place(t_ref[0] ^ k, ca)] = xs[k][rp:, :ca]
    parts = []
    inverses = []
    for x_ref, g_ref, first, last, size in (
        (xp_ref, gp_ref, 0, kp, dp),
        (xa_ref, ga_ref, kp, kp + ka, da),
    ):
        rows = x_ref[...].astype(F32)
        inverse = inverse_rms(rows)
        normed = (rows * inverse * g_ref[...]).astype(BF)
        parts.append(dot(normed, w_ref[:, first:last, :].reshape(size, -1)))
        inverses.append(inverse)
    qkv = jnp.concatenate(parts, axis=0)
    q_ref[...] = qkv[:, :width].astype(BF)
    kva_ref[...] = qkv[:half, width:].astype(BF)
    kvb_ref[...] = qkv[half:, width:].astype(BF)
    inv_ref[...] = jnp.broadcast_to(jnp.concatenate(inverses, axis=0), inv_ref.shape)


def key_step(count):
    for step in (2176, 1088, 544, 272):
        if count % step == 0:
            return step
    return count


def attend_kernel(q_ref, kv_ref, qc_ref, kc_ref, att_ref, mix_ref, lse_ref):
    rows = q_ref.shape[0]
    heads = q_ref.shape[1] // HD
    count = kv_ref.shape[0]
    step = key_step(count)
    code = qc_ref[...]
    low = code - code % 4
    for h in range(heads):
        query = q_ref[:, h * HD : (h + 1) * HD] * BF(HD**-0.5)
        top = jnp.full((rows, 1), NEG, F32)
        mass = jnp.zeros((rows, 1), F32)
        total = jnp.zeros((rows, HD), F32)
        for begin in range(0, count, step):
            keys = kv_ref[begin : begin + step, :HD]
            marks = kc_ref[:, begin : begin + step]
            allowed = (marks >= low) & (marks <= code)
            scores = jnp.where(allowed, dot_t(query, keys), NEG)
            new_top = jnp.maximum(top, jnp.max(scores, axis=1, keepdims=True))
            expo = jnp.where(allowed, jnp.exp(scores - new_top), 0.0)
            shrink = jnp.exp(top - new_top)
            mass = mass * shrink + jnp.sum(expo, axis=1, keepdims=True)
            total = total * shrink + dot(expo.astype(BF), kv_ref[begin : begin + step, HD:])
            top = new_top
        attended = total / mass
        att_ref[:, h * HD : (h + 1) * HD] = attended
        mix_ref[:, h * HD : (h + 1) * HD] = attended.astype(BF)
        lse_ref[:, h * 128 : (h + 1) * 128] = jnp.broadcast_to(top + jnp.log(mass), (rows, 128))


def attend_back_kernel(
    q_ref, kv_ref, qc_ref, kc_ref, att_ref, lse_ref, dm_ref, dq_ref, *dkv_refs
):
    rows = q_ref.shape[0]
    heads = q_ref.shape[1] // HD
    count = kv_ref.shape[0]
    step = key_step(count)
    each = dkv_refs[0].shape[0]
    code = qc_ref[...]
    low = code - code % 4
    dq = [jnp.zeros((rows, HD), F32) for _ in range(heads)]
    for begin in range(0, count, step):
        keys = kv_ref[begin : begin + step, :HD]
        vals = kv_ref[begin : begin + step, HD:]
        marks = kc_ref[:, begin : begin + step]
        allowed = (marks >= low) & (marks <= code)
        dk = jnp.zeros((step, HD), F32)
        dv = jnp.zeros((step, HD), F32)
        for h in range(heads):
            span = slice(h * HD, (h + 1) * HD)
            query = q_ref[:, span] * BF(HD**-0.5)
            dmix = dm_ref[:, span]
            delta = jnp.sum(dmix.astype(F32) * att_ref[:, span], axis=1, keepdims=True)
            scores = dot_t(query, keys)
            probs = jnp.where(allowed, jnp.exp(scores - lse_ref[:, h * 128 : h * 128 + 1]), 0.0)
            dscores = (probs * (dot_t(dmix, vals) - delta)).astype(BF)
            dq[h] = dq[h] + dot(dscores, keys)
            dk = dk + t_dot(dscores, query)
            dv = dv + t_dot(probs.astype(BF), dmix)
        dkv = jnp.concatenate([dk, dv], axis=1).astype(BF)
        for part in range(len(dkv_refs)):
            first, last = max(begin, part * each), min(begin + step, (part + 1) * each)
            if first < last:
                dkv_refs[part][first - part * each : last - part * each, :] = dkv[
                    first - begin : last - begin
                ]
    for h in range(heads):
        dq_ref[:, h * HD : (h + 1) * HD] = (dq[h] * HD**-0.5).astype(BF)


def branch_kernel(t_ref, mix_ref, w_ref, *outs):
    tp = len(outs)
    n = w_ref.shape[0]
    cp = outs[0].shape[1]
    ra = mix_ref.shape[0] - (outs[0].shape[0] - 16)
    rp = mix_ref.shape[0] - ra
    kp = cp * tp // n
    for k in range(tp):
        rank = t_ref[0] ^ k
        prefix, action = [], []
        for i in range(n // tp):
            block = w_ref[rank * (n // tp) + i]
            prefix.append(dot(mix_ref[:rp, :], block[:, :kp]))
            action.append(dot(mix_ref[rp:, :], block[:, kp:]))
        action = jnp.concatenate(action, axis=1)
        outs[k][:rp, :] = jnp.concatenate(prefix, axis=1).astype(BF)
        outs[k][rp:, :] = jnp.concatenate(
            [action, jnp.zeros((ra, cp - action.shape[1]), F32)], axis=1
        ).astype(BF)


def middle_kernel(t_ref, *refs):
    tp = lax.axis_size("tp")
    mids = refs[:tp]
    gp_ref, ga_ref, mp_ref, ma_ref, a_ref, b_ref = refs[tp:]
    rp, dp = mp_ref.shape
    ra, da = ma_ref.shape
    cp, ca = dp // tp, da // tp
    for k in range(tp):
        mp_ref[:, place(t_ref[0] ^ k, cp)] = mids[k][:rp, :]
        ma_ref[:, place(t_ref[0] ^ k, ca)] = mids[k][rp:, :ca]
    rows = mp_ref[...].astype(F32)
    prefix = rows * inverse_rms(rows) * gp_ref[...]
    rows = ma_ref[...].astype(F32)
    action = rows * inverse_rms(rows) * ga_ref[...]
    action = jnp.concatenate([action, jnp.zeros((ra, dp - da), F32)], axis=1)
    for number, out in enumerate((a_ref, b_ref)):
        out[...] = jnp.concatenate(
            [
                prefix[number * (rp // 2) : (number + 1) * (rp // 2)],
                action[number * (ra // 2) : (number + 1) * (ra // 2)],
            ],
            axis=0,
        ).astype(BF)


def gelu_parts(value):
    scale = 0.7978845608028654
    square = value * value
    bent = jnp.tanh(scale * (value + 0.044715 * value * square))
    gelu = 0.5 * value * (1.0 + bent)
    slope = 0.5 * (1.0 + bent) + 0.5 * value * (1.0 - bent * bent) * scale * (
        1.0 + 3.0 * 0.044715 * square
    )
    return gelu, slope


def forward_back(rows, cot_rows, gate_up, down):
    f = down.shape[0]
    both = dot(rows, gate_up)
    gelu, slope = gelu_parts(both[:, :f])
    up = both[:, f:]
    dhidden = dot_t(cot_rows, down)
    return gelu * up, jnp.concatenate([dhidden * up * slope, dhidden * gelu], axis=1)


def feed_kernel(pair, x_ref, c_ref, w_ref, d_ref, act_ref, h_ref, g_ref, dn_ref):
    rows, dp = x_ref.shape
    each = rows // pair
    prefix = each - act_ref.shape[0] // pair
    hidden, dgate_up = forward_back(x_ref[...], c_ref[...], w_ref[...], d_ref[...])
    inside = lax.broadcasted_iota(jnp.int32, (rows, 1), 0) % each < prefix
    dgate_up = jnp.where(inside, dgate_up, 0.0).astype(BF)
    h_ref[...] = jnp.where(inside, hidden, 0.0).astype(BF)
    g_ref[...] = dgate_up
    dn = dot_t(dgate_up, w_ref[...])
    action = act_ref[...]
    action = jnp.concatenate(
        [action, jnp.zeros((action.shape[0], dp - action.shape[1]), F32)], axis=1
    )
    begin = 0
    for i in range(pair):
        first, last = i * each + prefix, (i + 1) * each
        low, high = first // 16 * 16, -(-last // 16) * 16
        dn_ref[begin:low, :] = dn[begin:low].astype(BF)
        piece = [dn[low:first], action[i * (each - prefix) : (i + 1) * (each - prefix)]]
        piece = [p for p in piece + [dn[last:high]] if p.shape[0]]
        dn_ref[low:high, :] = jnp.concatenate(piece, axis=0).astype(BF)
        begin = high


def feed(rows_in, cot_rows, gate_up, down, dn_action, each):
    total, dp = rows_in.shape
    pair = 2
    step = pair * each
    f = down.shape[0]
    act_step = dn_action.shape[0] * step // total
    row_spec = pl.BlockSpec((step, dp), lambda i: (i, 0))
    in_specs = [
        row_spec,
        row_spec,
        pl.BlockSpec(gate_up.shape, lambda i: (0, 0)),
        pl.BlockSpec(down.shape, lambda i: (0, 0)),
        pl.BlockSpec((act_step, dn_action.shape[1]), lambda i: (i, 0)),
    ]
    return pl.pallas_call(
        lambda *refs: feed_kernel(pair, *refs),
        grid=(total // step,),
        in_specs=in_specs,
        out_specs=(
            pl.BlockSpec((step, f), lambda i: (i, 0)),
            pl.BlockSpec((step, 2 * f), lambda i: (i, 0)),
            row_spec,
        ),
        out_shape=(
            jax.ShapeDtypeStruct((total, f), BF),
            jax.ShapeDtypeStruct((total, 2 * f), BF),
            jax.ShapeDtypeStruct((total, dp), BF),
        ),
        compiler_params=pltpu.CompilerParams(vmem_limit_bytes=36 * MIB),
        cost_estimate=pl.CostEstimate(
            flops=10 * total * dp * f,
            bytes_accessed=8 * total * dp + 6 * f * dp,
            transcendentals=total * f,
        ),
    )(rows_in, cot_rows, gate_up, down, dn_action)


def feed_action_kernel(x_ref, c_ref, w_ref, d_ref, dn_ref, lift_ref, gw_ref, gd_ref):
    rows, cot_rows = x_ref[...], c_ref[...]
    hidden, dgate_up = forward_back(rows, cot_rows, w_ref[...], d_ref[...])
    hidden, dgate_up = hidden.astype(BF), dgate_up.astype(BF)
    dn_ref[...] = dot_t(dgate_up, w_ref[...])
    lift_ref[...] = dot(hidden, d_ref[...])
    gw_ref[...] = t_dot(rows, dgate_up).astype(BF)
    gd_ref[...] = t_dot(hidden, cot_rows).astype(BF)


def weights_kernel(
    xo_ref, xe_ref, co_ref, ce_ref, ho_ref, he_ref, go_ref, ge_ref, act_ref, gg_ref, gu_ref,
    gd_ref,
):
    f = ho_ref.shape[1]
    kp = gd_ref.shape[2]
    both = t_dot(xo_ref[...], go_ref[...]) + t_dot(xe_ref[...], ge_ref[...])
    gg_ref[...] = both[:, :f].astype(BF)
    gu_ref[...] = both[:, f:].astype(BF)
    down = (t_dot(ho_ref[...], co_ref[...]) + t_dot(he_ref[...], ce_ref[...])).astype(BF)
    for i in range(gd_ref.shape[0]):
        gd_ref[i, :f, :] = down[:, i * kp : (i + 1) * kp]
        gd_ref[i, f:, :] = act_ref[i]


def weight_grads(x_odd, x_even, c_odd, c_even, h_odd, h_even, g_odd, g_even, action):
    total, dp = x_odd.shape
    f = h_odd.shape[1]
    n, extra, kp = action.shape
    wide = 256
    cols = pl.BlockSpec((total, wide), lambda i: (0, i))
    h_spec = pl.BlockSpec((total, f), lambda i: (0, 0))
    g_spec = pl.BlockSpec((total, 2 * f), lambda i: (0, 0))
    return pl.pallas_call(
        weights_kernel,
        grid=(dp // wide,),
        in_specs=[
            cols,
            cols,
            cols,
            cols,
            h_spec,
            h_spec,
            g_spec,
            g_spec,
            pl.BlockSpec((wide // kp, extra, kp), lambda i: (i, 0, 0)),
        ],
        out_specs=(
            pl.BlockSpec((wide, f), lambda i: (i, 0)),
            pl.BlockSpec((wide, f), lambda i: (i, 0)),
            pl.BlockSpec((wide // kp, f + extra, kp), lambda i: (i, 0, 0)),
        ),
        out_shape=(
            jax.ShapeDtypeStruct((dp, f), BF),
            jax.ShapeDtypeStruct((dp, f), BF),
            jax.ShapeDtypeStruct((n, f + extra, kp), BF),
        ),
        compiler_params=pltpu.CompilerParams(vmem_limit_bytes=48 * MIB),
        cost_estimate=pl.CostEstimate(
            flops=12 * total * dp * f, bytes_accessed=8 * total * dp, transcendentals=0
        ),
    )(x_odd, x_even, c_odd, c_even, h_odd, h_even, g_odd, g_even, action)


def lift_kernel(
    odd_ref, pa_ref, pb_ref, la_ref, lb_ref,
    oa_ref, ea_ref, ob_ref, eb_ref, aa_ref, ab_ref, d_ref, out_ref,
):
    odd = odd_ref[pl.program_id(0)] == 1
    dp = out_ref.shape[2]
    prefix = oa_ref.shape[0] - aa_ref.shape[0]
    outs = []
    for o_ref, e_ref in ((oa_ref, ea_ref), (ob_ref, eb_ref)):
        hidden = jnp.where(odd, o_ref[...].astype(F32), e_ref[...].astype(F32)).astype(BF)
        outs.append(dot(hidden, d_ref[...])[:prefix])
    action = jnp.concatenate([aa_ref[...], ab_ref[...]], axis=0)
    action = jnp.concatenate(
        [action, jnp.zeros((action.shape[0], dp - action.shape[1]), F32)], axis=1
    )
    out_ref[0] = jnp.concatenate(outs + [action], axis=0).astype(BF)


def lift(odd, place_a, place_b, lift_a, lift_b, h_odd, h_even, lifted_action, down, each, ra):
    n = odd.shape[0]
    f, dp = down.shape
    da = lifted_action.shape[1]
    a_spec = pl.BlockSpec((each, f), lambda j, o, a, b, la, lb: (a[j], 0))
    b_spec = pl.BlockSpec((each, f), lambda j, o, a, b, la, lb: (b[j], 0))
    rows = 2 * each
    return pl.pallas_call(
        lift_kernel,
        grid_spec=pltpu.PrefetchScalarGridSpec(
            num_scalar_prefetch=5,
            grid=(n,),
            in_specs=[
                a_spec,
                a_spec,
                b_spec,
                b_spec,
                pl.BlockSpec((ra // 2, da), lambda j, o, a, b, la, lb: (la[j], 0)),
                pl.BlockSpec((ra // 2, da), lambda j, o, a, b, la, lb: (lb[j], 0)),
                pl.BlockSpec((f, dp), lambda j, o, a, b, la, lb: (0, 0)),
            ],
            out_specs=pl.BlockSpec((1, rows, dp), lambda j, o, a, b, la, lb: (j, 0, 0)),
        ),
        out_shape=pltpu.HBM((n, rows, dp), BF),
        compiler_params=pltpu.CompilerParams(vmem_limit_bytes=32 * MIB),
        cost_estimate=pl.CostEstimate(
            flops=2 * n * rows * dp * f, bytes_accessed=2 * n * rows * dp, transcendentals=0
        ),
    )(odd, place_a, place_b, lift_a, lift_b, h_odd, h_even, h_odd, h_even,
      lifted_action, lifted_action, down)


def pieces_kernel(t_ref, ka_ref, ga_ref, kb_ref, gb_ref, *outs):
    tp = len(outs)
    each, dp = ka_ref.shape
    cp = dp // tp
    rp = outs[0].shape[0] * 2 * each // (2 * each)
    extra = 8
    prefix = each - extra
    ca = outs[0].shape[1] // 2
    del rp
    for k in range(tp):
        rank = t_ref[0] ^ k
        tops, ends = [], []
        for keep, got in ((ka_ref, ga_ref), (kb_ref, gb_ref)):
            wide = place(rank, cp)
            tops.append(keep[:prefix, wide].astype(F32) + got[:prefix, wide].astype(F32))
            slim = place(rank, ca)
            ends.append(
                keep[prefix:, slim].astype(F32) + got[prefix:, slim].astype(F32)
            )
        action = jnp.concatenate(ends, axis=0)
        action = jnp.concatenate(
            [action, jnp.zeros((action.shape[0], cp - ca), F32)], axis=1
        )
        outs[k][...] = jnp.concatenate(tops + [action], axis=0).astype(BF)


def middle_back_kernel(t_ref, *refs):
    tp = lax.axis_size("tp")
    ds = refs[:tp]
    mp_ref, ma_ref, gp_ref, ga_ref, cp_ref, ca_ref, w_ref = refs[tp : tp + 7]
    bp_ref, ba_ref, own_ref, lp_ref, la_ref, dm_ref, dp_scr, da_scr, rp_scr, ra_scr = refs[tp + 7 :]
    rp, dp = mp_ref.shape
    ra, da = ma_ref.shape
    cp, ca = dp // tp, da // tp
    n = w_ref.shape[0]
    kp = dp // n
    t = t_ref[0]
    for k in range(tp):
        dp_scr[:, place(t ^ k, cp)] = ds[k][:rp, :]
        da_scr[:, place(t ^ k, ca)] = ds[k][rp:, :ca]
    mixes = []
    for d_ref, m_ref, g_ref, c_ref, b_ref, r_ref, l_ref, first, last in (
        (dp_scr, mp_ref, gp_ref, cp_ref, bp_ref, rp_scr, lp_ref, 0, kp),
        (da_scr, ma_ref, ga_ref, ca_ref, ba_ref, ra_scr, la_ref, kp, w_ref.shape[2]),
    ):
        gradient = d_ref[...].astype(F32)
        rows = m_ref[...].astype(F32)
        inverse = inverse_rms(rows)
        centered = rows * inverse
        inner = gradient * g_ref[...]
        dresid = c_ref[...].astype(F32) + inverse * (
            inner - centered * jnp.mean(inner * centered, axis=1, keepdims=True)
        )
        l_ref[...] = jnp.sum(gradient * centered, axis=0, keepdims=True)
        r_ref[...] = dresid
        branch = dresid.astype(BF)
        b_ref[...] = branch
        size = last - first
        mix = jnp.zeros((rows.shape[0], dm_ref.shape[1]), F32)
        for d in range(n):
            mix = mix + dot_t(branch[:, d * size : (d + 1) * size], w_ref[d, :, first:last])
        mixes.append(mix)
    dm_ref[...] = jnp.concatenate(mixes, axis=0).astype(BF)
    own_ref[:rp, :] = rp_scr[:, place(t, cp)]
    own_ref[rp:, :] = jnp.concatenate(
        [ra_scr[:, place(t, ca)], jnp.zeros((ra, cp - ca), F32)], axis=1
    )


def out_grad_kernel(bp_ref, ba_ref, mix_ref, out_ref):
    rp, dp = bp_ref.shape
    n = out_ref.shape[0]
    kp = dp // n
    ka = ba_ref.shape[1] // n
    for d in range(n):
        out_ref[d, :, :kp] = t_dot(mix_ref[:rp, :], bp_ref[:, d * kp : (d + 1) * kp]).astype(BF)
        out_ref[d, :, kp:] = t_dot(mix_ref[rp:, :], ba_ref[:, d * ka : (d + 1) * ka]).astype(BF)


def front_back_kernel(heads_width, s_ref, t_ref, dq_ref, *refs):
    tp = lax.axis_size("tp")
    n = lax.axis_size("seq")
    (ka_ref, ra_ref, kb_ref, rb_ref, xp_ref, xa_ref, inv_ref, gp_ref, ga_ref, w_ref, lp_ref,
     la_ref, lifted_ref) = refs[:13]
    groups = refs[13:17]
    pieces = refs[17 : 17 + tp]
    gwp_scr, gwa_scr, gain_scr, dp_scr, da_scr = refs[17 + tp :]
    rp, dp = xp_ref.shape
    ra, da = xa_ref.shape
    kp, ka = dp // n, da // n
    cp, ca = dp // tp, da // tp
    width = heads_width
    dkv = jnp.concatenate(
        [
            ka_ref[...].astype(F32) + ra_ref[...].astype(F32),
            kb_ref[...].astype(F32) + rb_ref[...].astype(F32),
        ],
        axis=0,
    )
    dqkv = jnp.concatenate([dq_ref[...].astype(F32), dkv], axis=1)
    gain_scr[...] = jnp.zeros(gain_scr.shape, F32)
    dots = []
    for x_ref, g_ref, d_scr, gw_scr, l_ref, begin, end, first, last, size, at in (
        (xp_ref, gp_ref, dp_scr, gwp_scr, lp_ref, 0, rp, 0, kp, kp, 0),
        (xa_ref, ga_ref, da_scr, gwa_scr, la_ref, rp, rp + ra, kp, kp + ka, ka, 256),
    ):
        grad_rows = dqkv[begin:end].astype(BF)
        centered = x_ref[...].astype(F32) * inv_ref[begin:end, :1]
        normed = (centered * g_ref[...]).astype(BF)
        gw_scr[...] = t_dot(normed, grad_rows).astype(BF)
        weights = w_ref[:, first:last, :].reshape(x_ref.shape[1], -1)
        partial = dot_t(grad_rows, weights)
        d_scr[...] = partial
        product = partial * centered
        gains = jnp.sum(product, axis=0, keepdims=True)
        mlp_gains = l_ref[...]
        for d in range(n):
            gain_scr[d, 0:1, at : at + size] = gains[:, d * size : (d + 1) * size]
            gain_scr[d, 0:1, at + 512 : at + 512 + size] = mlp_gains[
                :, d * size : (d + 1) * size
            ]
        dots.append(jnp.sum(product * g_ref[...], axis=1, keepdims=True))
    column = jnp.concatenate(dots, axis=0)
    lanes = lax.broadcasted_iota(jnp.int32, (rp + ra, cp), 1)
    rows = lax.broadcasted_iota(jnp.int32, (rp + ra, cp), 0)
    row = jnp.sum(jnp.where(lanes == rows, column, 0.0), axis=0, keepdims=True)
    high = row.astype(BF).astype(F32)
    tail = jnp.concatenate([high, row - high, jnp.zeros((6, cp), F32)], axis=0)
    for k in range(tp):
        rank = t_ref[0] ^ k
        action = jnp.concatenate(
            [da_scr[:, place(rank, ca)], jnp.zeros((ra, cp - ca), F32)], axis=1
        )
        lifted_action = jnp.concatenate(
            [lifted_ref[rp:, place(rank, ca)].astype(F32), jnp.zeros((ra, cp - ca), F32)], axis=1
        )
        lifted = lifted_ref[:rp, place(rank, cp)].astype(F32)
        pieces[k][...] = jnp.concatenate(
            [dp_scr[:, place(rank, cp)], action, tail, lifted, lifted_action], axis=0
        ).astype(BF)
    for odd in range(2):
        for number in range(2):
            out = groups[2 * odd + number]
            for i, k in enumerate(block_order(number)):
                d = s_ref[0] ^ (k ^ odd)
                hp, ha = kp // 2, ka // 2
                out[i, :hp, :] = gwp_scr[
                    pl.ds(pl.multiple_of(d * kp + number * hp, hp), hp), :
                ]
                out[i, hp : hp + ha, :] = gwa_scr[
                    pl.ds(pl.multiple_of(d * ka + number * ha, ha), ha), :
                ]
                out[i, hp + ha :, :] = gain_scr[d].astype(BF) * BF(1 - number)


def grad_x_kernel(t_ref, *refs):
    tp = lax.axis_size("tp")
    ds = refs[:tp]
    x_ref, inv_ref, gp_ref, ga_ref, r_ref, op_ref, oa_ref = refs[tp:]
    rp, cp = op_ref.shape
    ra, ca = oa_ref.shape
    t = t_ref[0]
    total = ds[0][...].astype(F32)
    for k in range(1, tp):
        total = total + ds[k][...].astype(F32)
    row = total[rp + ra : rp + ra + 1] + total[rp + ra + 1 : rp + ra + 2]
    lanes = lax.broadcasted_iota(jnp.int32, (rp + ra, cp), 1)
    rows = lax.broadcasted_iota(jnp.int32, (rp + ra, cp), 0)
    column = jnp.sum(jnp.where(lanes == rows, row, 0.0), axis=1, keepdims=True)
    for o_ref, g_ref, begin, end, wide in (
        (op_ref, gp_ref, 0, rp, cp),
        (oa_ref, ga_ref, rp, rp + ra, ca),
    ):
        inverse = inv_ref[begin:end, :1]
        centered = x_ref[begin:end, :wide].astype(F32) * inverse
        mean = column[begin:end] / (wide * tp)
        moved = inverse * (
            total[begin:end, :wide] * g_ref[:, place(t, wide)] - centered * mean
        )
        o_ref[...] = (r_ref[begin:end, :wide] + moved).astype(BF)


def home_kernel(token_ref, g_ref, d_ref, gate_ref, down_ref, act_ref):
    del token_ref
    f = gate_ref.shape[1]
    gate_ref[...] = g_ref[0].astype(F32)
    down_ref[...] = d_ref[0, :f, :].astype(F32)
    act_ref[0] = d_ref[0, f:, :].astype(F32)


def home(token, got_gate, got_down):
    n, kp, f = got_gate.shape
    tall = got_down.shape[1]
    return pl.pallas_call(
        home_kernel,
        grid=(n,),
        in_specs=[
            pl.BlockSpec(memory_space=pltpu.SMEM),
            pl.BlockSpec((1, kp, f), lambda j: (j, 0, 0)),
            pl.BlockSpec((1, tall, kp), lambda j: (j, 0, 0)),
        ],
        out_specs=(
            pl.BlockSpec((kp, f), lambda j: (0, j)),
            pl.BlockSpec((f, kp), lambda j: (j, 0)),
            pl.BlockSpec((1, tall - f, kp), lambda j: (j, 0, 0)),
        ),
        out_shape=(
            jax.ShapeDtypeStruct((kp, n * f), F32),
            jax.ShapeDtypeStruct((n * f, kp), F32),
            jax.ShapeDtypeStruct((n, tall - f, kp), F32),
        ),
        cost_estimate=pl.CostEstimate(
            flops=0, bytes_accessed=6 * n * kp * (f + tall), transcendentals=0
        ),
    )(token, got_gate, got_down)


def home_up_kernel(u_ref, up_ref):
    up_ref[...] = u_ref[0].astype(F32)


def home_up(got):
    n, kp, f = got.shape
    return pl.pallas_call(
        home_up_kernel,
        grid=(n,),
        in_specs=[pl.BlockSpec((1, kp, f), lambda j: (j, 0, 0))],
        out_specs=pl.BlockSpec((kp, f), lambda j: (0, j)),
        out_shape=jax.ShapeDtypeStruct((kp, n * f), F32),
        cost_estimate=pl.CostEstimate(
            flops=0, bytes_accessed=6 * n * kp * f, transcendentals=0
        ),
    )(got)


def shards(
    x_prefix,
    x_action,
    prefix_segment,
    prefix_attn_gain,
    prefix_query,
    prefix_key,
    prefix_value,
    prefix_out,
    prefix_mlp_gain,
    prefix_gate,
    prefix_up,
    prefix_down,
    action_attn_gain,
    action_query,
    action_key,
    action_value,
    action_out,
    action_mlp_gain,
    action_gate,
    action_up,
    action_down,
    cot_prefix,
    cot_action,
):
    n = lax.axis_size("seq")
    tp = lax.axis_size("tp")
    s = lax.axis_index("seq")
    t = lax.axis_index("tp")
    rank_t = t.astype(jnp.int32).reshape(1)
    rank_s = s.astype(jnp.int32).reshape(1)
    rp, cp = x_prefix.shape
    ra, ca = x_action.shape
    rows = rp + ra
    half = rows // 2
    dp, da = cp * tp, ca * tp
    kp, ka = dp // n, da // n
    width = prefix_query.shape[1]
    qkv_width = width + 2 * HD
    fp, fa = prefix_gate.shape[1] // n, action_gate.shape[1] // n

    x_pack = jnp.concatenate(
        [x_prefix, jnp.pad(x_action, ((0, 0), (0, cp - ca)))], axis=0
    )
    x_pieces = gather_tp(x_pack)
    gains = jnp.concatenate(
        [prefix_attn_gain, prefix_mlp_gain, action_attn_gain, action_mlp_gain]
    )
    gain_rows = -(-gains.shape[0] // qkv_width)
    gains = jnp.pad(gains, (0, 8 * qkv_width - gains.shape[0])).reshape(8, qkv_width)
    pack_qkv = jnp.concatenate(
        [
            jnp.concatenate([prefix_query, prefix_key, prefix_value], axis=1),
            jnp.concatenate([action_query, action_key, action_value], axis=1),
            gains,
        ],
        axis=0,
    )
    got_qkv = lax.all_gather(pack_qkv, "seq", axis=0)
    got_gains = got_qkv[:, kp + ka : kp + ka + gain_rows].reshape(n, -1).astype(F32)
    attn_gain_p = got_gains[:, :kp].reshape(1, dp)
    mlp_gain_p = got_gains[:, kp : 2 * kp].reshape(1, dp)
    attn_gain_a = got_gains[:, 2 * kp : 2 * kp + ka].reshape(1, da)
    mlp_gain_a = got_gains[:, 2 * kp + ka : 2 * kp + 2 * ka].reshape(1, da)
    pack_out = jnp.concatenate([prefix_out, action_out], axis=1)
    cot_wide = jnp.pad(cot_action, ((0, 0), (0, dp - da)))
    cot_stages, cot_last = gather_stacked(
        [
            jnp.concatenate(
                [
                    cot_prefix[i * (rp // 2) : (i + 1) * (rp // 2)],
                    cot_wide[i * (ra // 2) : (i + 1) * (ra // 2)],
                ],
                axis=0,
            )
            for i in range(2)
        ]
    )
    cot_odd, cot_even = near_rows(cot_stages[-1])

    def by_units(w, f):
        return w.reshape(w.shape[0], n, f).transpose(1, 0, 2)

    gate_up_sent = jnp.concatenate([by_units(prefix_gate, fp), by_units(prefix_up, fp)], axis=2)
    action_sent = jnp.concatenate(
        [
            by_units(action_gate, fa),
            by_units(action_up, fa),
            action_down.reshape(n, fa, ka).transpose(0, 2, 1),
        ],
        axis=2,
    ).reshape(n, -1, kp)
    extra = action_sent.shape[1]
    down_sent = jnp.concatenate([prefix_down.reshape(n, fp, kp), action_sent], axis=1)

    queries, kv_a, kv_b, x_full_p, x_full_a, inverse1 = whole_call(
        front_kernel,
        (
            ((rows, width), BF),
            ((half, 2 * HD), BF),
            ((half, 2 * HD), BF),
            ((rp, dp), BF),
            ((ra, da), BF),
            ((rows, 128), F32),
        ),
        [after(rank_t, *cot_last), *x_pieces, got_qkv, attn_gain_p, attn_gain_a],
        2 * rp * dp * qkv_width,
    )
    kv_even = [jnp.concatenate(blocks, axis=0) for blocks in gather_far([kv_a, kv_b])]
    kv_odd = [swap(e, "seq", 1) for e in kv_even]
    keys_values = jnp.concatenate([kv_even[0], kv_odd[0], kv_even[1], kv_odd[1]], axis=0)
    codes = token_codes(prefix_segment, n, ra)
    query_code = lax.dynamic_slice_in_dim(codes, s, 1, 0).reshape(rows, 1)
    key_code = jnp.concatenate(
        [
            lax.dynamic_slice(codes, (s ^ k ^ odd, number * half), (1, half))
            for number in range(2)
            for odd in range(2)
            for k in block_order(number)
        ],
        axis=1,
    )
    attended, mixed, log_sum = whole_call(
        attend_kernel,
        (
            ((rows, width), F32),
            ((rows, width), BF),
            ((rows, width // HD * 128), F32),
        ),
        [queries, keys_values, query_code, key_code],
        4 * rows * width * n * rows,
        transcendentals=rows * width // HD * n * rows,
    )
    got_out = lax.all_gather(after(pack_out, queries), "seq", axis=0)
    down_got = lax.all_to_all(after(down_sent, keys_values), "seq", 0, 0)

    piece = (((rows, cp), BF),)
    branch = sum_tp(
        whole_call(
            branch_kernel, piece * tp, [rank_t, mixed, got_out], 2 * rows * dp * width
        )
    )
    residual = x_pack.astype(F32) + branch
    mid_own = after(residual.astype(BF), down_got)
    gate_up = lax.all_to_all(after(gate_up_sent, branch), "seq", 0, 0).reshape(dp, 2 * fp)
    down = down_got[:, :fp].transpose(1, 0, 2).reshape(fp, dp)
    action_got = down_got[:, fp:].reshape(da, 3 * fa)
    gate_up_action = action_got[:, : 2 * fa]
    down_action = action_got[:, 2 * fa :].T


    def action_rows(blocks):
        return blocks.reshape(n, half, dp)[:, rp // 2 :, :da].reshape(-1, da)

    cot_action_all = jnp.concatenate([action_rows(cot_odd), action_rows(cot_even)], axis=0)
    block = (((half, dp), BF),)
    mid_p, mid_a, normed_a, normed_b = whole_call(
        middle_kernel,
        (((rp, dp), BF), ((ra, da), BF)) + block * 2,
        [after(rank_t, gate_up, down, gate_up_action, down_action, cot_action_all), *gather_tp(mid_own), mlp_gain_p, mlp_gain_a],
        rp * dp,
    )

    normed_odd, normed_even = near_rows(
        [b for blocks in gather_far([normed_a, normed_b]) for b in blocks]
    )
    normed_action = jnp.concatenate([action_rows(normed_odd), action_rows(normed_even)], axis=0)
    tokens = n * ra
    dn_action, lifted_action, grad_gu_action, grad_down_action = whole_call(
        feed_action_kernel,
        (
            ((tokens, da), F32),
            ((tokens, da), F32),
            ((da, 2 * fa), BF),
            ((fa, da), BF),
        ),
        [normed_action, cot_action_all, gate_up_action, down_action],
        18 * tokens * da * fa,
    )
    h_odd, g_odd, dn_odd = feed(
        normed_odd, cot_odd, gate_up, down, dn_action[: tokens // 2], half
    )
    h_even, g_even, dn_even = feed(
        normed_even, cot_even, gate_up, down, dn_action[tokens // 2 :], half
    )
    dn_blocks = [
        d.reshape(2, n // 2, half, dp) for d in (dn_even, swap(dn_odd, "seq", 1))
    ]

    grad_gu_action, grad_down_action = after((grad_gu_action, grad_down_action), dn_even)
    action_grads = jnp.concatenate(
        [
            grad_gu_action.reshape(n, ka, 2 * fa),
            grad_down_action.reshape(fa, n, ka).transpose(1, 2, 0),
        ],
        axis=2,
    ).reshape(n, extra, kp)
    grad_gate, grad_up, grad_down = weight_grads(
        normed_odd, normed_even, cot_odd, cot_even, h_odd, h_even, g_odd, g_even, action_grads
    )
    ranks = s ^ jnp.arange(n, dtype=jnp.int32)
    odd_bits = ranks & 1
    places = []
    for number in range(2):
        table = [0] * n
        for i, k in enumerate(block_order(number)):
            table[k] = table[k ^ 1] = number * (n // 2) + i
        places.append(jnp.array(table, jnp.int32)[ranks])
    lift_places = [p + (1 - odd_bits) * n for p in places]
    lifted = lift(
        odd_bits, *places, *lift_places, h_odd, h_even, lifted_action, down, half, ra
    )
    ((keep_a, got_a), (keep_b, got_b)), *_ = scatter_rows(
        [(dn_blocks[0][i], dn_blocks[1][i]) for i in range(2)], grad_gate
    )
    sent_pieces = whole_call(
        pieces_kernel,
        piece * tp,
        [after(rank_t, lifted), keep_a, got_a, keep_b, got_b],
        rp * dp,
    )
    dn_own = sum_tp(sent_pieces)
    dn_pieces = gather_tp(dn_own.astype(BF))
    lifted_home = lax.psum_scatter(after(lifted, got_a, got_b), "seq", scatter_dimension=0)
    grad_down_home = lax.all_to_all(after(grad_down, sent_pieces[0]), "seq", 0, 0)

    grad_gate_home = lax.all_to_all(
        after(grad_gate, grad_down_home).reshape(n, kp, fp), "seq", 0, 0
    )

    row = ((1, dp), F32)
    row_a = ((1, da), F32)
    dbranch_p, dbranch_a, dresid, mlp_gains_p, mlp_gains_a, dmixed = whole_call(
        middle_back_kernel,
        (((rp, dp), BF), ((ra, da), BF), ((rows, cp), F32), row, row_a, ((rows, width), BF)),
        [after(rank_t, grad_down_home), *dn_pieces, mid_p, mid_a, mlp_gain_p, mlp_gain_a, cot_prefix, cot_action, got_out],
        2 * rows * dp * width,
        scratch=(
            pltpu.VMEM((rp, dp), BF),
            pltpu.VMEM((ra, da), BF),
            pltpu.VMEM((rp, dp), F32),
            pltpu.VMEM((ra, da), F32),
        ),
    )
    dquery, *dkv_parts = whole_call(
        attend_back_kernel,
        (((rows, width), BF),) + (((n * rows // 4, 2 * HD), BF),) * 4,
        [queries, keys_values, query_code, key_code, attended, log_sum, dmixed],
        10 * rows * width * n * rows,
        limit=56,
        transcendentals=rows * width // HD * n * rows,
    )
    dkv_halves = [
        [d.reshape(n // 2, half, 2 * HD) for d in (e, swap(o, "seq", 1))]
        for e, o in ((dkv_parts[0], dkv_parts[1]), (dkv_parts[2], dkv_parts[3]))
    ]
    dkv = [part for pair in scatter_rows(dkv_halves, grad_gate_home)[0] for part in pair]
    (out_grads,) = whole_call(
        out_grad_kernel,
        (((n, width, kp + ka), BF),),
        [dbranch_p, dbranch_a, after(mixed, dquery)],
        2 * rows * dp * width,
    )
    out_home = lax.psum_scatter(out_grads, "seq", scatter_dimension=0)
    tall = (kp + ka) // 2 + 8
    *groups_and_pieces, = whole_call(
        lambda *refs: front_back_kernel(width, *refs),
        (((n // 2, tall, qkv_width), BF),) * 4 + (((2 * rows + 8, cp), BF),) * tp,
        [
            rank_s, rank_t, dquery, *dkv, x_full_p, x_full_a, inverse1, attn_gain_p, attn_gain_a,
            got_qkv, mlp_gains_p, mlp_gains_a, lifted_home,
        ],
        4 * rows * dp * qkv_width,
        scratch=(
            pltpu.VMEM((dp, qkv_width), BF),
            pltpu.VMEM((da, qkv_width), BF),
            pltpu.VMEM((n, 8, qkv_width), F32),
            pltpu.VMEM((rp, dp), F32),
            pltpu.VMEM((ra, da), F32),
        ),
    )
    groups, pieces = groups_and_pieces[:4], groups_and_pieces[4:]
    tree, history, (tp_parts, _) = scatter_rows(
        [(e, swap(o, "seq", 1)) for e, o in ((groups[0], groups[2]), (groups[1], groups[3]))],
        None,
        (trade_tp(pieces), ()),
    )
    lifted_parts = [part[rows + 8 :] for part in tp_parts]
    grad_up_home = lax.all_to_all(
        after(grad_up, grad_gate_home, groups[0]).reshape(n, kp, fp), "seq", 0, 0
    )
    qkv_a, qkv_b = [add(keep, got) for keep, got in tree]
    output = (residual + total_of(lifted_parts)).astype(BF)
    grad_x_p, grad_x_a = whole_call(
        grad_x_kernel,
        (((rp, cp), BF), ((ra, ca), BF)),
        [
            after(rank_t, history[-1]), *tp_parts, x_pack,
            inverse1, attn_gain_p, attn_gain_a, dresid,
        ],
        rp * dp,
    )
    hp, ha = kp // 2, ka // 2
    qkv_home_p = jnp.concatenate([qkv_a[:hp], qkv_b[:hp]], axis=0)
    qkv_home_a = jnp.concatenate([qkv_a[hp : hp + ha], qkv_b[hp : hp + ha]], axis=0)
    gains_home = qkv_a[hp + ha :]
    qp, qa = kp // tp, ka // tp

    attn_gains = jnp.pad(gains_home[:1, :512], ((0, 7), (0, 0)))

    def shared_piece(rank):
        return jnp.concatenate(
            [
                lax.dynamic_slice_in_dim(qkv_home_p[:, width:], rank * qp, qp, 0),
                lax.dynamic_slice_in_dim(qkv_home_a[:, width:], rank * qa, qa, 0),
                attn_gains,
            ],
            axis=0,
        )

    shared_home = sum_tp([shared_piece(t ^ k) for k in range(tp)])
    attn_gains_home = shared_home[qp + qa]
    out_home = after(out_home, *history[-1]).astype(F32)
    grad_gate_p, grad_down_p, action_home = home(
        after(rank_t, history[0]), grad_gate_home, grad_down_home
    )
    grad_up_p = home_up(grad_up_home)
    action_home = action_home.reshape(n, ka, 3 * fa)

    def units(part):
        return part.transpose(1, 0, 2).reshape(ka, n * fa)

    grad_gate_a = units(action_home[:, :, :fa])
    grad_up_a = units(action_home[:, :, fa : 2 * fa])
    grad_down_a = action_home[:, :, 2 * fa :].transpose(0, 2, 1).reshape(n * fa, ka)
    return (
        output[:rp],
        output[rp:, :ca],
        grad_x_p,
        grad_x_a,
        attn_gains_home[:kp],
        qkv_home_p[:, :width],
        shared_home[:qp, :HD],
        shared_home[:qp, HD:],
        out_home[:, :kp],
        gains_home[0, 512 : 512 + kp],
        grad_gate_p,
        grad_up_p,
        grad_down_p,
        attn_gains_home[256 : 256 + ka],
        qkv_home_a[:, :width],
        shared_home[qp : qp + qa, :HD],
        shared_home[qp : qp + qa, HD:],
        out_home[:, kp:],
        gains_home[0, 768 : 768 + ka],
        grad_gate_a,
        grad_up_a,
        grad_down_a,
    )


def solution(mesh):
    split = P("seq", "tp")
    turned = P("tp", "seq")
    both = P(("seq", "tp"), None)
    one = P("seq")
    rows = P("seq", None)
    stream_in = (one, split, rows, rows, turned, one, split, split, turned)
    stream_out = (one, split, both, both, turned, one, split, split, turned)
    return jax.shard_map(
        shards,
        mesh=mesh,
        in_specs=(split, split, P()) + stream_in + stream_in + (rows, rows),
        out_specs=(split, split, split, split) + stream_out + stream_out,
        check_vma=False,
    )
```
